32 devices in a mesh: section: 2 (over core), dp: 16 (over z, y, x).
Axes of the slice: x: 2, y: 2, z: 4, core: 2. Of those that a mesh axis runs over, the one named last changes fastest.
Arguments:
- text: bfloat16 [8192, 768], P('dp'), may hold values from -6 to 6
- image: bfloat16 [128, 576, 768], P('dp', 'section'), may hold values from -6 to 6
- image_counts: int32 [128], P('dp'), may hold values from 196 to 576, as said below
- cotangent: bfloat16 [8192, 768], P('dp'), may hold values from -6 to 6
- attn_norm_gain: float32 [2, 768], P('section'), may hold values from 0.5 to 1.5
- attn_norm_bias: float32 [2, 768], P('section'), may hold values from -1.75 to 1.75
- qkv_weight: bfloat16 [2, 768, 2304], P('section'), may hold values from -0.21875 to 0.21875
- attn_out_weight: bfloat16 [2, 768, 768], P('section'), may hold values from -0.625 to 0.625
- mlp_norm_gain: float32 [2, 768], P('section'), may hold values from 0.5 to 1.5
- mlp_norm_bias: float32 [2, 768], P('section'), may hold values from -1.75 to 1.75
- up_weight: bfloat16 [2, 768, 3072], P('section'), may hold values from -0.21875 to 0.21875
- up_bias: float32 [2, 3072], P('section'), may hold values from -1.75 to 1.75
- down_weight: bfloat16 [2, 3072, 768], P('section'), may hold values from -0.109375 to 0.109375
- down_bias: float32 [2, 768], P('section'), may hold values from -1.75 to 1.75
- cross_norm_gain: float32 [2, 768], replicated, may hold values from 0.5 to 1.5
- cross_norm_bias: float32 [2, 768], replicated, may hold values from -1.75 to 1.75
- cross_query: bfloat16 [768, 768], replicated, may hold values from -0.21875 to 0.21875
- cross_key_value: bfloat16 [768, 1536], replicated, may hold values from -0.21875 to 0.21875
- cross_out: bfloat16 [768, 768], replicated, may hold values from -0.875 to 0.875
Outputs:
- layer_outputs: bfloat16 [2, 8192, 768], P('section', 'dp')
- input_grads: float32 [2, 8192, 768], P('section', 'dp')
- image_grad: float32 [128, 576, 768], P('dp', 'section')
- grad_attn_norm_gain: float32 [2, 768], P('section', 'dp')
- grad_attn_norm_bias: float32 [2, 768], P('section', 'dp')
- grad_qkv_weight: float32 [2, 768, 2304], P('section', 'dp')
- grad_attn_out_weight: float32 [2, 768, 768], P('section', 'dp')
- grad_mlp_norm_gain: float32 [2, 768], P('section', 'dp')
- grad_mlp_norm_bias: float32 [2, 768], P('section', 'dp')
- grad_up_weight: float32 [2, 768, 3072], P('section', 'dp')
- grad_up_bias: float32 [2, 3072], P('section', 'dp')
- grad_down_weight: float32 [2, 3072, 768], P('section', 'dp')
- grad_down_bias: float32 [2, 768], P('section', 'dp')
- grad_cross_norm_gain: float32 [2, 768], P(None, ('section', 'dp'))
- grad_cross_norm_bias: float32 [2, 768], P(None, ('section', 'dp'))
- grad_cross_query: float32 [768, 768], P(('section', 'dp'))
- grad_cross_key_value: float32 [768, 1536], P(('section', 'dp'))
- grad_cross_out: float32 [768, 768], P(('section', 'dp'))
The draws below stay inside these ranges and needn't reach their ends.
Inputs may be any that keep to these rules, and one draw needn't show every extreme that they name: `image_counts`: each caption has 196 or 576 valid image tokens, the first ones of its row; the rest is padding.
All inputs are finite; a program needn't handle non-finite values.
Results may differ from the reference program's by a relative error of at most 0.02.
Values may be sent and summed in bfloat16 or wider, within the bound.
No kernel may reach another device: no remote copies, remote signals or barrier semaphores. Data moves between devices by JAX's collectives and lax.ppermute only.
A program may use at most 384 MiB of HBM per device.

```python
import jax
import jax.numpy as jnp
from jax import lax

D = 768
HEADS = 12
HEAD_DIM = 64
FF = 3072
SEQ = 64
PATCHES = 576
VALID_SMALL = 196
CAPTIONS = 128
TOKENS = 8192
N_DP = 16


def draw_image_counts(key, part):
    coin_flips = jax.random.randint(key, (CAPTIONS,), 0, 2)
    counts = jnp.where(coin_flips == 1, PATCHES, VALID_SMALL)
    positions = jnp.arange(CAPTIONS, dtype=jnp.int32)
    counts = jnp.where(positions == 0, PATCHES, counts)
    counts = jnp.where(positions == 1, VALID_SMALL, counts)
    return counts.astype(jnp.int32)


def steps_of(rng, extent, cuts, low, top_value):
    factor_of, own = 1.0, jax.random.fold_in(rng, 6)
    for dim, parts in cuts:
        steps = jnp.exp(jax.random.uniform(jax.random.fold_in(own, dim), (parts,), jnp.float32, low / len(cuts), top_value / len(cuts)))
        factor_of = factor_of * jnp.repeat(steps, extent[dim] // parts).reshape([-1 if axis == dim else 1 for axis in range(len(extent))])
    return factor_of


def gaussian(stream_key, shape, scale, reach, cuts=(), held_as=jnp.bfloat16):
    result = jax.random.normal(stream_key, shape, jnp.float32) * scale
    if len(cuts) > 0:
        result = steps_of(stream_key, shape, cuts, -0.22, 0.18) * result
    return jnp.clip(result, min=-reach, max=reach).astype(held_as)


def setup_inputs(seed: int = 0) -> dict:
    key_of = jax.random.split(jax.random.key(seed), 20)
    return {
        "text": gaussian(key_of[0], (TOKENS, D), 1.0, 6.0, ((0, 16),)),
        "image": gaussian(key_of[1], (CAPTIONS, PATCHES, D), 1.0, 6.0, ((0, 16), (1, 2))),
        "image_counts": draw_image_counts(jax.random.fold_in(key_of[19], 71), 0),
        "cotangent": gaussian(key_of[3], (TOKENS, D), 1.0, 6.0, ((0, 16),)),
        "attn_norm_gain": jnp.clip(1.0 + 0.1 * jax.random.normal(key_of[4], (2, D), jnp.float32), 0.5, 1.5),
        "attn_norm_bias": gaussian(key_of[5], (2, D), 0.3, 1.75, ((0, 2),), jnp.float32),
        "qkv_weight": gaussian(key_of[6], (2, D, 3 * D), D ** -0.5, 0.21875, ((0, 2),)),
        "attn_out_weight": gaussian(key_of[7], (2, D, D), (D // 8) ** -0.5, 0.625, ((0, 2),)),
        "mlp_norm_gain": jnp.clip(1.0 + 0.1 * jax.random.normal(key_of[8], (2, D), jnp.float32), 0.5, 1.5),
        "mlp_norm_bias": gaussian(key_of[9], (2, D), 0.3, 1.75, ((0, 2),), jnp.float32),
        "up_weight": gaussian(key_of[10], (2, D, FF), D ** -0.5, 0.21875, ((0, 2),)),
        "up_bias": gaussian(key_of[11], (2, FF), 0.3, 1.75, ((0, 2),), jnp.float32),
        "down_weight": gaussian(key_of[12], (2, FF, D), FF ** -0.5, 0.109375, ((0, 2),)),
        "down_bias": gaussian(key_of[13], (2, D), 0.3, 1.75, ((0, 2),), jnp.float32),
        "cross_norm_gain": jnp.clip(1.0 + 0.1 * jax.random.normal(key_of[14], (2, D), jnp.float32), 0.5, 1.5),
        "cross_norm_bias": gaussian(key_of[15], (2, D), 0.3, 1.75, (), jnp.float32),
        "cross_query": gaussian(key_of[16], (D, D), D ** -0.5, 0.21875),
        "cross_key_value": gaussian(key_of[17], (D, 2 * D), D ** -0.5, 0.21875),
        "cross_out": gaussian(key_of[18], (D, D), (D // 16) ** -0.5, 0.875),
    }


@jax.custom_vjp
def low(v):
    return lax.optimization_barrier(v.astype(jnp.bfloat16)).astype(jnp.float32)

@jax.custom_vjp
def low_back(v):
    return v

def low_keep(v):
    return (low(v), None)

def low_pass(kept, grad):
    return (grad,)

def back_keep(v):
    return (v, None)

def back_low(kept, grad):
    return (low(grad),)
low.defvjp(low_keep, low_pass)
low_back.defvjp(back_keep, back_low)
eps = 1e-05
neg_large = -1e+30
highest = lax.Precision.HIGHEST

def layer_norm(stream, gain, bias):
    centred = stream - lax.optimization_barrier(jnp.mean(stream, -1, keepdims=True))
    spread = lax.optimization_barrier(jnp.mean(centred * centred, -1, keepdims=True))
    return centred * lax.rsqrt(spread + eps) * gain + bias

def product_high(left, right):
    return jnp.dot(left, right, precision=highest, preferred_element_type=jnp.float32)

def attend(query, keys, values, key_mask):
    scores = jnp.einsum('cqhd,ckhd->chqk', query, keys, precision=highest) * HEAD_DIM ** (-0.5)
    scores = jnp.where(key_mask, low_back(scores), neg_large)
    row_max = lax.optimization_barrier(jnp.max(scores, -1, keepdims=True))
    powers = jnp.exp(scores - row_max)
    attn_prob = powers / lax.optimization_barrier(jnp.sum(powers, -1, keepdims=True))
    return jnp.einsum('chqk,ckhd->cqhd', low(attn_prob), values, precision=highest)

def self_part(stream, gain, bias, w_qkv, w_out, caption_count):
    normed = low(layer_norm(stream, gain, bias))
    joined = low(low_back(product_high(normed, w_qkv))).reshape(caption_count, SEQ, 3, HEADS, HEAD_DIM)
    positions = jnp.arange(SEQ, dtype=jnp.int32)
    causal = (positions[:, None] >= positions[None, :])[None, None]
    attended = attend(joined[:, :, 0], joined[:, :, 1], joined[:, :, 2], causal)
    attended = low(low_back(attended.reshape(stream.shape[0], D)))
    return low_back(product_high(attended, w_out))

def cross_part(stream, image, counts, gains, biases, w_query, w_key_value, w_out, caption_count):
    normed = low(layer_norm(stream, gains[1], biases[1]))
    query = low(low_back(product_high(normed, w_query))).reshape(caption_count, SEQ, HEADS, HEAD_DIM)
    patches = low(layer_norm(image.reshape(caption_count * PATCHES, D), gains[0], biases[0]))
    joined = low(low_back(product_high(patches, w_key_value))).reshape(caption_count, PATCHES, 2, HEADS, HEAD_DIM)
    positions = jnp.arange(PATCHES, dtype=jnp.int32)
    key_mask = (positions[None, :] < counts[:, None])[:, None, None, :]
    attended = attend(query, joined[:, :, 0], joined[:, :, 1], key_mask)
    attended = low(low_back(attended.reshape(stream.shape[0], D)))
    return low_back(product_high(attended, w_out))

def feed_forward(stream, gain, bias, w_up, b_up, w_down, b_down):
    normed = low(layer_norm(stream, gain, bias))
    hidden = low_back(product_high(normed, w_up) + b_up)
    activated = low(jax.nn.gelu(hidden))
    return low_back(product_high(activated, w_down) + b_down)

def two_layers(params, text, image, extra_zero, counts):
    g_one, b_one, w_qkv, w_out, g_two, b_two, w_up, b_up, w_down, b_down, cross_gain, cross_bias, w_query, w_key_value, w_cross = params
    caption_count = text.shape[0] // SEQ
    stream = text + self_part(text, g_one[0], b_one[0], w_qkv[0], w_out[0], caption_count)
    stream = stream + feed_forward(stream, g_two[0], b_two[0], w_up[0], b_up[0], w_down[0], b_down[0])
    first_out = low(stream)
    stream = low_back(first_out + extra_zero)
    stream = stream + self_part(stream, g_one[1], b_one[1], w_qkv[1], w_out[1], caption_count)
    stream = stream + cross_part(stream, image, counts, cross_gain, cross_bias, w_query, w_key_value, w_cross, caption_count)
    stream = stream + feed_forward(stream, g_two[1], b_two[1], w_up[1], b_up[1], w_down[1], b_down[1])
    return (stream, first_out)

def reference(text, image, image_counts, cotangent, attn_norm_gain, attn_norm_bias, qkv_weight, attn_out_weight, mlp_norm_gain, mlp_norm_bias, up_weight, up_bias, down_weight, down_bias, cross_norm_gain, cross_norm_bias, cross_query, cross_key_value, cross_out):
    params = tuple((weight.astype(jnp.float32) for weight in (attn_norm_gain, attn_norm_bias, qkv_weight, attn_out_weight, mlp_norm_gain, mlp_norm_bias, up_weight, up_bias, down_weight, down_bias, cross_norm_gain, cross_norm_bias, cross_query, cross_key_value, cross_out)))
    group_size = N_DP
    blocks = CAPTIONS // group_size
    text_blocks = text.astype(jnp.float32).reshape(blocks, group_size * SEQ, D)
    image_blocks = image.astype(jnp.float32).reshape(blocks, group_size, PATCHES, D)
    count_blocks = image_counts.reshape(blocks, group_size)
    cot_blocks = cotangent.astype(jnp.float32).reshape(blocks, group_size * SEQ, D)

    def step_block(summed, pieces):
        text_piece, image_piece, count_piece, cot_piece = pieces
        extra_zero = jnp.zeros_like(text_piece)

        def forward_fn(params_in, text_in, image_in, extra_in):
            return two_layers(params_in, text_in, image_in, extra_in, count_piece)
        final_out, pullback, first_out = jax.vjp(forward_fn, params, text_piece, image_piece, extra_zero, has_aux=True)
        grad_params, grad_text, grad_image, grad_extra = pullback(cot_piece)
        summed = jax.tree.map(jnp.add, summed, grad_params)
        return (summed, (final_out.astype(jnp.bfloat16), first_out.astype(jnp.bfloat16), grad_text, grad_extra, grad_image))
    zeros_start = jax.tree.map(jnp.zeros_like, params)
    summed, (finals, firsts, grad_texts, grad_extras, grad_images) = lax.scan(step_block, zeros_start, (text_blocks, image_blocks, count_blocks, cot_blocks))
    layer_outputs = jnp.stack([firsts.reshape(TOKENS, D), finals.reshape(TOKENS, D)])
    input_grads = jnp.stack([grad_texts.reshape(TOKENS, D), grad_extras.reshape(TOKENS, D)])
    image_grad = grad_images.reshape(CAPTIONS, PATCHES, D)
    return (layer_outputs, input_grads, image_grad, summed[0], summed[1], summed[2], summed[3], summed[4], summed[5], summed[6], summed[7], summed[8], summed[9], summed[10], summed[11], summed[12], summed[13], summed[14])
```

```python
import jax
import jax.numpy as jnp
from jax import lax
from jax.experimental import pallas as pl
from jax.experimental.pallas import tpu as pltpu
from jax.sharding import PartitionSpec as P

HEAD_DIM = 64
SEQ = 64
LANES = 128
PAIR_ROWS = 2 * SEQ
CHUNK = 64
EPS = 1e-05
NEG = -1e30
SCALE = HEAD_DIM**-0.5
BF = jnp.bfloat16
F32 = jnp.float32


def nn(a, b):
    return lax.dot_general(a, b, (((1,), (0,)), ((), ())), preferred_element_type=F32)


def nt(a, b):
    return lax.dot_general(a, b, (((1,), (1,)), ((), ())), preferred_element_type=F32)


def tn(a, b):
    return lax.dot_general(a, b, (((0,), (0,)), ((), ())), preferred_element_type=F32)


def normalized(v):
    c = v - jnp.mean(v, -1, keepdims=True)
    inv = lax.rsqrt(jnp.mean(c * c, -1, keepdims=True) + EPS)
    return c * inv, inv


def norm(v, g, b):
    return normalized(v)[0] * g + b


def norm_grad(v, g, dh):
    nh, inv = normalized(v)
    e = dh * g
    dv = (e - jnp.mean(e, -1, keepdims=True) - nh * jnp.mean(e * nh, -1, keepdims=True)) * inv
    return dv, dh * nh


def fold(v):
    return jnp.sum(v.reshape(v.shape[0] // 8, 8, v.shape[1]), 0)


def gelu_pair(u):
    k = 0.7978845608028654
    t = jnp.tanh(k * (u + 0.044715 * u * u * u))
    g = 0.5 * u * (1.0 + t)
    dg = 0.5 * (1.0 + t) + 0.5 * u * (1.0 - t * t) * (k * (1.0 + 3 * 0.044715 * u * u))
    return g, dg


def gelu(u):
    k = 0.7978845608028654
    return 0.5 * u * (1.0 + jnp.tanh(k * (u + 0.044715 * u * u * u)))


def two_heads(v):
    low = lax.broadcasted_iota(jnp.int32, v.shape, 1) < HEAD_DIM
    zero = jnp.zeros_like(v)
    return jnp.concatenate([jnp.where(low, v, zero), jnp.where(low, zero, v)], 0)


def join_heads(v):
    half = v.shape[0] // 2
    low = lax.broadcasted_iota(jnp.int32, (half, LANES), 1) < HEAD_DIM
    return jnp.where(low, v[:half], v[half:])


def softmax(s):
    e = jnp.exp(s - jnp.max(s, -1, keepdims=True))
    return e / jnp.sum(e, -1, keepdims=True)


def self_probs(q2, k):
    s = nt(q2, k) * SCALE
    row = lax.broadcasted_iota(jnp.int32, s.shape, 0) % PAIR_ROWS
    col = lax.broadcasted_iota(jnp.int32, s.shape, 1)
    ok = (row // SEQ == col // SEQ) & (col <= row)
    return softmax(jnp.where(ok, s, NEG))


def cross_probs(q2, k, limits):
    s = nt(q2, k) * SCALE
    half = k.shape[0] // 2
    col = lax.broadcasted_iota(jnp.int32, s.shape, 1)
    bound = jnp.where(col < half, limits[0], limits[1] + half)
    return softmax(jnp.where(col < bound, s, NEG))


def attend_grad(q2, k, v, p, go):
    go2 = two_heads(go)
    dp = nt(go2, v)
    ds = (p * (dp - jnp.sum(p * dp, -1, keepdims=True))).astype(BF)
    dq = join_heads(nn(ds, k)) * SCALE
    dk = tn(ds, q2) * SCALE
    dv = tn(p.astype(BF), go2)
    return dq, dk, dv


def loop(count, body):
    def step(i, carry):
        body(i)
        return carry

    lax.fori_loop(0, count, step, 0)


def rows(i, size):
    return pl.ds(pl.multiple_of(i * size, size), size)


def lane(start, size):
    return pl.ds(pl.multiple_of(start, LANES), size)


def call(name, body, grid, scalars, ins, outs, scratch=(), flops=0):
    def spec(shape, item):
        block, index = item
        if block is None:
            block = shape
        if index is None:
            index = lambda *_, n=len(shape): (0,) * n
        return pl.BlockSpec(block, index)

    shapes = [jax.ShapeDtypeStruct(o[0], o[1]) for o in outs]
    moved = sum(a[0].size * a[0].dtype.itemsize for a in ins)
    moved += sum(s.size * s.dtype.itemsize for s in shapes)
    return pl.pallas_call(
        body,
        name=name,
        out_shape=shapes,
        grid_spec=pltpu.PrefetchScalarGridSpec(
            num_scalar_prefetch=len(scalars),
            grid=grid,
            in_specs=[spec(a[0].shape, a[1:]) for a in ins],
            out_specs=[spec(o[0], o[2:]) for o in outs],
            scratch_shapes=list(scratch),
        ),
        compiler_params=pltpu.CompilerParams(vmem_limit_bytes=56 << 20),
        cost_estimate=pl.CostEstimate(flops=int(flops), bytes_accessed=int(moved), transcendentals=0),
    )(*scalars, *[a[0] for a in ins])


def whole(a):
    return (a, None, None)


def out_whole(shape, dtype):
    return (shape, dtype, None, None)


class Half:
    def __init__(self, layer, own, got, width):
        self.layer, self.own, self.got, self.width = layer, own, got, width

    def cols(self, per, steps):
        layer, width = self.layer, self.width
        d = self.own.shape[0]

        def own_map(j, ids, *_):
            return (0, jnp.where(ids[0] == layer, per(j, ids[0]), 0))

        def got_map(j, ids, *_):
            return (0, jnp.where(ids[0] == layer, 0, j))

        return [(self.own, (d, width), own_map), (self.got, (d, width), got_map)]

    def rowblocks(self, per):
        layer, width = self.layer, self.width
        d = self.own.shape[1]

        def own_map(j, ids, *_):
            return (jnp.where(ids[0] == layer, per(j, ids[0]), 0), 0)

        def got_map(j, ids, *_):
            return (jnp.where(ids[0] == layer, 0, j), 0)

        return [(self.own, (width, d), own_map), (self.got, (width, d), got_map)]


def pick(ids, layer, own_ref, got_ref):
    return jnp.where(ids[0] == layer, own_ref[...], got_ref[...])


def self_fwd(layer, ids, stream, gain, bias, wqkv, wout):
    first = len(stream) == 1
    t, d = stream[0].shape
    h2 = d // 2
    n_in = len(stream)

    def body(ids_ref, *refs):
        xs, refs = refs[:n_in], refs[n_in:]
        g_ref, b_ref, own, got, o_own, o_got = refs[:6]
        outs = refs[6:]
        h_ref, qkv_ref, att_ref, part_ref, send_ref = outs[:5]
        j = pl.program_id(0)

        @pl.when(j == 0)
        def _():
            def chunk(i):
                sl = rows(i, CHUNK)
                if first:
                    x = xs[0][sl, :].astype(F32)
                else:
                    z = (xs[0][sl, :] + xs[1][sl, :] + xs[2][sl, :].astype(F32)).astype(BF)
                    outs[5][sl, :] = z
                    x = z.astype(F32)
                h_ref[sl, :] = norm(x, g_ref[...], b_ref[...]).astype(BF)

            loop(t // CHUNK, chunk)

        w = pick(ids_ref, layer, own, got)

        def project(i):
            sl = rows(i, 256)
            qkv_ref[j, sl, :] = nn(h_ref[sl, :], w).astype(BF)

        loop(t // 256, project)

        @pl.when(j == 2)
        def _():
            def block(i):
                sl = rows(i, PAIR_ROWS)
                for p in range(h2 // LANES):
                    ln = slice(p * LANES, (p + 1) * LANES)
                    k = qkv_ref[1, sl, ln]
                    probs = self_probs(two_heads(qkv_ref[0, sl, ln]), k).astype(BF)
                    att_ref[sl, ln] = join_heads(nn(probs, qkv_ref[2, sl, ln])).astype(BF)

            loop(t // PAIR_ROWS, block)
            wo = pick(ids_ref, layer, o_own, o_got)

            def finish(i):
                sl = rows(i, 256)
                part = nn(att_ref[sl, :], wo)
                part_ref[sl, :] = part
                send_ref[sl, :] = part.astype(BF)

            loop(t // 256, finish)

    outs = [
        out_whole((t, d), BF),
        out_whole((3, t, h2), BF),
        out_whole((t, h2), BF),
        out_whole((t, d), F32),
        out_whole((t, d), BF),
    ]
    if not first:
        outs.append(out_whole((t, d), BF))
    ins = [whole(x) for x in stream] + [whole(gain), whole(bias)]
    ins += wqkv.cols(lambda j, s: 2 * j + s, 3) + wout.rowblocks(lambda j, s: s)[:1]
    ins += [whole(wout.got)]
    return call(
        f"self_fwd_{layer}", body, (3,), [ids], ins, outs, flops=2 * t * d * 4 * h2 + 2e8
    )


def mlp_fwd(layer, ids, x, a_own, a_got, gain, bias, wup, b_up, wdown, b_down):
    t, d = x.shape
    fh = b_up.shape[1]
    width = wup.width

    def body(ids_ref, x_ref, p_ref, q_ref, g_ref, b_ref, u_own, u_got, bu_ref, d_own, d_got, bd_ref,
             x1_ref, n_ref, part_ref, send_ref):
        j = pl.program_id(0)

        @pl.when(j == 0)
        def _():
            def chunk(i):
                sl = rows(i, CHUNK)
                x1 = x_ref[sl, :].astype(F32) + p_ref[sl, :] + q_ref[sl, :].astype(F32)
                x1_ref[sl, :] = x1
                n_ref[sl, :] = norm(x1, g_ref[...], b_ref[...]).astype(BF)
                part_ref[sl, :] = jnp.broadcast_to(
                    jnp.where(ids_ref[0] == 0, bd_ref[...], 0.0), (CHUNK, d)
                )

            loop(t // CHUNK, chunk)

        up = pick(ids_ref, layer, u_own, u_got)
        down = pick(ids_ref, layer, d_own, d_got)

        def tile(i):
            sl = rows(i, 128)
            u = nn(n_ref[sl, :], up) + bu_ref[...]
            part_ref[sl, :] += nn(gelu(u).astype(BF), down)

        loop(t // 128, tile)

        @pl.when(j == pl.num_programs(0) - 1)
        def _():
            def chunk(i):
                sl = rows(i, CHUNK)
                send_ref[sl, :] = part_ref[sl, :].astype(BF)

            loop(t // CHUNK, chunk)

    per = fh // width
    ins = [whole(x), whole(a_own), whole(a_got), whole(gain), whole(bias)]
    ins += wup.cols(lambda j, s: s * per + j, per)
    ins += [(b_up, (1, width), lambda j, *_: (0, j))]
    ins += wdown.rowblocks(lambda j, s: s * per + j)
    ins += [whole(b_down)]
    outs = [
        out_whole((t, d), F32),
        out_whole((t, d), BF),
        out_whole((t, d), F32),
        out_whole((t, d), BF),
    ]
    return call(f"mlp_fwd_{layer}", body, (per,), [ids], ins, outs, flops=4 * t * d * fh)


def mlp_grad(layer, ids, lead, gain, bias, wup, b_up, wdown, b_down):
    second = layer == 1
    t, d = lead[0].shape
    fh = b_up.shape[1]
    width = wup.width
    n_in = len(lead)

    def body(ids_ref, *refs):
        lead_refs, refs = refs[:n_in], refs[n_in:]
        g_ref, b_ref, u_own, u_got, bu_ref, d_own, d_got, bd_ref = refs[:8]
        outs = refs[8:]
        act_ref, du_ref, dn_ref, dsend_ref, sums_ref, bup_ref = outs[:6]
        extra = outs[6:]
        j = pl.program_id(0)

        @pl.when(j == 0)
        def _():
            sums_ref[...] = jnp.zeros_like(sums_ref)

            def chunk(i):
                sl = rows(i, CHUNK)
                if second:
                    x_ref, p_ref, q_ref, cot_ref = lead_refs
                    x = x_ref[sl, :] + p_ref[sl, :] + q_ref[sl, :].astype(F32)
                    extra[0][sl, :] = x
                    extra[1][sl, :] = norm(x, g_ref[...], b_ref[...]).astype(BF)
                    extra[2][sl, :] = jnp.broadcast_to(
                        jnp.where(ids_ref[0] == 0, bd_ref[...], 0.0), (CHUNK, d)
                    )
                    sums_ref[2] += fold(cot_ref[sl, :].astype(F32))
                else:
                    grad_ref, p_ref, q_ref, z_ref, zg_ref, n_ref = lead_refs
                    dh = p_ref[sl, :] + q_ref[sl, :].astype(F32)
                    dv, dhn = norm_grad(z_ref[sl, :].astype(F32), zg_ref[...], dh)
                    dz = (grad_ref[sl, :] + dv).astype(BF)
                    extra[0][sl, :] = dz
                    sums_ref[0] += fold(dhn)
                    sums_ref[1] += fold(dh)
                    sums_ref[2] += fold(dz.astype(F32))
                dn_ref[sl, :] = jnp.zeros((CHUNK, d), F32)

            loop(t // CHUNK, chunk)

        up = pick(ids_ref, layer, u_own, u_got)
        down = pick(ids_ref, layer, d_own, d_got)
        bup_ref[...] = jnp.zeros_like(bup_ref)
        n_src = extra[1] if second else lead_refs[5]
        dm_src = lead_refs[3] if second else extra[0]

        def tile(i):
            sl = rows(i, 128)
            u = nn(n_src[sl, :], up) + bu_ref[...]
            g, dg = gelu_pair(u)
            g = g.astype(BF)
            act_ref[sl, :] = g
            du = (nt(dm_src[sl, :], down) * dg).astype(BF)
            du_ref[sl, :] = du
            bup_ref[...] += fold(du.astype(F32))
            dn_ref[sl, :] += nt(du, up)
            if second:
                extra[2][sl, :] += nn(g, down)

        loop(t // 128, tile)

        @pl.when(j == pl.num_programs(0) - 1)
        def _():
            def chunk(i):
                sl = rows(i, CHUNK)
                dsend_ref[sl, :] = dn_ref[sl, :].astype(BF)
                if second:
                    extra[3][sl, :] = extra[2][sl, :].astype(BF)

            loop(t // CHUNK, chunk)

    per = fh // width
    ins = [whole(a) for a in lead] + [whole(gain), whole(bias)]
    ins += wup.cols(lambda j, s: s * per + j, per)
    ins += [(b_up, (1, width), lambda j, *_: (0, j))]
    ins += wdown.rowblocks(lambda j, s: s * per + j)
    ins += [whole(b_down)]
    outs = [
        ((t, fh), BF, (t, width), lambda j, *_: (0, j)),
        ((t, fh), BF, (t, width), lambda j, *_: (0, j)),
        out_whole((t, d), F32),
        out_whole((t, d), BF),
        out_whole((3, 8, d), F32),
        ((8, fh), F32, (8, width), lambda j, *_: (0, j)),
    ]
    if second:
        outs += [
            out_whole((t, d), F32),
            out_whole((t, d), BF),
            out_whole((t, d), F32),
            out_whole((t, d), BF),
        ]
    else:
        outs += [out_whole((t, d), BF)]
    return call(
        f"mlp_grad_{layer}", body, (per,), [ids], ins, outs,
        flops=(8 if second else 6) * t * d * fh,
    )


def key_value(ids, image, gain, bias, w):
    caps, half, d = image.shape
    h2 = d // 2

    def body(ids_ref, im_ref, g_ref, b_ref, k_own, v_own, k_oth, v_oth, r_ref, own_ref, oth_ref):
        def chunk(i):
            sl = rows(i, 96)
            r_ref[0, sl, :] = norm(im_ref[0, sl, :].astype(F32), g_ref[...], b_ref[...]).astype(BF)

        loop(half // 96, chunk)
        r = r_ref[0]
        own_ref[0, :, :h2] = nn(r, k_own[...]).astype(BF)
        own_ref[0, :, h2:] = nn(r, v_own[...]).astype(BF)
        oth_ref[0, :, :h2] = nn(r, k_oth[...]).astype(BF)
        oth_ref[0, :, h2:] = nn(r, v_oth[...]).astype(BF)

    part = lambda off: (w, (d, h2), lambda c, ids: (0, off(ids[0])))
    blk = ((1, half, d), lambda c, *_: (c, 0, 0))
    ins = [(image,) + blk, whole(gain), whole(bias)]
    ins += [
        part(lambda s: s), part(lambda s: 2 + s), part(lambda s: 1 - s), part(lambda s: 3 - s)
    ]
    outs = [((caps, half, d), BF) + blk] * 3
    return call("key_value", body, (caps,), [ids], ins, outs, flops=4 * caps * half * d * d)


def key_value_grad(ids, image, gain, g_own, g_oth, w):
    caps, half, d = image.shape
    h2 = d // 2

    def body(ids_ref, im_ref, g_ref, own_ref, oth_ref, k_own, v_own, k_oth, v_oth, dx_ref, sums_ref):
        @pl.when(pl.program_id(0) == 0)
        def _():
            sums_ref[...] = jnp.zeros_like(sums_ref)

        def chunk(i):
            sl = rows(i, 96)
            dr = nt(own_ref[0, sl, :h2], k_own[...]) + nt(own_ref[0, sl, h2:], v_own[...])
            dr += nt(oth_ref[0, sl, :h2], k_oth[...]) + nt(oth_ref[0, sl, h2:], v_oth[...])
            dv, dhn = norm_grad(im_ref[0, sl, :].astype(F32), g_ref[...], dr)
            dx_ref[0, sl, :] = dv
            sums_ref[0] += fold(dhn)
            sums_ref[1] += fold(dr)

        loop(half // 96, chunk)

    part = lambda off: (w, (d, h2), lambda c, ids: (0, off(ids[0])))
    blk = ((1, half, d), lambda c, *_: (c, 0, 0))
    ins = [(image,) + blk, whole(gain), (g_own,) + blk, (g_oth,) + blk]
    ins += [
        part(lambda s: s), part(lambda s: 2 + s), part(lambda s: 1 - s), part(lambda s: 3 - s)
    ]
    outs = [((caps, half, d), F32) + blk, out_whole((2, 8, d), F32)]
    return call("key_value_grad", body, (caps,), [ids], ins, outs, flops=4 * caps * half * d * d)


def patch_limits(ids_ref, counts_ref, c, half):
    s = ids_ref[0]
    return counts_ref[c] - s * half, counts_ref[c] - (1 - s) * half


def cross_fwd(ids, counts, z, a_own, a_got, gain, bias, wq, wco, kv_own, kv_got):
    caps, half, d = kv_own.shape
    h2 = d // 2
    t = z.shape[0]

    def body(ids_ref, cnt_ref, z_ref, p_ref, q_ref, g_ref, b_ref, wq_ref, wo_ref, own_ref, got_ref,
             z2_ref, h_ref, cq_ref, att_ref, part_ref, send_ref):
        c = pl.program_id(0)

        @pl.when(c == 0)
        def _():
            def chunk(i):
                sl = rows(i, CHUNK)
                x = z_ref[sl, :].astype(F32) + p_ref[sl, :] + q_ref[sl, :].astype(F32)
                z2_ref[sl, :] = x
                h_ref[sl, :] = norm(x, g_ref[...], b_ref[...]).astype(BF)

            loop(t // CHUNK, chunk)

            def project(i):
                sl = rows(i, 256)
                cq_ref[sl, :] = nn(h_ref[sl, :], wq_ref[...]).astype(BF)

            loop(t // 256, project)

        limits = patch_limits(ids_ref, cnt_ref, c, half)
        sl = rows(c, SEQ)
        for p in range(h2 // LANES):
            ln = slice(p * LANES, (p + 1) * LANES)
            lv = slice(h2 + p * LANES, h2 + (p + 1) * LANES)
            k = jnp.concatenate([own_ref[0, :, ln], got_ref[0, :, ln]], 0)
            v = jnp.concatenate([own_ref[0, :, lv], got_ref[0, :, lv]], 0)
            probs = cross_probs(two_heads(cq_ref[sl, ln]), k, limits).astype(BF)
            att_ref[sl, ln] = join_heads(nn(probs, v)).astype(BF)

        @pl.when(c == pl.num_programs(0) - 1)
        def _():
            def finish(i):
                sl = rows(i, 256)
                part = nn(att_ref[sl, :], wo_ref[...])
                part_ref[sl, :] = part
                send_ref[sl, :] = part.astype(BF)

            loop(t // 256, finish)

    blk = ((1, half, d), lambda c, *_: (c, 0, 0))
    ins = [whole(z), whole(a_own), whole(a_got), whole(gain), whole(bias)]
    ins += [(wq, (d, h2), lambda c, ids, *_: (0, ids[0])), (wco, (h2, d), lambda c, ids, *_: (ids[0], 0))]
    ins += [(kv_own,) + blk, (kv_got,) + blk]
    outs = [
        out_whole((t, d), F32),
        out_whole((t, d), BF),
        out_whole((t, h2), BF),
        out_whole((t, h2), BF),
        out_whole((t, d), F32),
        out_whole((t, d), BF),
    ]
    return call(
        "cross_fwd", body, (caps,), [ids, counts], ins, outs, flops=4 * t * d * h2 + 16e8
    )


def cross_grad(ids, counts, grad, n_own, n_got, x3, gain3, cq, wq, wco, kv_own, kv_got):
    caps, half, d = kv_own.shape
    h2 = d // 2
    t = x3.shape[0]

    def body(ids_ref, cnt_ref, gr_ref, p_ref, q_ref, x_ref, g_ref, cq_ref, wq_ref, wo_ref, own_ref, got_ref,
             dz_ref, dc_ref, dcq_ref, down_ref, dgot_ref, dh_ref, dsend_ref, sums_ref, da_ref):
        c = pl.program_id(0)

        @pl.when(c == 0)
        def _():
            sums_ref[...] = jnp.zeros_like(sums_ref)

            def chunk(i):
                sl = rows(i, CHUNK)
                dh = p_ref[sl, :] + q_ref[sl, :].astype(F32)
                dv, dhn = norm_grad(x_ref[sl, :], g_ref[...], dh)
                dz = gr_ref[sl, :].astype(F32) + dv
                dz_ref[sl, :] = dz
                dc_ref[sl, :] = dz.astype(BF)
                sums_ref[0] += fold(dhn)
                sums_ref[1] += fold(dh)

            loop(t // CHUNK, chunk)

            def project(i):
                sl = rows(i, 256)
                da_ref[sl, :] = nt(dc_ref[sl, :], wo_ref[...]).astype(BF)

            loop(t // 256, project)

        limits = patch_limits(ids_ref, cnt_ref, c, half)
        sl = rows(c, SEQ)
        for p in range(h2 // LANES):
            ln = slice(p * LANES, (p + 1) * LANES)
            lv = slice(h2 + p * LANES, h2 + (p + 1) * LANES)
            k = jnp.concatenate([own_ref[0, :, ln], got_ref[0, :, ln]], 0)
            v = jnp.concatenate([own_ref[0, :, lv], got_ref[0, :, lv]], 0)
            q2 = two_heads(cq_ref[sl, ln])
            probs = cross_probs(q2, k, limits)
            dq, dk, dv = attend_grad(q2, k, v, probs, da_ref[sl, ln])
            dcq_ref[sl, ln] = dq.astype(BF)
            dk, dv = dk.astype(BF), dv.astype(BF)
            down_ref[0, :, ln] = dk[:half]
            dgot_ref[0, :, ln] = dk[half:]
            down_ref[0, :, lv] = dv[:half]
            dgot_ref[0, :, lv] = dv[half:]

        @pl.when(c == pl.num_programs(0) - 1)
        def _():
            def finish(i):
                sl = rows(i, 256)
                part = nt(dcq_ref[sl, :], wq_ref[...])
                dh_ref[sl, :] = part
                dsend_ref[sl, :] = part.astype(BF)

            loop(t // 256, finish)

    blk = ((1, half, d), lambda c, *_: (c, 0, 0))
    ins = [whole(grad), whole(n_own), whole(n_got), whole(x3), whole(gain3), whole(cq)]
    ins += [(wq, (d, h2), lambda c, ids, *_: (0, ids[0])), (wco, (h2, d), lambda c, ids, *_: (ids[0], 0))]
    ins += [(kv_own,) + blk, (kv_got,) + blk]
    outs = [
        out_whole((t, d), F32),
        out_whole((t, d), BF),
        out_whole((t, h2), BF),
        ((caps, half, d), BF) + blk,
        ((caps, half, d), BF) + blk,
        out_whole((t, d), F32),
        out_whole((t, d), BF),
        out_whole((2, 8, d), F32),
    ]
    return call(
        "cross_grad", body, (caps,), [ids, counts], ins, outs,
        scratch=[pltpu.VMEM((t, h2), BF)], flops=4 * t * d * h2 + 5e9,
    )


def self_grad(layer, ids, grad, h_own, h_got, x, gain_x, qkv, wqkv, wout):
    t, d = x.shape
    h2 = d // 2

    def body(ids_ref, gr_ref, p_ref, q_ref, x_ref, g_ref, qkv_ref, own, got, o_own, o_got,
             dz_ref, da_ref, dqkv_ref, dh_ref, dsend_ref, sums_ref, datt_ref):
        j = pl.program_id(0)

        @pl.when(j == 0)
        def _():
            sums_ref[...] = jnp.zeros_like(sums_ref)

            def chunk(i):
                sl = rows(i, CHUNK)
                dh = p_ref[sl, :] + q_ref[sl, :].astype(F32)
                dv, dhn = norm_grad(x_ref[sl, :].astype(F32), g_ref[...], dh)
                dz = gr_ref[sl, :].astype(F32) + dv
                dz_ref[sl, :] = dz
                da_ref[sl, :] = dz.astype(BF)
                sums_ref[0] += fold(dhn)
                sums_ref[1] += fold(dh)

            loop(t // CHUNK, chunk)
            wo = pick(ids_ref, layer, o_own, o_got)

            def project(i):
                sl = rows(i, 256)
                datt_ref[sl, :] = nt(da_ref[sl, :], wo).astype(BF)

            loop(t // 256, project)

            def block(i):
                sl = rows(i, PAIR_ROWS)
                for p in range(h2 // LANES):
                    ln = slice(p * LANES, (p + 1) * LANES)
                    k, v = qkv_ref[1, sl, ln], qkv_ref[2, sl, ln]
                    q2 = two_heads(qkv_ref[0, sl, ln])
                    dq, dk, dv = attend_grad(q2, k, v, self_probs(q2, k), datt_ref[sl, ln])
                    dqkv_ref[0, sl, ln] = dq.astype(BF)
                    dqkv_ref[1, sl, ln] = dk.astype(BF)
                    dqkv_ref[2, sl, ln] = dv.astype(BF)

            loop(t // PAIR_ROWS, block)

        w = pick(ids_ref, layer, own, got)

        def back(i):
            sl = rows(i, 256)
            part = nt(dqkv_ref[j, sl, :], w)

            @pl.when(j == 0)
            def _():
                dh_ref[sl, :] = part

            @pl.when(j > 0)
            def _():
                total = dh_ref[sl, :] + part
                dh_ref[sl, :] = total
                dsend_ref[sl, :] = total.astype(BF)

        loop(t // 256, back)

    ins = [whole(grad), whole(h_own), whole(h_got), whole(x), whole(gain_x), whole(qkv)]
    ins += wqkv.cols(lambda j, s: 2 * j + s, 3) + wout.rowblocks(lambda j, s: s)[:1]
    ins += [whole(wout.got)]
    outs = [
        out_whole((t, d), F32),
        out_whole((t, d), BF),
        out_whole((3, t, h2), BF),
        out_whole((t, d), F32),
        out_whole((t, d), BF),
        out_whole((2, 8, d), F32),
    ]
    return call(
        f"self_grad_{layer}", body, (3,), [ids], ins, outs,
        scratch=[pltpu.VMEM((t, h2), BF)], flops=2 * t * d * 4 * h2 + 5e8,
    )


def text_grad(grad, h_own, h_got, x, gain):
    t, d = x.shape

    def body(gr_ref, p_ref, q_ref, x_ref, g_ref, dx_ref, sums_ref):
        sums_ref[...] = jnp.zeros_like(sums_ref)

        def chunk(i):
            sl = rows(i, CHUNK)
            dh = p_ref[sl, :] + q_ref[sl, :].astype(F32)
            dv, dhn = norm_grad(x_ref[sl, :].astype(F32), g_ref[...], dh)
            dx_ref[sl, :] = gr_ref[sl, :] + dv
            sums_ref[0] += fold(dhn)
            sums_ref[1] += fold(dh)

        loop(t // CHUNK, chunk)

    ins = [whole(a) for a in (grad, h_own, h_got, x, gain)]
    outs = [out_whole((t, d), F32), out_whole((2, 8, d), F32)]
    return call("text_grad", body, (1,), [], ins, outs)


def orders(count):
    bits = [1 << i for i in range(count.bit_length() - 1)]
    third = [bits[2], bits[0], bits[1]] + bits[3:]
    return [bits, [bits[1], bits[0]] + bits[2:], third]


def pieces(order, count):
    result, left = [], list(range(count))
    rank = lambda r: [0 if r & b else 1 for b in order]
    for bit in order:
        result.append(sorted([r for r in left if r & bit], key=rank))
        left = [r for r in left if not r & bit]
    return result + [left]


def halving(parts, order, sent=BF):
    count = lax.axis_size("dp")
    for step, bit in enumerate(order):
        arrived = lax.ppermute(parts[step].astype(sent), "dp", [(i, i ^ bit) for i in range(count)])
        at = 0
        for later in range(step + 1, len(parts)):
            size = parts[later].shape[0]
            parts[later] = parts[later].astype(F32) + arrived[at : at + size].astype(F32)
            at += size
    return parts[-1][0].astype(F32)


def weight_kernel(name, ids, ins, row_count, count, fill, flops):
    cols = 3 * LANES
    plan = [pieces(o, count) for o in orders(count)]
    flat = [(k, piece) for k in range(3) for piece in plan[k]]

    def body(ids_ref, *refs):
        scr = refs[-1]
        me = ids_ref[1]

        def put(dest, first, block):
            scr[dest ^ me, pl.ds(first, block.shape[0]), :] = block

        fill(ids_ref, refs[: len(ins)], put)
        for out, (k, piece) in zip(refs[len(ins) : -1], flat):
            for at, rel in enumerate(piece):
                out[at] = scr[rel, :, k * LANES : (k + 1) * LANES].astype(BF)

    outs = [out_whole((len(piece), row_count, LANES), BF) for _, piece in flat]
    got = call(
        name, body, (1,), [ids], [whole(a) for a in ins], outs,
        scratch=[pltpu.VMEM((count, row_count, cols), F32)], flops=flops,
    )
    step = len(plan[0])
    return [got[i * step : (i + 1) * step] for i in range(3)]


def reduced(parts, count):
    sums = [halving(list(p), o) for p, o in zip(parts, orders(count))]
    return jnp.concatenate(sums, -1)


def up_down_weights(layer, ids, normed, du, act_own, act_got, dm, count):
    t, d = normed.shape
    fh = du.shape[1]
    h2 = d // 2
    up_rows, down_rows = d // count, 2 * fh // count
    units = fh // h2
    half_dest = count // 2

    def fill(ids_ref, refs, put):
        n_ref, du_ref, own_ref, got_ref, dm_ref = refs

        def up(j):
            w = tn(n_ref[...], du_ref[:, lane(j * h2, h2)])
            for dest in range(count):
                put(dest, pl.multiple_of(j * up_rows, up_rows), w[dest * up_rows : (dest + 1) * up_rows])

        loop(units, up)
        base = units * up_rows
        s = ids_ref[0]
        dm_half = dm_ref[:, lane(s * h2, h2)]
        per = h2 // down_rows

        def down(j):
            for ref, side in ((own_ref, s), (got_ref, 1 - s)):
                w = tn(ref[:, lane(j * h2, h2)], dm_half)
                for i in range(per):
                    put(side * half_dest + j * per + i, base, w[i * down_rows : (i + 1) * down_rows])

        loop(fh // h2, down)

    return weight_kernel(
        f"mlp_weights_{layer}", ids, [normed, du, act_own, act_got, dm],
        units * up_rows + down_rows, count, fill, 4 * t * d * fh,
    )


def self_weights(layer, ids, h, dqkv, att_own, att_got, da, count):
    t, d = h.shape
    h2 = d // 2
    each = d // count
    half_dest = count // 2

    def fill(ids_ref, refs, put):
        h_ref, dqkv_ref, own_ref, got_ref, da_ref = refs

        def one(j):
            w = tn(h_ref[...], dqkv_ref[j])
            for dest in range(count):
                put(dest, pl.multiple_of(j * each, each), w[dest * each : (dest + 1) * each])

        loop(3, one)
        s = ids_ref[0]
        da_half = da_ref[:, lane(s * h2, h2)]
        for ref, side in ((own_ref, s), (got_ref, 1 - s)):
            w = tn(ref[...], da_half)
            for i in range(half_dest):
                put(side * half_dest + i, 3 * each, w[i * each : (i + 1) * each])

    return weight_kernel(
        f"self_weights_{layer}", ids, [h, dqkv, att_own, att_got, da], 4 * each, count, fill,
        8 * t * d * h2,
    )


def cross_weights(ids, h, dcq, att_own, att_got, dc, count):
    t, d = h.shape
    h2 = d // 2
    each = h2 // count

    def fill(ids_ref, refs, put):
        h_ref, dcq_ref, own_ref, got_ref, dc_ref = refs
        w = tn(h_ref[...], dcq_ref[...])
        for half in range(2):
            for dest in range(count):
                at = half * h2 + dest * each
                put(dest, half * each, w[at : at + each])
        s = ids_ref[0]
        dc_half = dc_ref[:, lane(s * h2, h2)]
        for ref, side in ((own_ref, s), (got_ref, 1 - s)):
            w = tn(ref[...], dc_half)
            for dest in range(count):
                put(dest, pl.multiple_of((2 + side) * each, each), w[dest * each : (dest + 1) * each])

    return weight_kernel(
        "cross_weights", ids, [h, dcq, att_own, att_got, dc], 4 * each, count, fill, 4 * t * d * h2
    )


def key_value_weights(ids, r_own, r_got, g_own, g_got, count):
    caps, half, d = r_own.shape
    h2 = d // 2
    each = h2 // count
    cols = 3 * LANES
    plan = [pieces(o, count) for o in orders(count)]
    flat = [(k, piece) for k in range(3) for piece in plan[k]]

    def body(ids_ref, ro, rg, go, gg, *refs):
        outs, scr, acc = refs[:-2], refs[-2], refs[-1]
        c = pl.program_id(0)
        me = ids_ref[1]

        @pl.when(c == 0)
        def _():
            acc[...] = jnp.zeros_like(acc)

        def add(i):
            sl = rows(i, 256)
            acc[sl, :] += tn(ro[0, :, lane(i * 256, 256)], go[0]) + tn(rg[0, :, lane(i * 256, 256)], gg[0])

        loop(d // 256, add)

        @pl.when(c == pl.num_programs(0) - 1)
        def _():
            for kind in range(2):
                for part in range(2):
                    for dest in range(count):
                        at = part * h2 + dest * each
                        first = (2 * kind + part) * each
                        scr[dest ^ me, first : first + each, :] = acc[
                            at : at + each, kind * h2 : (kind + 1) * h2
                        ]
            for out, (k, piece) in zip(outs, flat):
                for at, rel in enumerate(piece):
                    out[at] = scr[rel, :, k * LANES : (k + 1) * LANES].astype(BF)

    blk = ((1, half, d), lambda c, *_: (c, 0, 0))
    ins = [(a,) + blk for a in (r_own, r_got, g_own, g_got)]
    outs = [out_whole((len(piece), 4 * each, LANES), BF) for _, piece in flat]
    got = call(
        "key_value_weights", body, (caps,), [ids], ins, outs,
        scratch=[pltpu.VMEM((count, 4 * each, cols), F32), pltpu.VMEM((d, d), F32)],
        flops=4 * caps * half * d * d,
    )
    step = len(plan[0])
    return [got[i * step : (i + 1) * step] for i in range(3)]


def plain_sums(s, count, mlp2, cross, attn2, mlp1, image, attn1):
    scatter = lambda g: lax.psum_scatter(g, "dp", scatter_dimension=0, tiled=True)

    def full(act):
        come = swap(act)
        return jnp.concatenate([jnp.where(s == 0, act, come), jnp.where(s == 0, come, act)], 1)

    def side(grad):
        h2 = grad.shape[1] // 2
        return lax.dynamic_slice(grad, (0, s * h2), (grad.shape[0], h2))

    def stacked(w, h2):
        return jnp.concatenate([w[:, i : i + h2] for i in range(0, w.shape[1], h2)], 0)

    def by_section(w):
        parts = w.reshape(2, count, -1, w.shape[1]).swapaxes(0, 1)
        return scatter(parts.reshape(w.shape))

    def mlp(n, du, act, dm):
        return jnp.concatenate(
            [stacked(scatter(tn(n, du)), n.shape[1] // 2), scatter(tn(full(act), side(dm)))], 0
        )

    def attn(h, dqkv, att, da):
        return jnp.concatenate(
            [scatter(tn(h, dqkv[j])) for j in range(3)] + [scatter(tn(full(att), side(da)))], 0
        )

    h, dcq, att, dc = cross
    r_own, r_got, g_own, g_got = [x.reshape(-1, x.shape[-1]) for x in image]
    w_kv = tn(r_own, g_own) + tn(r_got, g_got)
    h2 = dcq.shape[1]
    c = jnp.concatenate([by_section(tn(h, dcq)), by_section(tn(full(att), side(dc)))], 0)
    kv = jnp.concatenate([by_section(w_kv[:, :h2]), by_section(w_kv[:, h2:])], 0)
    return mlp(*mlp2), c, attn(*attn2), mlp(*mlp1), kv, attn(*attn1)


def swap(value):
    return lax.ppermute(value, "section", [(0, 1), (1, 0)])


def on_device(
    text, image, image_counts, cotangent,
    attn_norm_gain, attn_norm_bias, qkv_weight, attn_out_weight, mlp_norm_gain, mlp_norm_bias,
    up_weight, up_bias, down_weight, down_bias,
    cross_norm_gain, cross_norm_bias, cross_query, cross_key_value, cross_out,
):
    s = lax.axis_index("section")
    me = lax.axis_index("dp")
    count = lax.axis_size("dp")
    ids = jnp.stack([s, me]).astype(jnp.int32)
    t, d = text.shape
    h2 = d // 2
    caps, half = image.shape[:2]
    ff = up_bias.shape[1]
    fh = ff // 2
    other = 1 - s

    w_qkv, w_out, w_up, w_down = qkv_weight[0], attn_out_weight[0], up_weight[0], down_weight[0]
    vec_own = jnp.concatenate(
        [attn_norm_gain, attn_norm_bias, mlp_norm_gain, mlp_norm_bias, down_bias, up_bias], 1
    )
    vec_got = swap(vec_own)
    got_qkv = swap(
        jnp.concatenate(
            [lax.dynamic_slice(w_qkv, (0, (2 * j + other) * h2), (d, h2)) for j in range(3)], 1
        )
    )
    got_out = swap(lax.dynamic_slice(w_out, (other * h2, 0), (h2, d)))
    got_up = swap(lax.dynamic_slice(w_up, (0, other * fh), (d, fh)))
    got_down = swap(lax.dynamic_slice(w_down, (other * fh, 0), (fh, d)))

    vectors = []
    for layer in range(2):
        v = jnp.where(s == layer, vec_own, vec_got)
        parts = [v[:, i * d : (i + 1) * d] for i in range(5)]
        parts.append(lax.dynamic_slice(v, (0, 5 * d + s * fh), (1, fh)))
        vectors.append(parts)
    halves = []
    for layer in range(2):
        halves.append(
            (
                Half(layer, w_qkv, got_qkv, h2),
                Half(layer, w_out, got_out, h2),
                Half(layer, w_up, got_up, h2),
                Half(layer, w_down, got_down, h2),
            )
        )
    gain_i, gain_t = cross_norm_gain[0:1], cross_norm_gain[1:2]
    bias_i, bias_t = cross_norm_bias[0:1], cross_norm_bias[1:2]

    r_own, kv_own, kv_send = key_value(ids, image, gain_i, bias_i, cross_key_value)
    kv_got = swap(kv_send)
    r_got = swap(r_own)

    ag1, ab1, mg1, mb1, bd1, bu1 = vectors[0]
    qw1, ow1, uw1, dw1 = halves[0]
    ag2, ab2, mg2, mb2, bd2, bu2 = vectors[1]
    qw2, ow2, uw2, dw2 = halves[1]

    h1, qkv1, att1, part, send = self_fwd(0, ids, [text], ag1, ab1, qw1, ow1)
    x1, n1, part, send = mlp_fwd(0, ids, text, part, swap(send), mg1, mb1, uw1, bu1, dw1, bd1)
    h2n, qkv2, att2, part, send, z = self_fwd(1, ids, [x1, part, swap(send)], ag2, ab2, qw2, ow2)
    z2, ch, cq, catt, part, send = cross_fwd(
        ids, image_counts, z, part, swap(send), gain_t, bias_t, cross_query, cross_out, kv_own, kv_got
    )
    (act2, du2, dpart, dsend, sums_m2, bup2, z3, n2, mpart, msend) = mlp_grad(
        1, ids, [z2, part, swap(send), cotangent], mg2, mb2, uw2, bu2, dw2, bd2
    )
    y = z3 + mpart + swap(msend).astype(F32)
    layer_out = jnp.where(s == 0, z, y.astype(BF))

    (dz3, dc, dcq, dkv_own, dkv_send, cpart, csend, sums_n2) = cross_grad(
        ids, image_counts, cotangent, dpart, swap(dsend), z3, mg2, cq, cross_query, cross_out, kv_own, kv_got
    )
    dz2, da2, dqkv2, hpart, hsend, sums_c = self_grad(
        1, ids, dz3, cpart, swap(csend), z2, gain_t, qkv2, qw2, ow2
    )
    act1, du1, npart, nsend, sums_a2, bup1, dz = mlp_grad(
        0, ids, [dz2, hpart, swap(hsend), z, ag2, n1], mg1, mb1, uw1, bu1, dw1, bd1
    )
    dx1, da1, dqkv1, hpart, hsend, sums_n1 = self_grad(
        0, ids, dz, npart, swap(nsend), x1, mg1, qkv1, qw1, ow1
    )
    dtext, sums_a1 = text_grad(dx1, hpart, swap(hsend), text, ag1)

    dkv_mine = swap(dkv_send)
    image_grad, sums_i = key_value_grad(ids, image, gain_i, dkv_own, dkv_mine, cross_key_value)
    input_grad = jnp.where(s == 0, dtext, dz.astype(F32))

    if d // count == 48:
        m2 = reduced(up_down_weights(1, ids, n2, du2, act2, swap(act2), cotangent, count), count)
        c2 = reduced(cross_weights(ids, ch, dcq, catt, swap(catt), dc, count), count)
        a2 = reduced(self_weights(1, ids, h2n, dqkv2, att2, swap(att2), da2, count), count)
        m1 = reduced(up_down_weights(0, ids, n1, du1, act1, swap(act1), dz, count), count)
        kv = reduced(key_value_weights(ids, r_own, r_got, dkv_own, dkv_send, count), count)
        a1 = reduced(self_weights(0, ids, h1, dqkv1, att1, swap(att1), da1, count), count)
    else:
        m2, c2, a2, m1, kv, a1 = plain_sums(
            s, count, (n2, du2, act2, cotangent), (ch, dcq, catt, dc), (h2n, dqkv2, att2, da2),
            (n1, du1, act1, dz), (r_own, r_got, dkv_own, dkv_send), (h1, dqkv1, att1, da1),
        )

    each = d // count
    small = each // 2
    first = jnp.concatenate([m1, a1], 0)
    second = jnp.concatenate([m2, a2], 0)
    mine = jnp.where(s == 0, first, second)
    theirs = swap(jnp.where(s == 0, second, first))
    left = jnp.where(s == 0, mine, theirs)
    right = jnp.where(s == 0, theirs, mine)
    units = fh // h2
    both = lambda a, b: jnp.concatenate([left[a:b], right[a:b]], 1)

    def columns(start, number):
        return [x[start + i * each : start + (i + 1) * each] for x in (left, right) for i in range(number)]

    g_up = jnp.concatenate(columns(0, units), 1)
    at = units * each
    wide = ff // count
    g_down = both(at, at + wide)
    at += wide
    g_qkv = jnp.concatenate(
        [x[at + i * each : at + (i + 1) * each] for i in range(3) for x in (left, right)], 1
    )
    g_out = both(at + 3 * each, at + 4 * each)

    cross = jnp.concatenate([c2, kv], 0).reshape(4, 2, small, h2)
    keep = lax.dynamic_index_in_dim(cross, s, 1, False)
    come = swap(lax.dynamic_index_in_dim(cross, other, 1, False))
    cross = jnp.concatenate(
        [jnp.where(s == 0, keep, come), jnp.where(s == 0, come, keep)], 2
    )
    g_cq, g_co = cross[0], cross[1]
    g_kv = jnp.concatenate([cross[2], cross[3]], 1)

    bup = [jnp.sum(b, 0) for b in (bup1, bup2)]
    bup_mine = jnp.where(s == 0, bup[0], bup[1])
    bup_come = swap(jnp.where(s == 0, bup[1], bup[0]))
    bup = jnp.concatenate(
        [jnp.where(s == 0, bup_mine, bup_come), jnp.where(s == 0, bup_come, bup_mine)]
    )
    sums_i = sums_i + swap(sums_i)
    pair = lambda a, b: jnp.sum(jnp.where(s == 0, a, b), 0).reshape(count, -1)
    split = lambda v: jnp.sum(v, 0).reshape(2, count, -1).swapaxes(0, 1).reshape(count, -1)
    packed = [
        pair(sums_a1[0], sums_a2[0]), pair(sums_a1[1], sums_a2[1]),
        pair(sums_n1[0], sums_n2[0]), pair(sums_n1[1], sums_n2[1]),
        pair(sums_a2[2], sums_m2[2]), bup.reshape(count, -1),
        split(sums_i[0]), split(sums_c[0]), split(sums_i[1]), split(sums_c[1]),
    ]
    widths = [v.shape[1] for v in packed]
    packed = jnp.take(jnp.concatenate(packed, 1), jnp.arange(count, dtype=jnp.int32) ^ me, axis=0)
    order = orders(count)[0]
    vec = halving([packed[jnp.array(p)] for p in pieces(order, count)], order, F32)
    cut, at = [], 0
    for w in widths:
        cut.append(vec[at : at + w])
        at += w
    own = lambda v: lax.dynamic_slice(v, (s * small,), (small,))
    return (
        layer_out[None], input_grad[None], image_grad,
        cut[0][None], cut[1][None], g_qkv[None], g_out[None], cut[2][None], cut[3][None],
        g_up[None], cut[5][None], g_down[None], cut[4][None],
        jnp.stack([own(cut[6]), own(cut[7])]), jnp.stack([own(cut[8]), own(cut[9])]),
        g_cq, g_kv, g_co,
    )


def solution(mesh):
    placed = (
        P("dp", None), P("dp", "section", None), P("dp"), P("dp", None),
        P("section", None), P("section", None), P("section", None, None), P("section", None, None),
        P("section", None), P("section", None), P("section", None, None), P("section", None),
        P("section", None, None), P("section", None), P(), P(), P(), P(), P(),
    )
    two, three = P("section", "dp"), P("section", "dp", None)
    last = P(("section", "dp"), None)
    return jax.shard_map(
        on_device,
        mesh=mesh,
        in_specs=placed,
        out_specs=(
            three, three, P("dp", "section", None), two, two, three, three, two, two, three, two,
            three, two, P(None, ("section", "dp")), P(None, ("section", "dp")), last, last, last,
        ),
        check_vma=False,
    )
```

```python
import jax
import jax.numpy as jnp
from jax import lax
from jax.experimental import pallas as pl
from jax.experimental.pallas import tpu as pltpu
from jax.sharding import PartitionSpec as P

HEAD_DIM = 64
SEQ = 64
LANES = 128
PAIR_ROWS = 2 * SEQ
CHUNK = 64
EPS = 1e-05
NEG = -1e30
SCALE = HEAD_DIM**-0.5
BF = jnp.bfloat16
F32 = jnp.float32


def nn(a, b):
    return lax.dot_general(a, b, (((1,), (0,)), ((), ())), preferred_element_type=F32)


def nt(a, b):
    return lax.dot_general(a, b, (((1,), (1,)), ((), ())), preferred_element_type=F32)


def tn(a, b):
    return lax.dot_general(a, b, (((0,), (0,)), ((), ())), preferred_element_type=F32)


def normalized(v):
    c = v - jnp.mean(v, -1, keepdims=True)
    inv = lax.rsqrt(jnp.mean(c * c, -1, keepdims=True) + EPS)
    return c * inv, inv


def norm(v, g, b):
    return normalized(v)[0] * g + b


def norm_grad(v, g, dh):
    nh, inv = normalized(v)
    e = dh * g
    dv = (e - jnp.mean(e, -1, keepdims=True) - nh * jnp.mean(e * nh, -1, keepdims=True)) * inv
    return dv, dh * nh


def fold(v):
    return jnp.sum(v.reshape(v.shape[0] // 8, 8, v.shape[1]), 0)


def gelu_pair(u):
    k = 0.7978845608028654
    t = jnp.tanh(k * (u + 0.044715 * u * u * u))
    g = 0.5 * u * (1.0 + t)
    dg = 0.5 * (1.0 + t) + 0.5 * u * (1.0 - t * t) * (k * (1.0 + 3 * 0.044715 * u * u))
    return g, dg


def gelu(u):
    k = 0.7978845608028654
    return 0.5 * u * (1.0 + jnp.tanh(k * (u + 0.044715 * u * u * u)))


def two_heads(v):
    low = lax.broadcasted_iota(jnp.int32, v.shape, 1) < HEAD_DIM
    zero = jnp.zeros_like(v)
    return jnp.concatenate([jnp.where(low, v, zero), jnp.where(low, zero, v)], 0)


def join_heads(v):
    half = v.shape[0] // 2
    low = lax.broadcasted_iota(jnp.int32, (half, LANES), 1) < HEAD_DIM
    return jnp.where(low, v[:half], v[half:])


def softmax(s):
    e = jnp.exp(s - jnp.max(s, -1, keepdims=True))
    return e / jnp.sum(e, -1, keepdims=True)


def self_probs(q2, k):
    s = nt(q2, k) * SCALE
    row = lax.broadcasted_iota(jnp.int32, s.shape, 0) % PAIR_ROWS
    col = lax.broadcasted_iota(jnp.int32, s.shape, 1)
    ok = (row // SEQ == col // SEQ) & (col <= row)
    return softmax(jnp.where(ok, s, NEG))


def cross_probs(q2, k, limits):
    s = nt(q2, k) * SCALE
    half = k.shape[0] // 2
    col = lax.broadcasted_iota(jnp.int32, s.shape, 1)
    bound = jnp.where(col < half, limits[0], limits[1] + half)
    return softmax(jnp.where(col < bound, s, NEG))


def attend_grad(q2, k, v, p, go):
    go2 = two_heads(go)
    dp = nt(go2, v)
    ds = (p * (dp - jnp.sum(p * dp, -1, keepdims=True))).astype(BF)
    dq = join_heads(nn(ds, k)) * SCALE
    dk = tn(ds, q2) * SCALE
    dv = tn(p.astype(BF), go2)
    return dq, dk, dv


def loop(count, body):
    def step(i, carry):
        body(i)
        return carry

    lax.fori_loop(0, count, step, 0)


def rows(i, size):
    return pl.ds(pl.multiple_of(i * size, size), size)


def lane(start, size):
    return pl.ds(pl.multiple_of(start, LANES), size)


def call(name, body, grid, scalars, ins, outs, scratch=(), flops=0):
    def spec(shape, item):
        block, index = item
        if block is None:
            block = shape
        if index is None:
            index = lambda *_, n=len(shape): (0,) * n
        return pl.BlockSpec(block, index)

    shapes = [jax.ShapeDtypeStruct(o[0], o[1]) for o in outs]
    moved = sum(a[0].size * a[0].dtype.itemsize for a in ins)
    moved += sum(s.size * s.dtype.itemsize for s in shapes)
    return pl.pallas_call(
        body,
        name=name,
        out_shape=shapes,
        grid_spec=pltpu.PrefetchScalarGridSpec(
            num_scalar_prefetch=len(scalars),
            grid=grid,
            in_specs=[spec(a[0].shape, a[1:]) for a in ins],
            out_specs=[spec(o[0], o[2:]) for o in outs],
            scratch_shapes=list(scratch),
        ),
        compiler_params=pltpu.CompilerParams(vmem_limit_bytes=56 << 20),
        cost_estimate=pl.CostEstimate(flops=int(flops), bytes_accessed=int(moved), transcendentals=0),
    )(*scalars, *[a[0] for a in ins])


def whole(a):
    return (a, None, None)


def out_whole(shape, dtype):
    return (shape, dtype, None, None)


class Half:
    def __init__(self, layer, own, got, width):
        self.layer, self.own, self.got, self.width = layer, own, got, width

    def cols(self, per):
        layer, width = self.layer, self.width
        d = self.own.shape[0]

        def own_map(j, ids, *_):
            return (0, jnp.where(ids[0] == layer, per(j, ids[0]), 0))

        def got_map(j, ids, *_):
            return (0, jnp.where(ids[0] == layer, 0, per(j, ids[0])))

        return [(self.own, (d, width), own_map), (self.got, (d, width), got_map)]

    def rowblocks(self, per):
        layer, width = self.layer, self.width
        d = self.own.shape[1]

        def own_map(j, ids, *_):
            return (jnp.where(ids[0] == layer, per(j, ids[0]), 0), 0)

        def got_map(j, ids, *_):
            return (jnp.where(ids[0] == layer, 0, per(j, ids[0])), 0)

        return [(self.own, (width, d), own_map), (self.got, (width, d), got_map)]


def pick(ids, layer, own_ref, got_ref):
    return jnp.where(ids[0] == layer, own_ref[...], got_ref[...])


def self_fwd(layer, ids, stream, gain, bias, wqkv, wout):
    first = len(stream) == 1
    t, d = stream[0].shape
    h2 = d // 2
    n_in = len(stream)

    def body(ids_ref, *refs):
        xs, refs = refs[:n_in], refs[n_in:]
        g_ref, b_ref, own, got, o_own, o_got = refs[:6]
        outs = refs[6:]
        h_ref, qkv_ref, att_ref, part_ref, send_ref = outs[:5]
        j = pl.program_id(0)

        @pl.when(j == 0)
        def _():
            def chunk(i):
                sl = rows(i, CHUNK)
                if first:
                    x = xs[0][sl, :].astype(F32)
                else:
                    z = (xs[0][sl, :] + xs[1][sl, :] + xs[2][sl, :].astype(F32)).astype(BF)
                    outs[5][sl, :] = z
                    x = z.astype(F32)
                h_ref[sl, :] = norm(x, g_ref[...], b_ref[...]).astype(BF)

            loop(t // CHUNK, chunk)

        w = pick(ids_ref, layer, own, got)

        def project(i):
            sl = rows(i, 256)
            qkv_ref[j, sl, :] = nn(h_ref[sl, :], w).astype(BF)

        loop(t // 256, project)

        @pl.when(j == 2)
        def _():
            def block(i):
                sl = rows(i, PAIR_ROWS)
                for p in range(h2 // LANES):
                    ln = slice(p * LANES, (p + 1) * LANES)
                    k = qkv_ref[1, sl, ln]
                    probs = self_probs(two_heads(qkv_ref[0, sl, ln]), k).astype(BF)
                    att_ref[sl, ln] = join_heads(nn(probs, qkv_ref[2, sl, ln])).astype(BF)

            loop(t // PAIR_ROWS, block)
            wo = pick(ids_ref, layer, o_own, o_got)

            def finish(i):
                sl = rows(i, 256)
                part = nn(att_ref[sl, :], wo)
                part_ref[sl, :] = part
                send_ref[sl, :] = part.astype(BF)

            loop(t // 256, finish)

    outs = [
        out_whole((t, d), BF),
        out_whole((3, t, h2), BF),
        out_whole((t, h2), BF),
        out_whole((t, d), F32),
        out_whole((t, d), BF),
    ]
    if not first:
        outs.append(out_whole((t, d), BF))
    ins = [whole(x) for x in stream] + [whole(gain), whole(bias)]
    ins += wqkv.cols(lambda j, s: 2 * j + s) + wout.rowblocks(lambda j, s: s)
    return call(
        f"self_fwd_{layer}", body, (3,), [ids], ins, outs, flops=2 * t * d * 4 * h2 + 2e8
    )


def mlp_fwd(layer, ids, x, a_own, a_got, gain, bias, wup, b_up, wdown, b_down):
    t, d = x.shape
    fh = b_up.shape[1]
    width = wup.width

    def body(ids_ref, x_ref, p_ref, q_ref, g_ref, b_ref, u_own, u_got, bu_ref, d_own, d_got, bd_ref,
             x1_ref, n_ref, part_ref, send_ref):
        j = pl.program_id(0)

        @pl.when(j == 0)
        def _():
            def chunk(i):
                sl = rows(i, CHUNK)
                x1 = x_ref[sl, :].astype(F32) + p_ref[sl, :] + q_ref[sl, :].astype(F32)
                x1_ref[sl, :] = x1
                n_ref[sl, :] = norm(x1, g_ref[...], b_ref[...]).astype(BF)
                part_ref[sl, :] = jnp.broadcast_to(
                    jnp.where(ids_ref[0] == 0, bd_ref[...], 0.0), (CHUNK, d)
                )

            loop(t // CHUNK, chunk)

        up = pick(ids_ref, layer, u_own, u_got)
        down = pick(ids_ref, layer, d_own, d_got)

        def tile(i):
            sl = rows(i, 128)
            u = nn(n_ref[sl, :], up) + bu_ref[...]
            part_ref[sl, :] += nn(gelu(u).astype(BF), down)

        loop(t // 128, tile)

        @pl.when(j == pl.num_programs(0) - 1)
        def _():
            def chunk(i):
                sl = rows(i, CHUNK)
                send_ref[sl, :] = part_ref[sl, :].astype(BF)

            loop(t // CHUNK, chunk)

    per = fh // width
    ins = [whole(x), whole(a_own), whole(a_got), whole(gain), whole(bias)]
    ins += wup.cols(lambda j, s: s * per + j)
    ins += [(b_up, (1, width), lambda j, *_: (0, j))]
    ins += wdown.rowblocks(lambda j, s: s * per + j)
    ins += [whole(b_down)]
    outs = [
        out_whole((t, d), F32),
        out_whole((t, d), BF),
        out_whole((t, d), F32),
        out_whole((t, d), BF),
    ]
    return call(f"mlp_fwd_{layer}", body, (per,), [ids], ins, outs, flops=4 * t * d * fh)


def mlp_grad(layer, ids, lead, gain, bias, wup, b_up, wdown, b_down):
    second = layer == 1
    t, d = lead[0].shape
    fh = b_up.shape[1]
    width = wup.width
    n_in = len(lead)

    def body(ids_ref, *refs):
        lead_refs, refs = refs[:n_in], refs[n_in:]
        g_ref, b_ref, u_own, u_got, bu_ref, d_own, d_got, bd_ref = refs[:8]
        outs = refs[8:]
        act_ref, du_ref, dn_ref, dsend_ref, sums_ref, bup_ref = outs[:6]
        extra = outs[6:]
        j = pl.program_id(0)

        @pl.when(j == 0)
        def _():
            sums_ref[...] = jnp.zeros_like(sums_ref)

            def chunk(i):
                sl = rows(i, CHUNK)
                if second:
                    x_ref, p_ref, q_ref, cot_ref = lead_refs
                    x = x_ref[sl, :] + p_ref[sl, :] + q_ref[sl, :].astype(F32)
                    extra[0][sl, :] = x
                    extra[1][sl, :] = norm(x, g_ref[...], b_ref[...]).astype(BF)
                    extra[2][sl, :] = jnp.broadcast_to(
                        jnp.where(ids_ref[0] == 0, bd_ref[...], 0.0), (CHUNK, d)
                    )
                    sums_ref[2] += fold(cot_ref[sl, :].astype(F32))
                else:
                    grad_ref, p_ref, q_ref, z_ref, zg_ref, n_ref = lead_refs
                    dh = p_ref[sl, :] + q_ref[sl, :].astype(F32)
                    dv, dhn = norm_grad(z_ref[sl, :].astype(F32), zg_ref[...], dh)
                    dz = (grad_ref[sl, :] + dv).astype(BF)
                    extra[0][sl, :] = dz
                    sums_ref[0] += fold(dhn)
                    sums_ref[1] += fold(dh)
                    sums_ref[2] += fold(dz.astype(F32))
                dn_ref[sl, :] = jnp.zeros((CHUNK, d), F32)

            loop(t // CHUNK, chunk)

        up = pick(ids_ref, layer, u_own, u_got)
        down = pick(ids_ref, layer, d_own, d_got)
        bup_ref[...] = jnp.zeros_like(bup_ref)
        n_src = extra[1] if second else lead_refs[5]
        dm_src = lead_refs[3] if second else extra[0]

        def tile(i):
            sl = rows(i, 128)
            u = nn(n_src[sl, :], up) + bu_ref[...]
            g, dg = gelu_pair(u)
            g = g.astype(BF)
            act_ref[sl, :] = g
            du = (nt(dm_src[sl, :], down) * dg).astype(BF)
            du_ref[sl, :] = du
            bup_ref[...] += fold(du.astype(F32))
            dn_ref[sl, :] += nt(du, up)
            if second:
                extra[2][sl, :] += nn(g, down)

        loop(t // 128, tile)

        @pl.when(j == pl.num_programs(0) - 1)
        def _():
            def chunk(i):
                sl = rows(i, CHUNK)
                dsend_ref[sl, :] = dn_ref[sl, :].astype(BF)
                if second:
                    extra[3][sl, :] = extra[2][sl, :].astype(BF)

            loop(t // CHUNK, chunk)

    per = fh // width
    ins = [whole(a) for a in lead] + [whole(gain), whole(bias)]
    ins += wup.cols(lambda j, s: s * per + j)
    ins += [(b_up, (1, width), lambda j, *_: (0, j))]
    ins += wdown.rowblocks(lambda j, s: s * per + j)
    ins += [whole(b_down)]
    outs = [
        ((t, fh), BF, (t, width), lambda j, *_: (0, j)),
        ((t, fh), BF, (t, width), lambda j, *_: (0, j)),
        out_whole((t, d), F32),
        out_whole((t, d), BF),
        out_whole((3, 8, d), F32),
        ((8, fh), F32, (8, width), lambda j, *_: (0, j)),
    ]
    if second:
        outs += [
            out_whole((t, d), F32),
            out_whole((t, d), BF),
            out_whole((t, d), F32),
            out_whole((t, d), BF),
        ]
    else:
        outs += [out_whole((t, d), BF)]
    return call(
        f"mlp_grad_{layer}", body, (per,), [ids], ins, outs,
        flops=(8 if second else 6) * t * d * fh,
    )


def key_value(ids, image, gain, bias, w):
    caps, half, d = image.shape
    h2 = d // 2

    def body(ids_ref, im_ref, g_ref, b_ref, k_own, v_own, k_oth, v_oth, r_ref, own_ref, oth_ref):
        def chunk(i):
            sl = rows(i, 96)
            r_ref[0, sl, :] = norm(im_ref[0, sl, :].astype(F32), g_ref[...], b_ref[...]).astype(BF)

        loop(half // 96, chunk)
        r = r_ref[0]
        own_ref[0, :, :h2] = nn(r, k_own[...]).astype(BF)
        own_ref[0, :, h2:] = nn(r, v_own[...]).astype(BF)
        oth_ref[0, :, :h2] = nn(r, k_oth[...]).astype(BF)
        oth_ref[0, :, h2:] = nn(r, v_oth[...]).astype(BF)

    part = lambda off: (w, (d, h2), lambda c, ids: (0, off(ids[0])))
    blk = ((1, half, d), lambda c, *_: (c, 0, 0))
    ins = [(image,) + blk, whole(gain), whole(bias)]
    ins += [
        part(lambda s: s), part(lambda s: 2 + s), part(lambda s: 1 - s), part(lambda s: 3 - s)
    ]
    outs = [((caps, half, d), BF) + blk] * 3
    return call("key_value", body, (caps,), [ids], ins, outs, flops=4 * caps * half * d * d)


def key_value_grad(ids, image, gain, g_own, g_oth, w):
    caps, half, d = image.shape
    h2 = d // 2

    def body(ids_ref, im_ref, g_ref, own_ref, oth_ref, k_own, v_own, k_oth, v_oth, dx_ref, sums_ref):
        @pl.when(pl.program_id(0) == 0)
        def _():
            sums_ref[...] = jnp.zeros_like(sums_ref)

        def chunk(i):
            sl = rows(i, 96)
            dr = nt(own_ref[0, sl, :h2], k_own[...]) + nt(own_ref[0, sl, h2:], v_own[...])
            dr += nt(oth_ref[0, sl, :h2], k_oth[...]) + nt(oth_ref[0, sl, h2:], v_oth[...])
            dv, dhn = norm_grad(im_ref[0, sl, :].astype(F32), g_ref[...], dr)
            dx_ref[0, sl, :] = dv
            sums_ref[0] += fold(dhn)
            sums_ref[1] += fold(dr)

        loop(half // 96, chunk)

    part = lambda off: (w, (d, h2), lambda c, ids: (0, off(ids[0])))
    blk = ((1, half, d), lambda c, *_: (c, 0, 0))
    ins = [(image,) + blk, whole(gain), (g_own,) + blk, (g_oth,) + blk]
    ins += [
        part(lambda s: s), part(lambda s: 2 + s), part(lambda s: 1 - s), part(lambda s: 3 - s)
    ]
    outs = [((caps, half, d), F32) + blk, out_whole((2, 8, d), F32)]
    return call("key_value_grad", body, (caps,), [ids], ins, outs, flops=4 * caps * half * d * d)


def patch_limits(ids_ref, counts_ref, c, half):
    s = ids_ref[0]
    return counts_ref[c] - s * half, counts_ref[c] - (1 - s) * half


def cross_fwd(ids, counts, z, a_own, a_got, gain, bias, wq, wco, kv_own, kv_got):
    caps, half, d = kv_own.shape
    h2 = d // 2
    t = z.shape[0]

    def body(ids_ref, cnt_ref, z_ref, p_ref, q_ref, g_ref, b_ref, wq_ref, wo_ref, own_ref, got_ref,
             z2_ref, h_ref, cq_ref, att_ref, part_ref, send_ref):
        c = pl.program_id(0)

        @pl.when(c == 0)
        def _():
            def chunk(i):
                sl = rows(i, CHUNK)
                x = z_ref[sl, :].astype(F32) + p_ref[sl, :] + q_ref[sl, :].astype(F32)
                z2_ref[sl, :] = x
                h_ref[sl, :] = norm(x, g_ref[...], b_ref[...]).astype(BF)

            loop(t // CHUNK, chunk)

            def project(i):
                sl = rows(i, 256)
                cq_ref[sl, :] = nn(h_ref[sl, :], wq_ref[...]).astype(BF)

            loop(t // 256, project)

        limits = patch_limits(ids_ref, cnt_ref, c, half)
        sl = rows(c, SEQ)
        for p in range(h2 // LANES):
            ln = slice(p * LANES, (p + 1) * LANES)
            lv = slice(h2 + p * LANES, h2 + (p + 1) * LANES)
            k = jnp.concatenate([own_ref[0, :, ln], got_ref[0, :, ln]], 0)
            v = jnp.concatenate([own_ref[0, :, lv], got_ref[0, :, lv]], 0)
            probs = cross_probs(two_heads(cq_ref[sl, ln]), k, limits).astype(BF)
            att_ref[sl, ln] = join_heads(nn(probs, v)).astype(BF)

        @pl.when(c == pl.num_programs(0) - 1)
        def _():
            def finish(i):
                sl = rows(i, 256)
                part = nn(att_ref[sl, :], wo_ref[...])
                part_ref[sl, :] = part
                send_ref[sl, :] = part.astype(BF)

            loop(t // 256, finish)

    blk = ((1, half, d), lambda c, *_: (c, 0, 0))
    ins = [whole(z), whole(a_own), whole(a_got), whole(gain), whole(bias)]
    ins += [(wq, (d, h2), lambda c, ids, *_: (0, ids[0])), (wco, (h2, d), lambda c, ids, *_: (ids[0], 0))]
    ins += [(kv_own,) + blk, (kv_got,) + blk]
    outs = [
        out_whole((t, d), F32),
        out_whole((t, d), BF),
        out_whole((t, h2), BF),
        out_whole((t, h2), BF),
        out_whole((t, d), F32),
        out_whole((t, d), BF),
    ]
    return call(
        "cross_fwd", body, (caps,), [ids, counts], ins, outs, flops=4 * t * d * h2 + 16e8
    )


def cross_grad(ids, counts, grad, n_own, n_got, x3, gain3, cq, wq, wco, kv_own, kv_got):
    caps, half, d = kv_own.shape
    h2 = d // 2
    t = x3.shape[0]

    def body(ids_ref, cnt_ref, gr_ref, p_ref, q_ref, x_ref, g_ref, cq_ref, wq_ref, wo_ref, own_ref, got_ref,
             dz_ref, dc_ref, dcq_ref, down_ref, dgot_ref, dh_ref, dsend_ref, sums_ref, da_ref):
        c = pl.program_id(0)

        @pl.when(c == 0)
        def _():
            sums_ref[...] = jnp.zeros_like(sums_ref)

            def chunk(i):
                sl = rows(i, CHUNK)
                dh = p_ref[sl, :] + q_ref[sl, :].astype(F32)
                dv, dhn = norm_grad(x_ref[sl, :], g_ref[...], dh)
                dz = gr_ref[sl, :].astype(F32) + dv
                dz_ref[sl, :] = dz
                dc_ref[sl, :] = dz.astype(BF)
                sums_ref[0] += fold(dhn)
                sums_ref[1] += fold(dh)

            loop(t // CHUNK, chunk)

            def project(i):
                sl = rows(i, 256)
                da_ref[sl, :] = nt(dc_ref[sl, :], wo_ref[...]).astype(BF)

            loop(t // 256, project)

        limits = patch_limits(ids_ref, cnt_ref, c, half)
        sl = rows(c, SEQ)
        for p in range(h2 // LANES):
            ln = slice(p * LANES, (p + 1) * LANES)
            lv = slice(h2 + p * LANES, h2 + (p + 1) * LANES)
            k = jnp.concatenate([own_ref[0, :, ln], got_ref[0, :, ln]], 0)
            v = jnp.concatenate([own_ref[0, :, lv], got_ref[0, :, lv]], 0)
            q2 = two_heads(cq_ref[sl, ln])
            probs = cross_probs(q2, k, limits)
            dq, dk, dv = attend_grad(q2, k, v, probs, da_ref[sl, ln])
            dcq_ref[sl, ln] = dq.astype(BF)
            dk, dv = dk.astype(BF), dv.astype(BF)
            down_ref[0, :, ln] = dk[:half]
            dgot_ref[0, :, ln] = dk[half:]
            down_ref[0, :, lv] = dv[:half]
            dgot_ref[0, :, lv] = dv[half:]

        @pl.when(c == pl.num_programs(0) - 1)
        def _():
            def finish(i):
                sl = rows(i, 256)
                part = nt(dcq_ref[sl, :], wq_ref[...])
                dh_ref[sl, :] = part
                dsend_ref[sl, :] = part.astype(BF)

            loop(t // 256, finish)

    blk = ((1, half, d), lambda c, *_: (c, 0, 0))
    ins = [whole(grad), whole(n_own), whole(n_got), whole(x3), whole(gain3), whole(cq)]
    ins += [(wq, (d, h2), lambda c, ids, *_: (0, ids[0])), (wco, (h2, d), lambda c, ids, *_: (ids[0], 0))]
    ins += [(kv_own,) + blk, (kv_got,) + blk]
    outs = [
        out_whole((t, d), F32),
        out_whole((t, d), BF),
        out_whole((t, h2), BF),
        ((caps, half, d), BF) + blk,
        ((caps, half, d), BF) + blk,
        out_whole((t, d), F32),
        out_whole((t, d), BF),
        out_whole((2, 8, d), F32),
    ]
    return call(
        "cross_grad", body, (caps,), [ids, counts], ins, outs,
        scratch=[pltpu.VMEM((t, h2), BF)], flops=4 * t * d * h2 + 5e9,
    )


def self_grad(layer, ids, grad, h_own, h_got, x, gain_x, qkv, wqkv, wout):
    t, d = x.shape
    h2 = d // 2

    def body(ids_ref, gr_ref, p_ref, q_ref, x_ref, g_ref, qkv_ref, own, got, o_own, o_got,
             dz_ref, da_ref, dqkv_ref, dh_ref, dsend_ref, sums_ref, datt_ref):
        j = pl.program_id(0)

        @pl.when(j == 0)
        def _():
            sums_ref[...] = jnp.zeros_like(sums_ref)

            def chunk(i):
                sl = rows(i, CHUNK)
                dh = p_ref[sl, :] + q_ref[sl, :].astype(F32)
                dv, dhn = norm_grad(x_ref[sl, :].astype(F32), g_ref[...], dh)
                dz = gr_ref[sl, :].astype(F32) + dv
                dz_ref[sl, :] = dz
                da_ref[sl, :] = dz.astype(BF)
                sums_ref[0] += fold(dhn)
                sums_ref[1] += fold(dh)

            loop(t // CHUNK, chunk)
            wo = pick(ids_ref, layer, o_own, o_got)

            def project(i):
                sl = rows(i, 256)
                datt_ref[sl, :] = nt(da_ref[sl, :], wo).astype(BF)

            loop(t // 256, project)

            def block(i):
                sl = rows(i, PAIR_ROWS)
                for p in range(h2 // LANES):
                    ln = slice(p * LANES, (p + 1) * LANES)
                    k, v = qkv_ref[1, sl, ln], qkv_ref[2, sl, ln]
                    q2 = two_heads(qkv_ref[0, sl, ln])
                    dq, dk, dv = attend_grad(q2, k, v, self_probs(q2, k), datt_ref[sl, ln])
                    dqkv_ref[0, sl, ln] = dq.astype(BF)
                    dqkv_ref[1, sl, ln] = dk.astype(BF)
                    dqkv_ref[2, sl, ln] = dv.astype(BF)

            loop(t // PAIR_ROWS, block)

        w = pick(ids_ref, layer, own, got)

        def back(i):
            sl = rows(i, 256)
            part = nt(dqkv_ref[j, sl, :], w)

            @pl.when(j == 0)
            def _():
                dh_ref[sl, :] = part

            @pl.when(j > 0)
            def _():
                total = dh_ref[sl, :] + part
                dh_ref[sl, :] = total
                dsend_ref[sl, :] = total.astype(BF)

        loop(t // 256, back)

    ins = [whole(grad), whole(h_own), whole(h_got), whole(x), whole(gain_x), whole(qkv)]
    ins += wqkv.cols(lambda j, s: 2 * j + s) + wout.rowblocks(lambda j, s: s)
    outs = [
        out_whole((t, d), F32),
        out_whole((t, d), BF),
        out_whole((3, t, h2), BF),
        out_whole((t, d), F32),
        out_whole((t, d), BF),
        out_whole((2, 8, d), F32),
    ]
    return call(
        f"self_grad_{layer}", body, (3,), [ids], ins, outs,
        scratch=[pltpu.VMEM((t, h2), BF)], flops=2 * t * d * 4 * h2 + 5e8,
    )


def text_grad(ids, grad, h_own, h_got, x, gain, dz):
    t, d = x.shape

    def body(ids_ref, gr_ref, p_ref, q_ref, x_ref, g_ref, dz_ref, dx_ref, sums_ref):
        sums_ref[...] = jnp.zeros_like(sums_ref)

        def chunk(i):
            sl = rows(i, CHUNK)
            dh = p_ref[sl, :] + q_ref[sl, :].astype(F32)
            dv, dhn = norm_grad(x_ref[sl, :].astype(F32), g_ref[...], dh)
            dx_ref[sl, :] = jnp.where(ids_ref[0] == 0, gr_ref[sl, :] + dv, dz_ref[sl, :].astype(F32))
            sums_ref[0] += fold(dhn)
            sums_ref[1] += fold(dh)

        loop(t // CHUNK, chunk)

    ins = [whole(a) for a in (grad, h_own, h_got, x, gain, dz)]
    outs = [out_whole((t, d), F32), out_whole((2, 8, d), F32)]
    return call("text_grad", body, (1,), [ids], ins, outs)


def paths(count, turn):
    bits = list(range(count.bit_length() - 1))
    near, far = bits[:3], bits[3:]
    return [near[k % 3 :] + near[: k % 3] + far for k in (turn, turn + 1)]


def route(s, me, count, turn):
    first, second = paths(count, turn)
    bits = [jnp.where(s == 0, a, b) for a, b in zip(first, second)]
    return jnp.stack([s, me] + bits).astype(jnp.int32)


def tie(value, *after):
    return lax.optimization_barrier((value, *after))[0]


class Sum:
    def __init__(self, parts, count, turn, own_order=True):
        self.parts, self.count, self.paths = parts, count, paths(count, turn)
        if not own_order:
            self.paths = [self.paths[0]] * 2
        self.arrived, self.result = [], None
        self.send(parts[0])

    def send(self, value):
        self.outgoing = value
        step, n = len(self.arrived), self.count
        perm = [(s * n + i, s * n + (i ^ (1 << self.paths[s][step]))) for s in range(2) for i in range(n)]
        self.flight = lax.ppermute(value, ("section", "dp"), perm)

    def land(self, *after):
        if self.result is not None:
            return
        self.arrived.append(tie(self.flight, *after) if after else self.flight)
        step = len(self.arrived)
        low = self.count >> (step + 1)
        high = max(2 * low, 1)
        total = self.parts[step].astype(F32)
        for a in self.arrived:
            total = total + a[low:high].astype(F32)
        if step < len(self.parts) - 1:
            self.send(total.astype(self.parts[0].dtype))
        else:
            self.result = self.outgoing = total[0]


def finish(sums):
    while any(x.result is None for x in sums):
        for x in sums:
            x.land()


def slots(outs, scr):
    high = scr.shape[0]
    for out in outs[:-1]:
        low = high // 2

        def one(i, out=out, low=low):
            out[i] = scr[low + i].astype(BF)

        loop(high - low, one)
        high = low
    outs[-1][0] = scr[0].astype(BF)


def putter(ids_ref, scr):
    def put(dest, first, block):
        rel, slot = dest ^ ids_ref[1], 0
        for k in range(scr.shape[0].bit_length() - 1):
            slot = slot * 2 + ((rel >> ids_ref[2 + k]) & 1)
        scr[slot, pl.ds(first, block.shape[0]), :] = block.astype(scr.dtype)

    return put


def slot_outs(count, row_count, cols):
    steps = count.bit_length() - 1
    sizes = [count >> k for k in range(1, steps + 1)] + [1]
    return [out_whole((n, row_count, cols), BF) for n in sizes]


def weight_kernel(name, ids, ins, row_count, count, fill, flops):
    cols = 3 * LANES

    def body(ids_ref, *refs):
        scr = refs[-1]
        fill(ids_ref, refs[: len(ins)], putter(ids_ref, scr))
        slots(refs[len(ins) : -1], scr)

    return call(
        name, body, (1,), [ids], [whole(a) for a in ins], slot_outs(count, row_count, cols),
        scratch=[pltpu.VMEM((count, row_count, cols), BF)], flops=flops,
    )


def up_down_weights(layer, ids, normed, du, act_own, act_got, dm, count):
    t, d = normed.shape
    fh = du.shape[1]
    h2 = d // 2
    up_rows, down_rows = d // count, 2 * fh // count
    units = fh // h2
    half_dest = count // 2

    def fill(ids_ref, refs, put):
        n_ref, du_ref, own_ref, got_ref, dm_ref = refs

        def up(j):
            w = tn(n_ref[...], du_ref[:, lane(j * h2, h2)])
            for dest in range(count):
                put(dest, pl.multiple_of(j * up_rows, up_rows), w[dest * up_rows : (dest + 1) * up_rows])

        loop(units, up)
        base = units * up_rows
        s = ids_ref[0]
        dm_half = dm_ref[:, lane(s * h2, h2)]
        per = h2 // down_rows

        def down(j):
            for ref, side in ((own_ref, s), (got_ref, 1 - s)):
                w = tn(ref[:, lane(j * h2, h2)], dm_half)
                for i in range(per):
                    put(side * half_dest + j * per + i, base, w[i * down_rows : (i + 1) * down_rows])

        loop(fh // h2, down)

    return weight_kernel(
        f"mlp_weights_{layer}", ids, [normed, du, act_own, act_got, dm],
        units * up_rows + down_rows, count, fill, 4 * t * d * fh,
    )


def self_weights(layer, ids, h, dqkv, att_own, att_got, da, count):
    t, d = h.shape
    h2 = d // 2
    each = d // count
    half_dest = count // 2

    def fill(ids_ref, refs, put):
        h_ref, dqkv_ref, own_ref, got_ref, da_ref = refs

        def one(j):
            w = tn(h_ref[...], dqkv_ref[j])
            for dest in range(count):
                put(dest, pl.multiple_of(j * each, each), w[dest * each : (dest + 1) * each])

        loop(3, one)
        s = ids_ref[0]
        da_half = da_ref[:, lane(s * h2, h2)]
        for ref, side in ((own_ref, s), (got_ref, 1 - s)):
            w = tn(ref[...], da_half)
            for i in range(half_dest):
                put(side * half_dest + i, 3 * each, w[i * each : (i + 1) * each])

    return weight_kernel(
        f"self_weights_{layer}", ids, [h, dqkv, att_own, att_got, da], 4 * each, count, fill,
        8 * t * d * h2,
    )


def cross_weights(ids, h, dcq, att_own, att_got, dc, r_own, r_got, g_own, g_got, count):
    t = h.shape[0]
    caps, half, d = r_own.shape
    h2 = d // 2
    each = h2 // count
    n_in = 9

    def body(ids_ref, *refs):
        h_ref, dcq_ref, own_ref, got_ref, dc_ref, ro, rg, go, gg = refs[:n_in]
        outs, scr, acc = refs[n_in:-2], refs[-2], refs[-1]
        c = pl.program_id(0)

        @pl.when(c == 0)
        def _():
            acc[...] = jnp.zeros_like(acc)

        def add(i):
            sl = rows(i, 256)
            acc[sl, :] += tn(ro[0, :, lane(i * 256, 256)], go[0]) + tn(rg[0, :, lane(i * 256, 256)], gg[0])

        loop(d // 256, add)

        @pl.when(c == pl.num_programs(0) - 1)
        def _():
            put = putter(ids_ref, scr)
            w = tn(h_ref[...], dcq_ref[...])
            for half_row in range(2):
                for dest in range(count):
                    at = half_row * h2 + dest * each
                    put(dest, half_row * each, w[at : at + each])
            s = ids_ref[0]
            dc_half = dc_ref[:, lane(s * h2, h2)]
            for ref, side in ((own_ref, s), (got_ref, 1 - s)):
                w = tn(ref[...], dc_half)
                for dest in range(count):
                    put(dest, pl.multiple_of((2 + side) * each, each), w[dest * each : (dest + 1) * each])
            for kind in range(2):
                for part in range(2):
                    for dest in range(count):
                        at = part * h2 + dest * each
                        put(
                            dest, (4 + 2 * kind + part) * each,
                            acc[at : at + each, kind * h2 : (kind + 1) * h2],
                        )
            slots(outs, scr)

    blk = ((1, half, d), lambda c, *_: (c, 0, 0))
    ins = [whole(a) for a in (h, dcq, att_own, att_got, dc)]
    ins += [(a,) + blk for a in (r_own, r_got, g_own, g_got)]
    return call(
        "cross_weights", body, (caps,), [ids], ins, slot_outs(count, 8 * each, h2),
        scratch=[pltpu.VMEM((count, 8 * each, h2), F32), pltpu.VMEM((d, d), F32)],
        flops=4 * caps * half * d * d,
    )


def pack_vectors(vectors):
    width = sum(v.shape[1] for v in vectors)

    def body(*refs):
        at = 0
        for ref in refs[:-1]:
            refs[-1][:, at : at + ref.shape[1]] = ref[...]
            at += ref.shape[1]

    return call("pack_vectors", body, (1,), [], [whole(v) for v in vectors], [out_whole((1, width), F32)])[0]


def choose_vectors(ids, own, got, d, fh):
    def body(ids_ref, own_ref, got_ref, *outs):
        s = ids_ref[0]
        for layer in range(2):
            pick_one = lambda a, b: jnp.where(s == layer, own_ref[:, a:b], got_ref[:, a:b])
            for i in range(5):
                outs[6 * layer + i][...] = pick_one(i * d, (i + 1) * d)
            low, high = pick_one(5 * d, 5 * d + fh), pick_one(5 * d + fh, 5 * d + 2 * fh)
            outs[6 * layer + 5][...] = jnp.where(s == 0, low, high)

    outs = [out_whole((1, n), F32) for _ in range(2) for n in [d] * 5 + [fh]]
    got = call("choose_vectors", body, (1,), [ids], [whole(own), whole(got)], outs)
    return got[:6], got[6:]


def plain_sums(s, count, mlp2, cross, attn2, mlp1, image, attn1):
    scatter = lambda g: lax.psum_scatter(g, "dp", scatter_dimension=0, tiled=True)

    def full(act):
        come = swap(act)
        return jnp.concatenate([jnp.where(s == 0, act, come), jnp.where(s == 0, come, act)], 1)

    def side(grad):
        h2 = grad.shape[1] // 2
        return lax.dynamic_slice(grad, (0, s * h2), (grad.shape[0], h2))

    def stacked(w, h2):
        return jnp.concatenate([w[:, i : i + h2] for i in range(0, w.shape[1], h2)], 0)

    def by_section(w):
        parts = w.reshape(2, count, -1, w.shape[1]).swapaxes(0, 1)
        return scatter(parts.reshape(w.shape))

    def mlp(n, du, act, dm):
        return jnp.concatenate(
            [stacked(scatter(tn(n, du)), n.shape[1] // 2), scatter(tn(full(act), side(dm)))], 0
        )

    def attn(h, dqkv, att, da):
        return jnp.concatenate(
            [scatter(tn(h, dqkv[j])) for j in range(3)] + [scatter(tn(full(att), side(da)))], 0
        )

    h, dcq, att, dc = cross
    r_own, r_got, g_own, g_got = [x.reshape(-1, x.shape[-1]) for x in image]
    w_kv = tn(r_own, g_own) + tn(r_got, g_got)
    h2 = dcq.shape[1]
    c = jnp.concatenate([by_section(tn(h, dcq)), by_section(tn(full(att), side(dc)))], 0)
    kv = jnp.concatenate([by_section(w_kv[:, :h2]), by_section(w_kv[:, h2:])], 0)
    return mlp(*mlp2), c, attn(*attn2), mlp(*mlp1), kv, attn(*attn1)


def swap(value):
    return lax.ppermute(value, "section", [(0, 1), (1, 0)])


def on_device(
    text, image, image_counts, cotangent,
    attn_norm_gain, attn_norm_bias, qkv_weight, attn_out_weight, mlp_norm_gain, mlp_norm_bias,
    up_weight, up_bias, down_weight, down_bias,
    cross_norm_gain, cross_norm_bias, cross_query, cross_key_value, cross_out,
):
    s = lax.axis_index("section")
    me = lax.axis_index("dp")
    count = lax.axis_size("dp")
    ids = jnp.stack([s, me]).astype(jnp.int32)
    t, d = text.shape
    h2 = d // 2
    caps, half = image.shape[:2]
    ff = up_bias.shape[1]
    fh = ff // 2
    other = 1 - s

    fast = d // count == 48
    w_qkv, w_out, w_up, w_down = qkv_weight[0], attn_out_weight[0], up_weight[0], down_weight[0]
    vec_own = pack_vectors(
        [attn_norm_gain, attn_norm_bias, mlp_norm_gain, mlp_norm_bias, down_bias, up_bias]
    )
    vec_got = swap(vec_own)
    got_qkv, got_out, got_up, got_down = swap(w_qkv), swap(w_out), swap(w_up), swap(w_down)
    vectors = choose_vectors(ids, vec_own, vec_got, d, fh)
    halves = []
    for layer in range(2):
        halves.append(
            (
                Half(layer, w_qkv, got_qkv, h2),
                Half(layer, w_out, got_out, h2),
                Half(layer, w_up, got_up, h2),
                Half(layer, w_down, got_down, h2),
            )
        )
    gain_i, gain_t = cross_norm_gain[0:1], cross_norm_gain[1:2]
    bias_i, bias_t = cross_norm_bias[0:1], cross_norm_bias[1:2]

    r_own, kv_own, kv_send = key_value(ids, image, gain_i, bias_i, cross_key_value)
    kv_got = swap(kv_send)
    r_got = swap(r_own)

    ag1, ab1, mg1, mb1, bd1, bu1 = vectors[0]
    qw1, ow1, uw1, dw1 = halves[0]
    ag2, ab2, mg2, mb2, bd2, bu2 = vectors[1]
    qw2, ow2, uw2, dw2 = halves[1]

    h1, qkv1, att1, part, send = self_fwd(0, ids, [text], ag1, ab1, qw1, ow1)
    x1, n1, part, send = mlp_fwd(0, ids, text, part, swap(send), mg1, mb1, uw1, bu1, dw1, bd1)
    h2n, qkv2, att2, part, send, z = self_fwd(1, ids, [x1, part, swap(send)], ag2, ab2, qw2, ow2)
    z2, ch, cq, catt, part, send = cross_fwd(
        ids, image_counts, z, part, swap(send), gain_t, bias_t, cross_query, cross_out, kv_own, kv_got
    )
    (act2, du2, dpart, dsend, sums_m2, bup2, z3, n2, mpart, msend) = mlp_grad(
        1, ids, [z2, part, swap(send), cotangent], mg2, mb2, uw2, bu2, dw2, bd2
    )
    y = z3 + mpart + swap(msend).astype(F32)
    layer_out = jnp.where(s == 0, z, y.astype(BF))

    turned = [route(s, me, count, turn) for turn in range(3)] if fast else None
    live = []

    def begin(parts, turn):
        live.append(Sum(parts, count, turn))
        return live[-1]

    def step(*after):
        for x in live:
            x.land(*after)

    def after_live(value, *more):
        return tie(value, *[x.outgoing for x in live], *more) if fast else value

    if fast:
        m2 = begin(up_down_weights(1, turned[0], n2, du2, act2, swap(act2), cotangent, count), 0)
    (dz3, dc, dcq, dkv_own, dkv_send, cpart, csend, sums_n2) = cross_grad(
        ids, image_counts, cotangent, dpart, after_live(swap(dsend)), z3, mg2, cq, cross_query, cross_out,
        kv_own, kv_got,
    )
    dkv_mine = swap(dkv_send)
    if fast:
        parts = cross_weights(
            turned[2], ch, dcq, catt, swap(catt), dc, r_own, r_got, dkv_own, dkv_send, count
        )
        step(parts[-1])
        ckv = begin(parts, 2)
    dz2, da2, dqkv2, hpart, hsend, sums_c = self_grad(
        1, ids, dz3, cpart, after_live(swap(csend)), z2, gain_t, qkv2, qw2, ow2
    )
    if fast:
        step(sums_c)
        parts = self_weights(1, turned[1], h2n, dqkv2, att2, swap(att2), da2, count)
        a2 = begin(parts, 1)
    act1, du1, npart, nsend, sums_a2, bup1, dz = mlp_grad(
        0, ids, [dz2, hpart, after_live(swap(hsend)), z, ag2, n1], mg1, mb1, uw1, bu1, dw1, bd1
    )
    if fast:
        step(sums_a2)
        parts = up_down_weights(0, turned[0], n1, du1, act1, after_live(swap(act1)), dz, count)
        m1 = begin(parts, 0)
    dx1, da1, dqkv1, hpart, hsend, sums_n1 = self_grad(
        0, ids, dz, npart, after_live(swap(nsend)), x1, mg1, qkv1, qw1, ow1
    )
    if fast:
        step(sums_n1)
        parts = self_weights(0, turned[2], h1, dqkv1, att1, after_live(swap(att1)), da1, count)
        a1 = begin(parts, 2)
    input_grad, sums_a1 = text_grad(ids, dx1, hpart, after_live(swap(hsend)), text, ag1, dz)
    image_grad, sums_i = key_value_grad(
        ids, image, gain_i, dkv_own, after_live(dkv_mine, sums_a1), cross_key_value
    )
    if fast:
        step(sums_i)
        finish(live)
        m2, ckv, a2, m1, a1 = [x.result for x in live]
        c2, kv = ckv[: 2 * d // count], ckv[2 * d // count :]
    else:
        m2, c2, a2, m1, kv, a1 = plain_sums(
            s, count, (n2, du2, act2, cotangent), (ch, dcq, catt, dc), (h2n, dqkv2, att2, da2),
            (n1, du1, act1, dz), (r_own, r_got, dkv_own, dkv_send), (h1, dqkv1, att1, da1),
        )

    each = d // count
    small = each // 2
    first = jnp.concatenate([m1, a1], 0)
    second = jnp.concatenate([m2, a2], 0)
    mine = jnp.where(s == 0, first, second)
    theirs = swap(jnp.where(s == 0, second, first))
    left = jnp.where(s == 0, mine, theirs)
    right = jnp.where(s == 0, theirs, mine)
    units = fh // h2
    both = lambda a, b: jnp.concatenate([left[a:b], right[a:b]], 1)

    def columns(start, number):
        return [x[start + i * each : start + (i + 1) * each] for x in (left, right) for i in range(number)]

    g_up = jnp.concatenate(columns(0, units), 1)
    at = units * each
    wide = ff // count
    g_down = both(at, at + wide)
    at += wide
    g_qkv = jnp.concatenate(
        [x[at + i * each : at + (i + 1) * each] for i in range(3) for x in (left, right)], 1
    )
    g_out = both(at + 3 * each, at + 4 * each)

    cross = jnp.concatenate([c2, kv], 0).reshape(4, 2, small, h2)
    keep = lax.dynamic_index_in_dim(cross, s, 1, False)
    come = swap(lax.dynamic_index_in_dim(cross, other, 1, False))
    cross = jnp.concatenate(
        [jnp.where(s == 0, keep, come), jnp.where(s == 0, come, keep)], 2
    )
    g_cq, g_co = cross[0], cross[1]
    g_kv = jnp.concatenate([cross[2], cross[3]], 1)

    bup = [jnp.sum(b, 0) for b in (bup1, bup2)]
    bup_mine = jnp.where(s == 0, bup[0], bup[1])
    bup_come = swap(jnp.where(s == 0, bup[1], bup[0]))
    bup = jnp.concatenate(
        [jnp.where(s == 0, bup_mine, bup_come), jnp.where(s == 0, bup_come, bup_mine)]
    )
    sums_i = sums_i + swap(sums_i)
    pair = lambda a, b: jnp.sum(jnp.where(s == 0, a, b), 0).reshape(count, -1)
    split = lambda v: jnp.sum(v, 0).reshape(2, count, -1).swapaxes(0, 1).reshape(count, -1)
    packed = [
        pair(sums_a1[0], sums_a2[0]), pair(sums_a1[1], sums_a2[1]),
        pair(sums_n1[0], sums_n2[0]), pair(sums_n1[1], sums_n2[1]),
        pair(sums_a2[2], sums_m2[2]), bup.reshape(count, -1),
        split(sums_i[0]), split(sums_c[0]), split(sums_i[1]), split(sums_c[1]),
    ]
    widths = [v.shape[1] for v in packed]
    packed = jnp.concatenate(packed, 1)
    if fast:
        packed = packed[:, None]
        order = paths(count, 0)[0]
        table = [sum(((r >> (len(order) - 1 - k)) & 1) << b for k, b in enumerate(order)) for r in range(count)]
        packed = jnp.take(packed, jnp.array(table, jnp.int32) ^ me, axis=0)
        split_at = [(count >> (k + 1), count >> k) for k in range(len(order))] + [(0, 1)]
        total = Sum([packed[a:b] for a, b in split_at], count, 0, own_order=False)
        finish([total])
        vec = total.result[0]
    else:
        vec = lax.psum_scatter(packed, "dp", scatter_dimension=0, tiled=True)[0]
    cut, at = [], 0
    for w in widths:
        cut.append(vec[at : at + w])
        at += w
    own = lambda v: lax.dynamic_slice(v, (s * small,), (small,))
    return (
        layer_out[None], input_grad[None], image_grad,
        cut[0][None], cut[1][None], g_qkv[None], g_out[None], cut[2][None], cut[3][None],
        g_up[None], cut[5][None], g_down[None], cut[4][None],
        jnp.stack([own(cut[6]), own(cut[7])]), jnp.stack([own(cut[8]), own(cut[9])]),
        g_cq, g_kv, g_co,
    )


def solution(mesh):
    placed = (
        P("dp", None), P("dp", "section", None), P("dp"), P("dp", None),
        P("section", None), P("section", None), P("section", None, None), P("section", None, None),
        P("section", None), P("section", None), P("section", None, None), P("section", None),
        P("section", None, None), P("section", None), P(), P(), P(), P(), P(),
    )
    two, three = P("section", "dp"), P("section", "dp", None)
    last = P(("section", "dp"), None)
    return jax.shard_map(
        on_device,
        mesh=mesh,
        in_specs=placed,
        out_specs=(
            three, three, P("dp", "section", None), two, two, three, three, two, two, three, two,
            three, two, P(None, ("section", "dp")), P(None, ("section", "dp")), last, last, last,
        ),
        check_vma=False,
    )
```

```python
import jax
import jax.numpy as jnp
from jax import lax
from jax.experimental import pallas as pl
from jax.experimental.pallas import tpu as pltpu
from jax.sharding import PartitionSpec as P

HEAD_DIM = 64
SEQ = 64
LANES = 128
CHUNK = 32
ANY = pl.ANY
MT = 256
EPS = 1e-05
NEG = -1e30
SCALE = HEAD_DIM**-0.5
BF = jnp.bfloat16
F32 = jnp.float32


def nn(a, b):
    return lax.dot_general(a, b, (((1,), (0,)), ((), ())), preferred_element_type=F32)


def nt(a, b):
    return lax.dot_general(a, b, (((1,), (1,)), ((), ())), preferred_element_type=F32)


def tn(a, b):
    return lax.dot_general(a, b, (((0,), (0,)), ((), ())), preferred_element_type=F32)


def normalized(v):
    c = v - jnp.mean(v, -1, keepdims=True)
    inv = lax.rsqrt(jnp.mean(c * c, -1, keepdims=True) + EPS)
    return c * inv, inv


def norm(v, g, b):
    return normalized(v)[0] * g + b


def norm_grad(v, g, dh):
    nh, inv = normalized(v)
    e = dh * g
    dv = (e - jnp.mean(e, -1, keepdims=True) - nh * jnp.mean(e * nh, -1, keepdims=True)) * inv
    return dv, dh * nh


def fold(v):
    return jnp.sum(v.reshape(v.shape[0] // 8, 8, v.shape[1]), 0)


def gelu_pair(u):
    k = 0.7978845608028654
    t = jnp.tanh(k * (u + 0.044715 * u * u * u))
    g = 0.5 * u * (1.0 + t)
    dg = 0.5 * (1.0 + t) + 0.5 * u * (1.0 - t * t) * (k * (1.0 + 3 * 0.044715 * u * u))
    return g, dg


def gelu(u):
    k = 0.7978845608028654
    return 0.5 * u * (1.0 + jnp.tanh(k * (u + 0.044715 * u * u * u)))


def two_heads(v):
    low = lax.broadcasted_iota(jnp.int32, v.shape, 1) < HEAD_DIM
    zero = jnp.zeros_like(v)
    return jnp.concatenate([jnp.where(low, v, zero), jnp.where(low, zero, v)], 0)


def join_heads(v):
    half = v.shape[0] // 2
    low = lax.broadcasted_iota(jnp.int32, (half, LANES), 1) < HEAD_DIM
    return jnp.where(low, v[:half], v[half:])


def key_softmax(scores):
    top = jnp.max(scores[0], 0, keepdims=True)
    for s in scores[1:]:
        top = jnp.maximum(top, jnp.max(s, 0, keepdims=True))
    e = [jnp.exp((s - top) * SCALE) for s in scores]
    scale = 1.0 / sum(jnp.sum(x, 0, keepdims=True) for x in e)
    return [x * scale for x in e]


def causal(s):
    key = lax.broadcasted_iota(jnp.int32, s.shape, 0)
    query = lax.broadcasted_iota(jnp.int32, s.shape, 1) % SEQ
    return jnp.where(key <= query, s, NEG)


def below(s, limit):
    return jnp.where(lax.broadcasted_iota(jnp.int32, s.shape, 0) < limit, s, NEG)


def attend(probs, values):
    return join_heads(sum(tn(p.astype(BF), v) for p, v in zip(probs, values)))


def attend_grad(q2, keys, values, probs, go):
    go2 = two_heads(go)
    dp = [nt(v, go2) for v in values]
    mean = sum(jnp.sum(p * d, 0, keepdims=True) for p, d in zip(probs, dp))
    ds = [(p * (d - mean)).astype(BF) for p, d in zip(probs, dp)]
    dq = join_heads(sum(tn(x, k) for x, k in zip(ds, keys))) * SCALE
    dk = [nn(x, q2) * SCALE for x in ds]
    dv = [nn(p.astype(BF), go2) for p in probs]
    return dq, dk, dv


def loop(count, body, unroll=1):
    def step(i, carry):
        for u in range(unroll):
            body(i * unroll + u)
        return carry

    if count == unroll:
        step(0, 0)
    else:
        lax.fori_loop(0, count // unroll, step, 0)


def rows(i, size):
    start = i * size
    return pl.ds(start if isinstance(start, int) else pl.multiple_of(start, size), size)


def lane(start, size):
    return pl.ds(start if isinstance(start, int) else pl.multiple_of(start, LANES), size)


def call(name, body, grid, scalars, ins, outs, scratch=(), flops=0):
    def spec(shape, item):
        block, index = item
        if block is ANY:
            return pl.BlockSpec(memory_space=ANY)
        if block is None:
            block = shape
        if index is None:
            index = lambda *_, n=len(shape): (0,) * n
        return pl.BlockSpec(block, index)

    shapes = [jax.ShapeDtypeStruct(o[0], o[1]) for o in outs]
    moved = sum(a[0].size * a[0].dtype.itemsize for a in ins)
    moved += sum(s.size * s.dtype.itemsize for s in shapes)
    return pl.pallas_call(
        body,
        name=name,
        out_shape=shapes,
        grid_spec=pltpu.PrefetchScalarGridSpec(
            num_scalar_prefetch=len(scalars),
            grid=grid,
            in_specs=[spec(a[0].shape, a[1:]) for a in ins],
            out_specs=[spec(o[0], o[2:]) for o in outs],
            scratch_shapes=list(scratch),
        ),
        compiler_params=pltpu.CompilerParams(vmem_limit_bytes=56 << 20),
        cost_estimate=pl.CostEstimate(flops=int(flops), bytes_accessed=int(moved), transcendentals=0),
    )(*scalars, *[a[0] for a in ins])


def whole(a):
    return (a, None, None)


def out_whole(shape, dtype):
    return (shape, dtype, None, None)


class Half:
    def __init__(self, layer, own, got, width):
        self.layer, self.own, self.got, self.width = layer, own, got, width

    def cols(self, per):
        layer, width = self.layer, self.width
        d = self.own.shape[0]

        def own_map(j, ids, *_):
            return (0, jnp.where(ids[0] == layer, per(j, ids[0]), 0))

        def got_map(j, ids, *_):
            return (0, jnp.where(ids[0] == layer, 0, per(j, ids[0])))

        return [(self.own, (d, width), own_map), (self.got, (d, width), got_map)]

    def rowblocks(self, per):
        layer, width = self.layer, self.width
        d = self.own.shape[1]

        def own_map(j, ids, *_):
            return (jnp.where(ids[0] == layer, per(j, ids[0]), 0), 0)

        def got_map(j, ids, *_):
            return (jnp.where(ids[0] == layer, 0, per(j, ids[0])), 0)

        return [(self.own, (width, d), own_map), (self.got, (width, d), got_map)]


def pick(ids, layer, own_ref, got_ref):
    return jnp.where(ids[0] == layer, own_ref[...], got_ref[...])


def self_fwd(layer, ids, stream, gain, bias, wqkv, wout):
    first = len(stream) == 1
    t, d = stream[0].shape
    h2 = d // 2
    n_in = len(stream)

    def body(ids_ref, *refs):
        xs, refs = refs[:n_in], refs[n_in:]
        g_ref, b_ref, own, got, o_own, o_got = refs[:6]
        outs = refs[6:]
        h_ref, qkv_ref, att_ref, part_ref, send_ref = outs[:5]
        j = pl.program_id(0)

        @pl.when(j == 0)
        def _():
            def chunk(i):
                sl = rows(i, CHUNK)
                if first:
                    x = xs[0][sl, :].astype(F32)
                else:
                    z = (xs[0][sl, :] + xs[1][sl, :] + xs[2][sl, :].astype(F32)).astype(BF)
                    outs[5][sl, :] = z
                    x = z.astype(F32)
                h_ref[sl, :] = norm(x, g_ref[...], b_ref[...]).astype(BF)

            loop(t // CHUNK, chunk, 4)

        w = pick(ids_ref, layer, own, got)

        qkv_ref[j] = nn(h_ref[...], w).astype(BF)

        @pl.when(j == 2)
        def _():
            def block(i):
                units = [
                    (rows(2 * i + c, SEQ), slice(p * LANES, (p + 1) * LANES))
                    for c in range(2) for p in range(h2 // LANES)
                ]
                loaded = [[qkv_ref[m, sl, ln] for m in range(3)] for sl, ln in units]
                scores = [causal(nt(k, two_heads(q))) for q, k, v in loaded]
                probs = [key_softmax([s]) for s in scores]
                done = [attend(p, [x[2]]) for p, x in zip(probs, loaded)]
                for (sl, ln), o in zip(units, done):
                    att_ref[sl, ln] = o.astype(BF)

            loop(t // (2 * SEQ), block)
            wo = pick(ids_ref, layer, o_own, o_got)
            part = nn(att_ref[...], wo)
            part_ref[...] = part
            send_ref[...] = part.astype(BF)

    outs = [
        out_whole((t, d), BF),
        out_whole((3, t, h2), BF),
        out_whole((t, h2), BF),
        out_whole((t, d), F32),
        out_whole((t, d), BF),
    ]
    if not first:
        outs.append(out_whole((t, d), BF))
    ins = [whole(x) for x in stream] + [whole(gain), whole(bias)]
    ins += wqkv.cols(lambda j, s: 2 * j + s) + wout.rowblocks(lambda j, s: s)
    return call(
        f"self_fwd_{layer}", body, (3,), [ids], ins, outs, flops=2 * t * d * 4 * h2 + 2e8
    )


def mlp_fwd(layer, ids, x, a_own, a_got, gain, bias, wup, b_up, wdown, b_down):
    t, d = x.shape
    fh = b_up.shape[1]
    width = wup.width

    def body(ids_ref, x_ref, p_ref, q_ref, g_ref, b_ref, u_own, u_got, bu_ref, d_own, d_got, bd_ref,
             x1_ref, n_ref, part_ref, send_ref):
        j = pl.program_id(0)

        @pl.when(j == 0)
        def _():
            def chunk(i):
                sl = rows(i, CHUNK)
                x1 = x_ref[sl, :].astype(F32) + p_ref[sl, :] + q_ref[sl, :].astype(F32)
                x1_ref[sl, :] = x1
                n_ref[sl, :] = norm(x1, g_ref[...], b_ref[...]).astype(BF)
                part_ref[sl, :] = jnp.broadcast_to(
                    jnp.where(ids_ref[0] == 0, bd_ref[...], 0.0), (CHUNK, d)
                )

            loop(t // CHUNK, chunk, 4)

        up = pick(ids_ref, layer, u_own, u_got)
        down = pick(ids_ref, layer, d_own, d_got)

        def tile(i):
            sl = rows(i, MT)
            u = nn(n_ref[sl, :], up) + bu_ref[...]
            part_ref[sl, :] += nn(gelu(u).astype(BF), down)

        loop(t // MT, tile, t // MT)

        @pl.when(j == pl.num_programs(0) - 1)
        def _():
            def chunk(i):
                sl = rows(i, CHUNK)
                send_ref[sl, :] = part_ref[sl, :].astype(BF)

            loop(t // CHUNK, chunk, 4)

    per = fh // width
    ins = [whole(x), whole(a_own), whole(a_got), whole(gain), whole(bias)]
    ins += wup.cols(lambda j, s: s * per + j)
    ins += [(b_up, (1, width), lambda j, *_: (0, j))]
    ins += wdown.rowblocks(lambda j, s: s * per + j)
    ins += [whole(b_down)]
    outs = [
        out_whole((t, d), F32),
        out_whole((t, d), BF),
        out_whole((t, d), F32),
        out_whole((t, d), BF),
    ]
    return call(f"mlp_fwd_{layer}", body, (per,), [ids], ins, outs, flops=4 * t * d * fh)


def mlp_grad(layer, ids, lead, gain, bias, wup, b_up, wdown, b_down):
    second = layer == 1
    t, d = lead[0].shape
    fh = b_up.shape[1]
    width = wup.width
    n_in = len(lead)

    def body(ids_ref, *refs):
        lead_refs, refs = refs[:n_in], refs[n_in:]
        g_ref, b_ref, u_own, u_got, bu_ref, d_own, d_got, bd_ref = refs[:8]
        outs = refs[8:]
        act_ref, du_ref, dn_ref, dsend_ref, sums_ref, bup_ref = outs[:6]
        extra = outs[6:]
        j = pl.program_id(0)

        @pl.when(j == 0)
        def _():
            sums_ref[...] = jnp.zeros_like(sums_ref)

            def chunk(i):
                sl = rows(i, CHUNK)
                if second:
                    x_ref, p_ref, q_ref, cot_ref = lead_refs
                    x = x_ref[sl, :] + p_ref[sl, :] + q_ref[sl, :].astype(F32)
                    extra[0][sl, :] = x
                    extra[1][sl, :] = norm(x, g_ref[...], b_ref[...]).astype(BF)
                    extra[2][sl, :] = jnp.broadcast_to(
                        jnp.where(ids_ref[0] == 0, bd_ref[...], 0.0), (CHUNK, d)
                    )
                    sums_ref[2] += fold(cot_ref[sl, :].astype(F32))
                else:
                    grad_ref, p_ref, q_ref, z_ref, zg_ref, n_ref = lead_refs
                    dh = p_ref[sl, :] + q_ref[sl, :].astype(F32)
                    dv, dhn = norm_grad(z_ref[sl, :].astype(F32), zg_ref[...], dh)
                    dz = (grad_ref[sl, :] + dv).astype(BF)
                    extra[0][sl, :] = dz
                    sums_ref[0] += fold(dhn)
                    sums_ref[1] += fold(dh)
                    sums_ref[2] += fold(dz.astype(F32))
                dn_ref[sl, :] = jnp.zeros((CHUNK, d), F32)

            loop(t // CHUNK, chunk, 4)

        up = pick(ids_ref, layer, u_own, u_got)
        down = pick(ids_ref, layer, d_own, d_got)
        bup_ref[...] = jnp.zeros_like(bup_ref)
        n_src = extra[1] if second else lead_refs[5]
        dm_src = lead_refs[3] if second else extra[0]

        def tile(i):
            sl = rows(i, MT)
            u = nn(n_src[sl, :], up) + bu_ref[...]
            g, dg = gelu_pair(u)
            g = g.astype(BF)
            act_ref[sl, :] = g
            du = (nt(dm_src[sl, :], down) * dg).astype(BF)
            du_ref[sl, :] = du
            bup_ref[...] += fold(du.astype(F32))
            dn_ref[sl, :] += nt(du, up)
            if second:
                extra[2][sl, :] += nn(g, down)

        loop(t // MT, tile, t // MT)

        @pl.when(j == pl.num_programs(0) - 1)
        def _():
            def chunk(i):
                sl = rows(i, CHUNK)
                dsend_ref[sl, :] = dn_ref[sl, :].astype(BF)
                if second:
                    extra[3][sl, :] = extra[2][sl, :].astype(BF)

            loop(t // CHUNK, chunk, 4)

    per = fh // width
    ins = [whole(a) for a in lead] + [whole(gain), whole(bias)]
    ins += wup.cols(lambda j, s: s * per + j)
    ins += [(b_up, (1, width), lambda j, *_: (0, j))]
    ins += wdown.rowblocks(lambda j, s: s * per + j)
    ins += [whole(b_down)]
    outs = [
        ((t, fh), BF, (t, width), lambda j, *_: (0, j)),
        ((t, fh), BF, (t, width), lambda j, *_: (0, j)),
        out_whole((t, d), F32),
        out_whole((t, d), BF),
        out_whole((3, 8, d), F32),
        ((8, fh), F32, (8, width), lambda j, *_: (0, j)),
    ]
    if second:
        outs += [
            out_whole((t, d), F32),
            out_whole((t, d), BF),
            out_whole((t, d), F32),
            out_whole((t, d), BF),
        ]
    else:
        outs += [out_whole((t, d), BF)]
    return call(
        f"mlp_grad_{layer}", body, (per,), [ids], ins, outs,
        flops=(8 if second else 6) * t * d * fh,
    )


def key_value(ids, image, gain, bias, w):
    caps, half, d = image.shape
    h2 = d // 2
    per = 2

    def body(ids_ref, im_ref, g_ref, b_ref, w_ref, r_ref, own_ref, oth_ref):
        for c in range(per):

            def chunk(i, c=c):
                sl = rows(i, 32)
                r_ref[c, sl, :] = norm(im_ref[c, sl, :].astype(F32), g_ref[...], b_ref[...]).astype(BF)

            loop(half // 32, chunk, 3)
        r = r_ref[...].reshape(per * half, d)
        first = ids_ref[0] == 0
        for i in range(2):
            x = nn(r, w_ref[:, i * d : (i + 1) * d]).astype(BF).reshape(per, half, d)
            low, high = x[:, :, :h2], x[:, :, h2:]
            own_ref[:, :, i * h2 : (i + 1) * h2] = jnp.where(first, low, high)
            oth_ref[:, :, i * h2 : (i + 1) * h2] = jnp.where(first, high, low)

    blk = ((per, half, d), lambda c, *_: (c, 0, 0))
    ins = [(image,) + blk, whole(gain), whole(bias), whole(w)]
    outs = [((caps, half, d), BF) + blk] * 3
    return call("key_value", body, (caps // per,), [ids], ins, outs, flops=4 * caps * half * d * d)


def key_value_grad(ids, image, gain, g_own, g_oth, w):
    caps, half, d = image.shape
    h2 = d // 2
    per = 2

    def body(ids_ref, im_ref, g_ref, own_ref, oth_ref, w_ref, dx_ref, sums_ref, dr_ref):
        @pl.when(pl.program_id(0) == 0)
        def _():
            sums_ref[...] = jnp.zeros_like(sums_ref)

        own = own_ref[...].reshape(per * half, d)
        oth = oth_ref[...].reshape(per * half, d)
        first = ids_ref[0] == 0
        low, high = jnp.where(first, own, oth), jnp.where(first, oth, own)
        g = [x[:, i * h2 : (i + 1) * h2] for i in range(2) for x in (low, high)]
        dr_ref[...] = nt(jnp.concatenate(g, 1), w_ref[...]).reshape(per, half, d)
        for c in range(per):

            def chunk(i, c=c):
                sl = rows(i, 32)
                dr = dr_ref[c, sl, :]
                dv, dhn = norm_grad(im_ref[c, sl, :].astype(F32), g_ref[...], dr)
                dx_ref[c, sl, :] = dv
                sums_ref[0] += fold(dhn)
                sums_ref[1] += fold(dr)

            loop(half // 32, chunk, 3)

    blk = ((per, half, d), lambda c, *_: (c, 0, 0))
    ins = [(image,) + blk, whole(gain), (g_own,) + blk, (g_oth,) + blk, whole(w)]
    outs = [((caps, half, d), F32) + blk, out_whole((2, 8, d), F32)]
    return call(
        "key_value_grad", body, (caps // per,), [ids], ins, outs,
        scratch=[pltpu.VMEM((per, half, d), F32)], flops=4 * caps * half * d * d,
    )


def patch_limits(ids_ref, counts_ref, c, half):
    s = ids_ref[0]
    return counts_ref[c] - s * half, counts_ref[c] - (1 - s) * half


def cross_fwd(ids, counts, z, a_own, a_got, gain, bias, wq, wco, kv_own, kv_got):
    caps, half, d = kv_own.shape
    h2 = d // 2
    t = z.shape[0]

    def body(ids_ref, cnt_ref, z_ref, p_ref, q_ref, g_ref, b_ref, wq_ref, wo_ref, own_ref, got_ref,
             z2_ref, h_ref, cq_ref, att_ref, part_ref, send_ref):
        c = pl.program_id(0)

        @pl.when(c == 0)
        def _():
            def chunk(i):
                sl = rows(i, CHUNK)
                x = z_ref[sl, :].astype(F32) + p_ref[sl, :] + q_ref[sl, :].astype(F32)
                z2_ref[sl, :] = x
                h_ref[sl, :] = norm(x, g_ref[...], b_ref[...]).astype(BF)

            loop(t // CHUNK, chunk, 4)

            cq_ref[...] = nn(h_ref[...], wq_ref[...]).astype(BF)

        limits = patch_limits(ids_ref, cnt_ref, c, half)
        sl = rows(c, SEQ)
        for p in range(h2 // LANES):
            ln = slice(p * LANES, (p + 1) * LANES)
            lv = slice(h2 + p * LANES, h2 + (p + 1) * LANES)
            q2 = two_heads(cq_ref[sl, ln])
            sides = (own_ref, got_ref)
            scores = [below(nt(ref[0, :, ln], q2), limit) for ref, limit in zip(sides, limits)]
            att_ref[sl, ln] = attend(key_softmax(scores), [ref[0, :, lv] for ref in sides]).astype(BF)

        @pl.when(c == pl.num_programs(0) - 1)
        def _():
            part = nn(att_ref[...], wo_ref[...])
            part_ref[...] = part
            send_ref[...] = part.astype(BF)

    blk = ((1, half, d), lambda c, *_: (c, 0, 0))
    ins = [whole(z), whole(a_own), whole(a_got), whole(gain), whole(bias)]
    ins += [(wq, (d, h2), lambda c, ids, *_: (0, ids[0])), (wco, (h2, d), lambda c, ids, *_: (ids[0], 0))]
    ins += [(kv_own,) + blk, (kv_got,) + blk]
    outs = [
        out_whole((t, d), F32),
        out_whole((t, d), BF),
        out_whole((t, h2), BF),
        out_whole((t, h2), BF),
        out_whole((t, d), F32),
        out_whole((t, d), BF),
    ]
    return call(
        "cross_fwd", body, (caps,), [ids, counts], ins, outs, flops=4 * t * d * h2 + 16e8
    )


def cross_grad(ids, counts, grad, n_own, n_got, x3, gain3, cq, wq, wco, kv_own, kv_got):
    caps, half, d = kv_own.shape
    h2 = d // 2
    t = x3.shape[0]

    def body(ids_ref, cnt_ref, gr_ref, p_ref, q_ref, x_ref, g_ref, cq_ref, wq_ref, wo_ref, own_ref, got_ref,
             dz_ref, dc_ref, dcq_ref, down_ref, dgot_ref, dh_ref, dsend_ref, sums_ref, da_ref):
        c = pl.program_id(0)

        @pl.when(c == 0)
        def _():
            sums_ref[...] = jnp.zeros_like(sums_ref)

            def chunk(i):
                sl = rows(i, CHUNK)
                dh = p_ref[sl, :] + q_ref[sl, :].astype(F32)
                dv, dhn = norm_grad(x_ref[sl, :], g_ref[...], dh)
                dz = gr_ref[sl, :].astype(F32) + dv
                dz_ref[sl, :] = dz
                dc_ref[sl, :] = dz.astype(BF)
                sums_ref[0] += fold(dhn)
                sums_ref[1] += fold(dh)

            loop(t // CHUNK, chunk, 4)

            da_ref[...] = nt(dc_ref[...], wo_ref[...]).astype(BF)

        limits = patch_limits(ids_ref, cnt_ref, c, half)
        sl = rows(c, SEQ)
        for p in range(h2 // LANES):
            ln = slice(p * LANES, (p + 1) * LANES)
            lv = slice(h2 + p * LANES, h2 + (p + 1) * LANES)
            sides = (own_ref, got_ref)
            keys, values = [ref[0, :, ln] for ref in sides], [ref[0, :, lv] for ref in sides]
            q2 = two_heads(cq_ref[sl, ln])
            probs = key_softmax([below(nt(k, q2), limit) for k, limit in zip(keys, limits)])
            dq, dk, dv = attend_grad(q2, keys, values, probs, da_ref[sl, ln])
            dcq_ref[sl, ln] = dq.astype(BF)
            for out, a, b in zip((down_ref, dgot_ref), dk, dv):
                out[0, :, ln] = a.astype(BF)
                out[0, :, lv] = b.astype(BF)

        @pl.when(c == pl.num_programs(0) - 1)
        def _():
            part = nt(dcq_ref[...], wq_ref[...])
            dh_ref[...] = part
            dsend_ref[...] = part.astype(BF)

    blk = ((1, half, d), lambda c, *_: (c, 0, 0))
    ins = [whole(grad), whole(n_own), whole(n_got), whole(x3), whole(gain3), whole(cq)]
    ins += [(wq, (d, h2), lambda c, ids, *_: (0, ids[0])), (wco, (h2, d), lambda c, ids, *_: (ids[0], 0))]
    ins += [(kv_own,) + blk, (kv_got,) + blk]
    outs = [
        out_whole((t, d), F32),
        out_whole((t, d), BF),
        out_whole((t, h2), BF),
        ((caps, half, d), BF) + blk,
        ((caps, half, d), BF) + blk,
        out_whole((t, d), F32),
        out_whole((t, d), BF),
        out_whole((2, 8, d), F32),
    ]
    return call(
        "cross_grad", body, (caps,), [ids, counts], ins, outs,
        scratch=[pltpu.VMEM((t, h2), BF)], flops=4 * t * d * h2 + 5e9,
    )


def self_grad(layer, ids, grad, h_own, h_got, x, gain_x, qkv, wqkv, wout):
    t, d = x.shape
    h2 = d // 2

    def body(ids_ref, gr_ref, p_ref, q_ref, x_ref, g_ref, qkv_ref, own, got, o_own, o_got,
             dz_ref, da_ref, dqkv_ref, dh_ref, dsend_ref, sums_ref, datt_ref):
        j = pl.program_id(0)

        @pl.when(j == 0)
        def _():
            sums_ref[...] = jnp.zeros_like(sums_ref)

            def chunk(i):
                sl = rows(i, CHUNK)
                dh = p_ref[sl, :] + q_ref[sl, :].astype(F32)
                dv, dhn = norm_grad(x_ref[sl, :].astype(F32), g_ref[...], dh)
                dz = gr_ref[sl, :].astype(F32) + dv
                dz_ref[sl, :] = dz
                da_ref[sl, :] = dz.astype(BF)
                sums_ref[0] += fold(dhn)
                sums_ref[1] += fold(dh)

            loop(t // CHUNK, chunk, 4)
            wo = pick(ids_ref, layer, o_own, o_got)

            datt_ref[...] = nt(da_ref[...], wo).astype(BF)

            def block(i):
                units = [
                    (rows(2 * i + c, SEQ), slice(p * LANES, (p + 1) * LANES))
                    for c in range(2) for p in range(h2 // LANES)
                ]
                loaded = [[qkv_ref[m, sl, ln] for m in range(3)] + [datt_ref[sl, ln]] for sl, ln in units]
                done = []
                for q, k, v, go in loaded:
                    q2 = two_heads(q)
                    probs = key_softmax([causal(nt(k, q2))])
                    dq, dk, dv = attend_grad(q2, [k], [v], probs, go)
                    done.append((dq, dk[0], dv[0]))
                for (sl, ln), grads in zip(units, done):
                    for m in range(3):
                        dqkv_ref[m, sl, ln] = grads[m].astype(BF)

            loop(t // (2 * SEQ), block)

        w = pick(ids_ref, layer, own, got)
        part = nt(dqkv_ref[j], w)

        @pl.when(j == 0)
        def _():
            dh_ref[...] = part

        @pl.when(j > 0)
        def _():
            total = dh_ref[...] + part
            dh_ref[...] = total
            dsend_ref[...] = total.astype(BF)

    ins = [whole(grad), whole(h_own), whole(h_got), whole(x), whole(gain_x), whole(qkv)]
    ins += wqkv.cols(lambda j, s: 2 * j + s) + wout.rowblocks(lambda j, s: s)
    outs = [
        out_whole((t, d), F32),
        out_whole((t, d), BF),
        out_whole((3, t, h2), BF),
        out_whole((t, d), F32),
        out_whole((t, d), BF),
        out_whole((2, 8, d), F32),
    ]
    return call(
        f"self_grad_{layer}", body, (3,), [ids], ins, outs,
        scratch=[pltpu.VMEM((t, h2), BF)], flops=2 * t * d * 4 * h2 + 5e8,
    )


def text_grad(ids, grad, h_own, h_got, x, gain, dz):
    t, d = x.shape

    def body(ids_ref, gr_ref, p_ref, q_ref, x_ref, g_ref, dz_ref, dx_ref, sums_ref):
        sums_ref[...] = jnp.zeros_like(sums_ref)

        def chunk(i):
            sl = rows(i, CHUNK)
            dh = p_ref[sl, :] + q_ref[sl, :].astype(F32)
            dv, dhn = norm_grad(x_ref[sl, :].astype(F32), g_ref[...], dh)
            dx_ref[sl, :] = jnp.where(ids_ref[0] == 0, gr_ref[sl, :] + dv, dz_ref[sl, :].astype(F32))
            sums_ref[0] += fold(dhn)
            sums_ref[1] += fold(dh)

        loop(t // CHUNK, chunk, 4)

    ins = [whole(a) for a in (grad, h_own, h_got, x, gain, dz)]
    outs = [out_whole((t, d), F32), out_whole((2, 8, d), F32)]
    return call("text_grad", body, (1,), [ids], ins, outs)


def paths(count, turn):
    bits = list(range(count.bit_length() - 1))
    near, far = bits[:3], bits[3:]
    return [near[k % 3 :] + near[: k % 3] + far for k in (turn, turn + 1)]


def route(s, me, count, turn):
    first, second = paths(count, turn)
    bits = [jnp.where(s == 0, a, b) for a, b in zip(first, second)]
    return jnp.stack([s, me] + bits).astype(jnp.int32)


def tie(value, *after):
    return lax.optimization_barrier((value, *after))[0]


class Sum:
    def __init__(self, parts, count, turn, own_order=True):
        self.parts, self.count, self.paths = parts, count, paths(count, turn)
        if not own_order:
            self.paths = [self.paths[0]] * 2
        self.arrived, self.result = [], None
        self.send(parts[0])

    def send(self, value):
        self.outgoing = value
        step, n = len(self.arrived), self.count
        perm = [(s * n + i, s * n + (i ^ (1 << self.paths[s][step]))) for s in range(2) for i in range(n)]
        self.flight = lax.ppermute(value, ("section", "dp"), perm)

    def land(self, *after):
        if self.result is not None:
            return
        self.arrived.append(tie(self.flight, *after) if after else self.flight)
        step = len(self.arrived)
        low = self.count >> (step + 1)
        high = max(2 * low, 1)
        total = self.parts[step].astype(F32)
        for a in self.arrived:
            total = total + a[low:high].astype(F32)
        if step < len(self.parts) - 1:
            self.send(total.astype(self.parts[0].dtype))
        else:
            self.result = self.outgoing = total[0]


def finish(sums):
    while any(x.result is None for x in sums):
        for x in sums:
            x.land()


def slots(outs, scr):
    high = scr.shape[0]
    for out in outs[:-1]:
        low = high // 2

        def one(i, out=out, low=low):
            out[i] = scr[low + i].astype(BF)

        loop(high - low, one)
        high = low
    outs[-1][0] = scr[0].astype(BF)


def putter(ids_ref, scr):
    def put(dest, first, block):
        rel, slot = dest ^ ids_ref[1], 0
        for k in range(scr.shape[0].bit_length() - 1):
            slot = slot * 2 + ((rel >> ids_ref[2 + k]) & 1)
        scr[slot, pl.ds(first, block.shape[0]), :] = block.astype(scr.dtype)

    return put


def slot_outs(count, row_count, cols):
    steps = count.bit_length() - 1
    sizes = [count >> k for k in range(1, steps + 1)] + [1]
    return [out_whole((n, row_count, cols), BF) for n in sizes]


def weight_kernel(name, ids, ins, row_count, count, fill, flops):
    cols = 3 * LANES

    def body(ids_ref, *refs):
        scr = refs[-1]
        fill(ids_ref, refs[: len(ins)], putter(ids_ref, scr))
        slots(refs[len(ins) : -1], scr)

    return call(
        name, body, (1,), [ids], [whole(a) for a in ins], slot_outs(count, row_count, cols),
        scratch=[pltpu.VMEM((count, row_count, cols), BF)], flops=flops,
    )


def up_down_weights(layer, ids, normed, du, act_own, act_got, dm, count):
    t, d = normed.shape
    fh = du.shape[1]
    h2 = d // 2
    up_rows, down_rows = d // count, 2 * fh // count
    units = fh // h2
    half_dest = count // 2

    def fill(ids_ref, refs, put):
        n_ref, du_ref, own_ref, got_ref, dm_ref = refs

        def up(j):
            w = tn(n_ref[...], du_ref[:, lane(j * h2, h2)])
            for dest in range(count):
                put(dest, pl.multiple_of(j * up_rows, up_rows), w[dest * up_rows : (dest + 1) * up_rows])

        loop(units, up)
        base = units * up_rows
        s = ids_ref[0]
        dm_half = dm_ref[:, lane(s * h2, h2)]
        per = h2 // down_rows

        def down(j):
            for ref, side in ((own_ref, s), (got_ref, 1 - s)):
                w = tn(ref[:, lane(j * h2, h2)], dm_half)
                for i in range(per):
                    put(side * half_dest + j * per + i, base, w[i * down_rows : (i + 1) * down_rows])

        loop(fh // h2, down)

    return weight_kernel(
        f"mlp_weights_{layer}", ids, [normed, du, act_own, act_got, dm],
        units * up_rows + down_rows, count, fill, 4 * t * d * fh,
    )


def self_weights(layer, ids, h, dqkv, att_own, att_got, da, count):
    t, d = h.shape
    h2 = d // 2
    each = d // count
    half_dest = count // 2

    def fill(ids_ref, refs, put):
        h_ref, dqkv_ref, own_ref, got_ref, da_ref = refs

        def one(j):
            w = tn(h_ref[...], dqkv_ref[j])
            for dest in range(count):
                put(dest, pl.multiple_of(j * each, each), w[dest * each : (dest + 1) * each])

        loop(3, one)
        s = ids_ref[0]
        da_half = da_ref[:, lane(s * h2, h2)]
        for ref, side in ((own_ref, s), (got_ref, 1 - s)):
            w = tn(ref[...], da_half)
            for i in range(half_dest):
                put(side * half_dest + i, 3 * each, w[i * each : (i + 1) * each])

    return weight_kernel(
        f"self_weights_{layer}", ids, [h, dqkv, att_own, att_got, da], 4 * each, count, fill,
        8 * t * d * h2,
    )


def cross_weights(ids, h, dcq, att_own, att_got, dc, r_own, r_got, g_own, g_got, count):
    t = h.shape[0]
    caps, half, d = r_own.shape
    h2 = d // 2
    each = h2 // count
    n_in = 9

    def body(ids_ref, *refs):
        h_ref, dcq_ref, own_ref, got_ref, dc_ref, ro, rg, go, gg = refs[:n_in]
        outs, scr, acc = refs[n_in:-2], refs[-2], refs[-1]
        c = pl.program_id(0)

        @pl.when(c == 0)
        def _():
            acc[...] = jnp.zeros_like(acc)

        def add(i):
            sl = rows(i, 256)
            acc[sl, :] += tn(ro[0, :, lane(i * 256, 256)], go[0]) + tn(rg[0, :, lane(i * 256, 256)], gg[0])

        loop(d // 256, add)

        @pl.when(c == pl.num_programs(0) - 1)
        def _():
            put = putter(ids_ref, scr)
            w = tn(h_ref[...], dcq_ref[...])
            for half_row in range(2):
                for dest in range(count):
                    at = half_row * h2 + dest * each
                    put(dest, half_row * each, w[at : at + each])
            s = ids_ref[0]
            dc_half = dc_ref[:, lane(s * h2, h2)]
            for ref, side in ((own_ref, s), (got_ref, 1 - s)):
                w = tn(ref[...], dc_half)
                for dest in range(count):
                    put(dest, pl.multiple_of((2 + side) * each, each), w[dest * each : (dest + 1) * each])
            for kind in range(2):
                for part in range(2):
                    for dest in range(count):
                        at = part * h2 + dest * each
                        put(
                            dest, (4 + 2 * kind + part) * each,
                            acc[at : at + each, kind * h2 : (kind + 1) * h2],
                        )
            slots(outs, scr)

    blk = ((1, half, d), lambda c, *_: (c, 0, 0))
    ins = [whole(a) for a in (h, dcq, att_own, att_got, dc)]
    ins += [(a,) + blk for a in (r_own, r_got, g_own, g_got)]
    return call(
        "cross_weights", body, (caps,), [ids], ins, slot_outs(count, 8 * each, h2),
        scratch=[pltpu.VMEM((count, 8 * each, h2), F32), pltpu.VMEM((d, d), F32)],
        flops=4 * caps * half * d * d,
    )


def pack_vectors(vectors):
    width = sum(v.shape[1] for v in vectors)

    def body(*refs):
        at = 0
        for ref in refs[:-1]:
            refs[-1][:, at : at + ref.shape[1]] = ref[...]
            at += ref.shape[1]

    return call("pack_vectors", body, (1,), [], [whole(v) for v in vectors], [out_whole((1, width), F32)])[0]


def choose_vectors(ids, own, got, d, fh):
    def body(ids_ref, own_ref, got_ref, *outs):
        s = ids_ref[0]
        for layer in range(2):
            pick_one = lambda a, b: jnp.where(s == layer, own_ref[:, a:b], got_ref[:, a:b])
            for i in range(5):
                outs[6 * layer + i][...] = pick_one(i * d, (i + 1) * d)
            low, high = pick_one(5 * d, 5 * d + fh), pick_one(5 * d + fh, 5 * d + 2 * fh)
            outs[6 * layer + 5][...] = jnp.where(s == 0, low, high)

    outs = [out_whole((1, n), F32) for _ in range(2) for n in [d] * 5 + [fh]]
    got = call("choose_vectors", body, (1,), [ids], [whole(own), whole(got)], outs)
    return got[:6], got[6:]


def plain_sums(s, count, mlp2, cross, attn2, mlp1, image, attn1):
    scatter = lambda g: lax.psum_scatter(g, "dp", scatter_dimension=0, tiled=True)

    def full(act):
        come = swap(act)
        return jnp.concatenate([jnp.where(s == 0, act, come), jnp.where(s == 0, come, act)], 1)

    def side(grad):
        h2 = grad.shape[1] // 2
        return lax.dynamic_slice(grad, (0, s * h2), (grad.shape[0], h2))

    def stacked(w, h2):
        return jnp.concatenate([w[:, i : i + h2] for i in range(0, w.shape[1], h2)], 0)

    def by_section(w):
        parts = w.reshape(2, count, -1, w.shape[1]).swapaxes(0, 1)
        return scatter(parts.reshape(w.shape))

    def mlp(n, du, act, dm):
        return jnp.concatenate(
            [stacked(scatter(tn(n, du)), n.shape[1] // 2), scatter(tn(full(act), side(dm)))], 0
        )

    def attn(h, dqkv, att, da):
        return jnp.concatenate(
            [scatter(tn(h, dqkv[j])) for j in range(3)] + [scatter(tn(full(att), side(da)))], 0
        )

    h, dcq, att, dc = cross
    r_own, r_got, g_own, g_got = [x.reshape(-1, x.shape[-1]) for x in image]
    w_kv = tn(r_own, g_own) + tn(r_got, g_got)
    h2 = dcq.shape[1]
    c = jnp.concatenate([by_section(tn(h, dcq)), by_section(tn(full(att), side(dc)))], 0)
    kv = jnp.concatenate([by_section(w_kv[:, :h2]), by_section(w_kv[:, h2:])], 0)
    return mlp(*mlp2), c, attn(*attn2), mlp(*mlp1), kv, attn(*attn1)


def swap(value):
    return lax.ppermute(value, "section", [(0, 1), (1, 0)])


def on_device(
    text, image, image_counts, cotangent,
    attn_norm_gain, attn_norm_bias, qkv_weight, attn_out_weight, mlp_norm_gain, mlp_norm_bias,
    up_weight, up_bias, down_weight, down_bias,
    cross_norm_gain, cross_norm_bias, cross_query, cross_key_value, cross_out,
):
    s = lax.axis_index("section")
    me = lax.axis_index("dp")
    count = lax.axis_size("dp")
    ids = jnp.stack([s, me]).astype(jnp.int32)
    t, d = text.shape
    h2 = d // 2
    caps, half = image.shape[:2]
    ff = up_bias.shape[1]
    fh = ff // 2
    other = 1 - s

    fast = d // count == 48
    w_qkv, w_out, w_up, w_down = qkv_weight[0], attn_out_weight[0], up_weight[0], down_weight[0]
    vec_own = pack_vectors(
        [attn_norm_gain, attn_norm_bias, mlp_norm_gain, mlp_norm_bias, down_bias, up_bias]
    )
    vec_got = swap(vec_own)
    got_qkv, got_out, got_up, got_down = swap(w_qkv), swap(w_out), swap(w_up), swap(w_down)
    vectors = choose_vectors(ids, vec_own, vec_got, d, fh)
    halves = []
    for layer in range(2):
        halves.append(
            (
                Half(layer, w_qkv, got_qkv, h2),
                Half(layer, w_out, got_out, h2),
                Half(layer, w_up, got_up, fh // 3),
                Half(layer, w_down, got_down, fh // 3),
            )
        )
    gain_i, gain_t = cross_norm_gain[0:1], cross_norm_gain[1:2]
    bias_i, bias_t = cross_norm_bias[0:1], cross_norm_bias[1:2]

    r_own, kv_own, kv_send = key_value(ids, image, gain_i, bias_i, cross_key_value)
    kv_got = swap(kv_send)
    r_got = swap(r_own)

    ag1, ab1, mg1, mb1, bd1, bu1 = vectors[0]
    qw1, ow1, uw1, dw1 = halves[0]
    ag2, ab2, mg2, mb2, bd2, bu2 = vectors[1]
    qw2, ow2, uw2, dw2 = halves[1]

    h1, qkv1, att1, part, send = self_fwd(0, ids, [text], ag1, ab1, qw1, ow1)
    x1, n1, part, send = mlp_fwd(0, ids, text, part, swap(send), mg1, mb1, uw1, bu1, dw1, bd1)
    h2n, qkv2, att2, part, send, z = self_fwd(1, ids, [x1, part, swap(send)], ag2, ab2, qw2, ow2)
    z2, ch, cq, catt, part, send = cross_fwd(
        ids, image_counts, z, part, swap(send), gain_t, bias_t, cross_query, cross_out, kv_own, kv_got
    )
    (act2, du2, dpart, dsend, sums_m2, bup2, z3, n2, mpart, msend) = mlp_grad(
        1, ids, [z2, part, swap(send), cotangent], mg2, mb2, uw2, bu2, dw2, bd2
    )
    y = z3 + mpart + swap(msend).astype(F32)
    layer_out = jnp.where(s == 0, z, y.astype(BF))

    turned = [route(s, me, count, turn) for turn in range(3)] if fast else None
    live = []

    def begin(parts, turn):
        live.append(Sum(parts, count, turn))
        return live[-1]

    def step(*after):
        for x in live:
            x.land(*after)

    def after_live(value, *more):
        return tie(value, *[x.outgoing for x in live], *more) if fast else value

    if fast:
        m2 = begin(up_down_weights(1, turned[0], n2, du2, act2, swap(act2), cotangent, count), 0)
    (dz3, dc, dcq, dkv_own, dkv_send, cpart, csend, sums_n2) = cross_grad(
        ids, image_counts, cotangent, dpart, after_live(swap(dsend)), z3, mg2, cq, cross_query, cross_out,
        kv_own, kv_got,
    )
    dkv_mine = swap(dkv_send)
    if fast:
        parts = cross_weights(
            turned[2], ch, dcq, catt, swap(catt), dc, r_own, r_got, dkv_own, dkv_send, count
        )
        step(parts[-1])
        ckv = begin(parts, 2)
    dz2, da2, dqkv2, hpart, hsend, sums_c = self_grad(
        1, ids, dz3, cpart, after_live(swap(csend)), z2, gain_t, qkv2, qw2, ow2
    )
    if fast:
        step(sums_c)
        parts = self_weights(1, turned[1], h2n, dqkv2, att2, swap(att2), da2, count)
        a2 = begin(parts, 1)
    act1, du1, npart, nsend, sums_a2, bup1, dz = mlp_grad(
        0, ids, [dz2, hpart, after_live(swap(hsend)), z, ag2, n1], mg1, mb1, uw1, bu1, dw1, bd1
    )
    if fast:
        step(sums_a2)
        parts = up_down_weights(0, turned[0], n1, du1, act1, after_live(swap(act1)), dz, count)
        m1 = begin(parts, 0)
    dx1, da1, dqkv1, hpart, hsend, sums_n1 = self_grad(
        0, ids, dz, npart, after_live(swap(nsend)), x1, mg1, qkv1, qw1, ow1
    )
    if fast:
        step(sums_n1)
        parts = self_weights(0, turned[2], h1, dqkv1, att1, after_live(swap(att1)), da1, count)
        a1 = begin(parts, 2)
    input_grad, sums_a1 = text_grad(ids, dx1, hpart, after_live(swap(hsend)), text, ag1, dz)
    image_grad, sums_i = key_value_grad(
        ids, image, gain_i, dkv_own, after_live(dkv_mine, sums_a1), cross_key_value
    )
    if fast:
        step(sums_i)
        finish(live)
        m2, ckv, a2, m1, a1 = [x.result for x in live]
        c2, kv = ckv[: 2 * d // count], ckv[2 * d // count :]
    else:
        m2, c2, a2, m1, kv, a1 = plain_sums(
            s, count, (n2, du2, act2, cotangent), (ch, dcq, catt, dc), (h2n, dqkv2, att2, da2),
            (n1, du1, act1, dz), (r_own, r_got, dkv_own, dkv_send), (h1, dqkv1, att1, da1),
        )

    each = d // count
    small = each // 2
    first = jnp.concatenate([m1, a1], 0)
    second = jnp.concatenate([m2, a2], 0)
    mine = jnp.where(s == 0, first, second)
    theirs = swap(jnp.where(s == 0, second, first))
    left = jnp.where(s == 0, mine, theirs)
    right = jnp.where(s == 0, theirs, mine)
    units = fh // h2
    both = lambda a, b: jnp.concatenate([left[a:b], right[a:b]], 1)

    def columns(start, number):
        return [x[start + i * each : start + (i + 1) * each] for x in (left, right) for i in range(number)]

    g_up = jnp.concatenate(columns(0, units), 1)
    at = units * each
    wide = ff // count
    g_down = both(at, at + wide)
    at += wide
    g_qkv = jnp.concatenate(
        [x[at + i * each : at + (i + 1) * each] for i in range(3) for x in (left, right)], 1
    )
    g_out = both(at + 3 * each, at + 4 * each)

    cross = jnp.concatenate([c2, kv], 0).reshape(4, 2, small, h2)
    keep = lax.dynamic_index_in_dim(cross, s, 1, False)
    come = swap(lax.dynamic_index_in_dim(cross, other, 1, False))
    cross = jnp.concatenate(
        [jnp.where(s == 0, keep, come), jnp.where(s == 0, come, keep)], 2
    )
    g_cq, g_co = cross[0], cross[1]
    g_kv = jnp.concatenate([cross[2], cross[3]], 1)

    bup = [jnp.sum(b, 0) for b in (bup1, bup2)]
    bup_mine = jnp.where(s == 0, bup[0], bup[1])
    bup_come = swap(jnp.where(s == 0, bup[1], bup[0]))
    bup = jnp.concatenate(
        [jnp.where(s == 0, bup_mine, bup_come), jnp.where(s == 0, bup_come, bup_mine)]
    )
    sums_i = sums_i + swap(sums_i)
    pair = lambda a, b: jnp.sum(jnp.where(s == 0, a, b), 0).reshape(count, -1)
    split = lambda v: jnp.sum(v, 0).reshape(2, count, -1).swapaxes(0, 1).reshape(count, -1)
    packed = [
        pair(sums_a1[0], sums_a2[0]), pair(sums_a1[1], sums_a2[1]),
        pair(sums_n1[0], sums_n2[0]), pair(sums_n1[1], sums_n2[1]),
        pair(sums_a2[2], sums_m2[2]), bup.reshape(count, -1),
        split(sums_i[0]), split(sums_c[0]), split(sums_i[1]), split(sums_c[1]),
    ]
    widths = [v.shape[1] for v in packed]
    packed = jnp.concatenate(packed, 1)
    if fast:
        packed = packed[:, None]
        order = paths(count, 0)[0]
        table = [sum(((r >> (len(order) - 1 - k)) & 1) << b for k, b in enumerate(order)) for r in range(count)]
        packed = jnp.take(packed, jnp.array(table, jnp.int32) ^ me, axis=0)
        split_at = [(count >> (k + 1), count >> k) for k in range(len(order))] + [(0, 1)]
        total = Sum([packed[a:b] for a, b in split_at], count, 0, own_order=False)
        finish([total])
        vec = total.result[0]
    else:
        vec = lax.psum_scatter(packed, "dp", scatter_dimension=0, tiled=True)[0]
    cut, at = [], 0
    for w in widths:
        cut.append(vec[at : at + w])
        at += w
    own = lambda v: lax.dynamic_slice(v, (s * small,), (small,))
    return (
        layer_out[None], input_grad[None], image_grad,
        cut[0][None], cut[1][None], g_qkv[None], g_out[None], cut[2][None], cut[3][None],
        g_up[None], cut[5][None], g_down[None], cut[4][None],
        jnp.stack([own(cut[6]), own(cut[7])]), jnp.stack([own(cut[8]), own(cut[9])]),
        g_cq, g_kv, g_co,
    )


def solution(mesh):
    placed = (
        P("dp", None), P("dp", "section", None), P("dp"), P("dp", None),
        P("section", None), P("section", None), P("section", None, None), P("section", None, None),
        P("section", None), P("section", None), P("section", None, None), P("section", None),
        P("section", None, None), P("section", None), P(), P(), P(), P(), P(),
    )
    two, three = P("section", "dp"), P("section", "dp", None)
    last = P(("section", "dp"), None)
    return jax.shard_map(
        on_device,
        mesh=mesh,
        in_specs=placed,
        out_specs=(
            three, three, P("dp", "section", None), two, two, three, three, two, two, three, two,
            three, two, P(None, ("section", "dp")), P(None, ("section", "dp")), last, last, last,
        ),
        check_vma=False,
    )
```

```python
import jax
import jax.numpy as jnp
from jax import lax
from jax.experimental import pallas as pl
from jax.experimental.pallas import tpu as pltpu
from jax.sharding import PartitionSpec as P

HEAD_DIM = 64
SEQ = 64
LANES = 128
CHUNK = 32
ANY = pl.ANY
MT = 256
EPS = 1e-05
NEG = -1e30
SCALE = HEAD_DIM**-0.5
BF = jnp.bfloat16
F32 = jnp.float32


def nn(a, b):
    return lax.dot_general(a, b, (((1,), (0,)), ((), ())), preferred_element_type=F32)


def nt(a, b):
    return lax.dot_general(a, b, (((1,), (1,)), ((), ())), preferred_element_type=F32)


def tn(a, b):
    return lax.dot_general(a, b, (((0,), (0,)), ((), ())), preferred_element_type=F32)


def normalized(v):
    c = v - jnp.mean(v, -1, keepdims=True)
    inv = lax.rsqrt(jnp.mean(c * c, -1, keepdims=True) + EPS)
    return c * inv, inv


def norm(v, g, b):
    return normalized(v)[0] * g + b


def norm_grad(v, g, dh):
    nh, inv = normalized(v)
    e = dh * g
    dv = (e - jnp.mean(e, -1, keepdims=True) - nh * jnp.mean(e * nh, -1, keepdims=True)) * inv
    return dv, dh * nh


def fold(v):
    return jnp.sum(v.reshape(v.shape[0] // 8, 8, v.shape[1]), 0)


def gelu_pair(u):
    k = 0.7978845608028654
    t = jnp.tanh(k * (u + 0.044715 * u * u * u))
    g = 0.5 * u * (1.0 + t)
    dg = 0.5 * (1.0 + t) + 0.5 * u * (1.0 - t * t) * (k * (1.0 + 3 * 0.044715 * u * u))
    return g, dg


def gelu(u):
    k = 0.7978845608028654
    return 0.5 * u * (1.0 + jnp.tanh(k * (u + 0.044715 * u * u * u)))


def two_heads(v):
    low = lax.broadcasted_iota(jnp.int32, v.shape, 1) < HEAD_DIM
    zero = jnp.zeros_like(v)
    return jnp.concatenate([jnp.where(low, v, zero), jnp.where(low, zero, v)], 0)


def join_heads(v):
    half = v.shape[0] // 2
    low = lax.broadcasted_iota(jnp.int32, (half, LANES), 1) < HEAD_DIM
    return jnp.where(low, v[:half], v[half:])


def key_softmax(scores):
    top = jnp.max(scores[0], 0, keepdims=True)
    for s in scores[1:]:
        top = jnp.maximum(top, jnp.max(s, 0, keepdims=True))
    e = [jnp.exp((s - top) * SCALE) for s in scores]
    scale = 1.0 / sum(jnp.sum(x, 0, keepdims=True) for x in e)
    return [x * scale for x in e]


def causal(s):
    key = lax.broadcasted_iota(jnp.int32, s.shape, 0)
    query = lax.broadcasted_iota(jnp.int32, s.shape, 1) % SEQ
    return jnp.where(key <= query, s, NEG)


def below(s, limit):
    return jnp.where(lax.broadcasted_iota(jnp.int32, s.shape, 0) < limit, s, NEG)


def attend(probs, values):
    return join_heads(sum(tn(p.astype(BF), v) for p, v in zip(probs, values)))


def attend_grad(q2, keys, values, probs, go):
    go2 = two_heads(go)
    dp = [nt(v, go2) for v in values]
    mean = sum(jnp.sum(p * d, 0, keepdims=True) for p, d in zip(probs, dp))
    ds = [(p * (d - mean)).astype(BF) for p, d in zip(probs, dp)]
    dq = join_heads(sum(tn(x, k) for x, k in zip(ds, keys))) * SCALE
    dk = [nn(x, q2) * SCALE for x in ds]
    dv = [nn(p.astype(BF), go2) for p in probs]
    return dq, dk, dv


def loop(count, body, unroll=1):
    def step(i, carry):
        for u in range(unroll):
            body(i * unroll + u)
        return carry

    if count == unroll:
        step(0, 0)
    else:
        lax.fori_loop(0, count // unroll, step, 0)


def rows(i, size):
    start = i * size
    return pl.ds(start if isinstance(start, int) else pl.multiple_of(start, size), size)


def lane(start, size):
    return pl.ds(start if isinstance(start, int) else pl.multiple_of(start, LANES), size)


def call(name, body, grid, scalars, ins, outs, scratch=(), flops=0, alias={}):
    def spec(shape, item):
        block, index = item
        if block is ANY:
            return pl.BlockSpec(memory_space=ANY)
        if block is None:
            block = shape
        if index is None:
            index = lambda *_, n=len(shape): (0,) * n
        return pl.BlockSpec(block, index)

    shapes = [jax.ShapeDtypeStruct(o[0], o[1]) for o in outs]
    moved = sum(a[0].size * a[0].dtype.itemsize for a in ins)
    moved += sum(s.size * s.dtype.itemsize for s in shapes)
    return pl.pallas_call(
        body,
        name=name,
        out_shape=shapes,
        input_output_aliases=alias,
        grid_spec=pltpu.PrefetchScalarGridSpec(
            num_scalar_prefetch=len(scalars),
            grid=grid,
            in_specs=[spec(a[0].shape, a[1:]) for a in ins],
            out_specs=[spec(o[0], o[2:]) for o in outs],
            scratch_shapes=list(scratch),
        ),
        compiler_params=pltpu.CompilerParams(vmem_limit_bytes=56 << 20),
        cost_estimate=pl.CostEstimate(flops=int(flops), bytes_accessed=int(moved), transcendentals=0),
    )(*scalars, *[a[0] for a in ins])


def whole(a):
    return (a, None, None)


def out_whole(shape, dtype):
    return (shape, dtype, None, None)


class Half:
    def __init__(self, layer, own, got, width):
        self.layer, self.own, self.got, self.width = layer, own, got, width

    def cols(self, per):
        layer, width = self.layer, self.width
        d = self.own.shape[0]

        def own_map(j, ids, *_):
            return (0, jnp.where(ids[0] == layer, per(j, ids[0]), 0))

        def got_map(j, ids, *_):
            return (0, jnp.where(ids[0] == layer, 0, per(j, ids[0])))

        return [(self.own, (d, width), own_map), (self.got, (d, width), got_map)]

    def rowblocks(self, per):
        layer, width = self.layer, self.width
        d = self.own.shape[1]

        def own_map(j, ids, *_):
            return (jnp.where(ids[0] == layer, per(j, ids[0]), 0), 0)

        def got_map(j, ids, *_):
            return (jnp.where(ids[0] == layer, 0, per(j, ids[0])), 0)

        return [(self.own, (width, d), own_map), (self.got, (width, d), got_map)]


def pick(ids, layer, own_ref, got_ref):
    return jnp.where(ids[0] == layer, own_ref[...], got_ref[...])


def self_fwd(layer, ids, stream, gain, bias, wqkv, wout):
    first = len(stream) == 1
    t, d = stream[0].shape
    h2 = d // 2
    n_in = len(stream)

    def body(ids_ref, *refs):
        xs, refs = refs[:n_in], refs[n_in:]
        g_ref, b_ref, own, got, o_own, o_got = refs[:6]
        outs = refs[6:]
        h_ref, qkv_ref, att_ref, part_ref, send_ref = outs[:5]
        j = pl.program_id(0)

        @pl.when(j == 0)
        def _():
            def chunk(i):
                sl = rows(i, CHUNK)
                if first:
                    x = xs[0][sl, :].astype(F32)
                else:
                    z = (xs[0][sl, :] + xs[1][sl, :] + xs[2][sl, :].astype(F32)).astype(BF)
                    outs[5][sl, :] = z
                    x = z.astype(F32)
                h_ref[sl, :] = norm(x, g_ref[...], b_ref[...]).astype(BF)

            loop(t // CHUNK, chunk, 4)

        w = pick(ids_ref, layer, own, got)

        qkv_ref[j] = nn(h_ref[...], w).astype(BF)

        @pl.when(j == 2)
        def _():
            def block(i):
                units = [
                    (rows(2 * i + c, SEQ), slice(p * LANES, (p + 1) * LANES))
                    for c in range(2) for p in range(h2 // LANES)
                ]
                loaded = [[qkv_ref[m, sl, ln] for m in range(3)] for sl, ln in units]
                scores = [causal(nt(k, two_heads(q))) for q, k, v in loaded]
                probs = [key_softmax([s]) for s in scores]
                done = [attend(p, [x[2]]) for p, x in zip(probs, loaded)]
                for (sl, ln), o in zip(units, done):
                    att_ref[sl, ln] = o.astype(BF)

            loop(t // (2 * SEQ), block)
            wo = pick(ids_ref, layer, o_own, o_got)
            part = nn(att_ref[...], wo)
            part_ref[...] = part
            send_ref[...] = part.astype(BF)

    outs = [
        out_whole((t, d), BF),
        out_whole((3, t, h2), BF),
        out_whole((t, h2), BF),
        out_whole((t, d), F32),
        out_whole((t, d), BF),
    ]
    if not first:
        outs.append(out_whole((t, d), BF))
    ins = [whole(x) for x in stream] + [whole(gain), whole(bias)]
    ins += wqkv.cols(lambda j, s: 2 * j + s) + wout.rowblocks(lambda j, s: s)
    return call(
        f"self_fwd_{layer}", body, (3,), [ids], ins, outs, flops=2 * t * d * 4 * h2 + 2e8
    )


def mlp_fwd(layer, ids, x, a_own, a_got, gain, bias, wup, b_up, wdown, b_down):
    t, d = x.shape
    fh = b_up.shape[1]
    width = wup.width

    def body(ids_ref, x_ref, p_ref, q_ref, g_ref, b_ref, u_own, u_got, bu_ref, d_own, d_got, bd_ref,
             x1_ref, n_ref, part_ref, send_ref):
        j = pl.program_id(0)

        @pl.when(j == 0)
        def _():
            def chunk(i):
                sl = rows(i, CHUNK)
                x1 = x_ref[sl, :].astype(F32) + p_ref[sl, :] + q_ref[sl, :].astype(F32)
                x1_ref[sl, :] = x1
                n_ref[sl, :] = norm(x1, g_ref[...], b_ref[...]).astype(BF)
                part_ref[sl, :] = jnp.broadcast_to(
                    jnp.where(ids_ref[0] == 0, bd_ref[...], 0.0), (CHUNK, d)
                )

            loop(t // CHUNK, chunk, 4)

        up = pick(ids_ref, layer, u_own, u_got)
        down = pick(ids_ref, layer, d_own, d_got)

        def tile(i):
            sl = rows(i, MT)
            u = nn(n_ref[sl, :], up) + bu_ref[...]
            part_ref[sl, :] += nn(gelu(u).astype(BF), down)

        loop(t // MT, tile, t // MT)

        @pl.when(j == pl.num_programs(0) - 1)
        def _():
            def chunk(i):
                sl = rows(i, CHUNK)
                send_ref[sl, :] = part_ref[sl, :].astype(BF)

            loop(t // CHUNK, chunk, 4)

    per = fh // width
    ins = [whole(x), whole(a_own), whole(a_got), whole(gain), whole(bias)]
    ins += wup.cols(lambda j, s: s * per + j)
    ins += [(b_up, (1, width), lambda j, *_: (0, j))]
    ins += wdown.rowblocks(lambda j, s: s * per + j)
    ins += [whole(b_down)]
    outs = [
        out_whole((t, d), F32),
        out_whole((t, d), BF),
        out_whole((t, d), F32),
        out_whole((t, d), BF),
    ]
    return call(f"mlp_fwd_{layer}", body, (per,), [ids], ins, outs, flops=4 * t * d * fh)


def mlp_grad(layer, ids, lead, gain, bias, wup, b_up, wdown, b_down):
    second = layer == 1
    t, d = lead[0].shape
    fh = b_up.shape[1]
    width = wup.width
    n_in = len(lead)

    def body(ids_ref, *refs):
        lead_refs, refs = refs[:n_in], refs[n_in:]
        g_ref, b_ref, u_own, u_got, bu_ref, d_own, d_got, bd_ref = refs[:8]
        outs = refs[8:]
        act_ref, du_ref, dn_ref, dsend_ref, sums_ref, bup_ref = outs[:6]
        extra = outs[6:]
        j = pl.program_id(0)

        @pl.when(j == 0)
        def _():
            sums_ref[...] = jnp.zeros_like(sums_ref)

            def chunk(i):
                sl = rows(i, CHUNK)
                if second:
                    x_ref, p_ref, q_ref, cot_ref = lead_refs
                    x = x_ref[sl, :] + p_ref[sl, :] + q_ref[sl, :].astype(F32)
                    extra[0][sl, :] = x
                    extra[1][sl, :] = norm(x, g_ref[...], b_ref[...]).astype(BF)
                    extra[2][sl, :] = jnp.broadcast_to(
                        jnp.where(ids_ref[0] == 0, bd_ref[...], 0.0), (CHUNK, d)
                    )
                    sums_ref[2] += fold(cot_ref[sl, :].astype(F32))
                else:
                    grad_ref, p_ref, q_ref, z_ref, zg_ref, n_ref = lead_refs
                    dh = p_ref[sl, :] + q_ref[sl, :].astype(F32)
                    dv, dhn = norm_grad(z_ref[sl, :].astype(F32), zg_ref[...], dh)
                    dz = (grad_ref[sl, :] + dv).astype(BF)
                    extra[0][sl, :] = dz
                    sums_ref[0] += fold(dhn)
                    sums_ref[1] += fold(dh)
                    sums_ref[2] += fold(dz.astype(F32))
                dn_ref[sl, :] = jnp.zeros((CHUNK, d), F32)

            loop(t // CHUNK, chunk, 4)

        up = pick(ids_ref, layer, u_own, u_got)
        down = pick(ids_ref, layer, d_own, d_got)
        bup_ref[...] = jnp.zeros_like(bup_ref)
        n_src = extra[1] if second else lead_refs[5]
        dm_src = lead_refs[3] if second else extra[0]

        def tile(i):
            sl = rows(i, MT)
            u = nn(n_src[sl, :], up) + bu_ref[...]
            g, dg = gelu_pair(u)
            g = g.astype(BF)
            act_ref[sl, :] = g
            du = (nt(dm_src[sl, :], down) * dg).astype(BF)
            du_ref[sl, :] = du
            bup_ref[...] += fold(du.astype(F32))
            dn_ref[sl, :] += nt(du, up)
            if second:
                extra[2][sl, :] += nn(g, down)

        loop(t // MT, tile, t // MT)

        @pl.when(j == pl.num_programs(0) - 1)
        def _():
            def chunk(i):
                sl = rows(i, CHUNK)
                dsend_ref[sl, :] = dn_ref[sl, :].astype(BF)
                if second:
                    extra[3][sl, :] = extra[2][sl, :].astype(BF)

            loop(t // CHUNK, chunk, 4)

    per = fh // width
    ins = [whole(a) for a in lead] + [whole(gain), whole(bias)]
    ins += wup.cols(lambda j, s: s * per + j)
    ins += [(b_up, (1, width), lambda j, *_: (0, j))]
    ins += wdown.rowblocks(lambda j, s: s * per + j)
    ins += [whole(b_down)]
    outs = [
        ((t, fh), BF, (t, width), lambda j, *_: (0, j)),
        ((t, fh), BF, (t, width), lambda j, *_: (0, j)),
        out_whole((t, d), F32),
        out_whole((t, d), BF),
        out_whole((3, 8, d), F32),
        ((8, fh), F32, (8, width), lambda j, *_: (0, j)),
    ]
    if second:
        outs += [
            out_whole((t, d), F32),
            out_whole((t, d), BF),
            out_whole((t, d), F32),
            out_whole((t, d), BF),
        ]
    else:
        outs += [out_whole((t, d), BF)]
    return call(
        f"mlp_grad_{layer}", body, (per,), [ids], ins, outs,
        flops=(8 if second else 6) * t * d * fh,
    )


def key_value(ids, image, gain, bias, w):
    caps, half, d = image.shape
    h2 = d // 2
    per = 2

    def body(ids_ref, im_ref, g_ref, b_ref, w_ref, r_ref, own_ref, oth_ref):
        for c in range(per):

            def chunk(i, c=c):
                sl = rows(i, 32)
                r_ref[c, sl, :] = norm(im_ref[c, sl, :].astype(F32), g_ref[...], b_ref[...]).astype(BF)

            loop(half // 32, chunk, 3)
        r = r_ref[...].reshape(per * half, d)
        first = ids_ref[0] == 0
        for i in range(2):
            x = nn(r, w_ref[:, i * d : (i + 1) * d]).astype(BF).reshape(per, half, d)
            low, high = x[:, :, :h2], x[:, :, h2:]
            own_ref[:, :, i * h2 : (i + 1) * h2] = jnp.where(first, low, high)
            oth_ref[:, :, i * h2 : (i + 1) * h2] = jnp.where(first, high, low)

    blk = ((per, half, d), lambda c, *_: (c, 0, 0))
    ins = [(image,) + blk, whole(gain), whole(bias), whole(w)]
    outs = [((caps, half, d), BF) + blk] * 3
    return call("key_value", body, (caps // per,), [ids], ins, outs, flops=4 * caps * half * d * d)


def key_value_grad(ids, image, gain, g_own, g_oth, w, before=None):
    caps, half, d = image.shape
    h2 = d // 2
    per = 2
    steps = caps // per // 2
    first_step = 0 if before is None else steps

    def body(ids_ref, im_ref, g_ref, own_ref, oth_ref, w_ref, *refs):
        dx_ref, sums_ref, dr_ref = refs[-3:]

        @pl.when(pl.program_id(0) == 0)
        def _():
            sums_ref[...] = jnp.zeros_like(sums_ref) if before is None else refs[1][...]

        own = own_ref[...].reshape(per * half, d)
        oth = oth_ref[...].reshape(per * half, d)
        first = ids_ref[0] == 0
        low, high = jnp.where(first, own, oth), jnp.where(first, oth, own)
        g = [x[:, i * h2 : (i + 1) * h2] for i in range(2) for x in (low, high)]
        dr_ref[...] = nt(jnp.concatenate(g, 1), w_ref[...]).reshape(per, half, d)
        for c in range(per):

            def chunk(i, c=c):
                sl = rows(i, 32)
                dr = dr_ref[c, sl, :]
                dv, dhn = norm_grad(im_ref[c, sl, :].astype(F32), g_ref[...], dr)
                dx_ref[c, sl, :] = dv
                sums_ref[0] += fold(dhn)
                sums_ref[1] += fold(dr)

            loop(half // 32, chunk, 3)

    blk = ((per, half, d), lambda c, *_: (c + first_step, 0, 0))
    ins = [(image,) + blk, whole(gain), (g_own,) + blk, (g_oth,) + blk, whole(w)]
    alias = {}
    if before is not None:
        ins += [(before[0], ANY, None), whole(before[1])]
        alias = {6: 0}
    outs = [((caps, half, d), F32) + blk, out_whole((2, 8, d), F32)]
    return call(
        "key_value_grad", body, (steps,), [ids], ins, outs, alias=alias,
        scratch=[pltpu.VMEM((per, half, d), F32)], flops=2 * caps * half * d * d,
    )


def patch_limits(ids_ref, counts_ref, c, half):
    s = ids_ref[0]
    return counts_ref[c] - s * half, counts_ref[c] - (1 - s) * half


def cross_fwd(ids, counts, z, a_own, a_got, gain, bias, wq, wco, kv_own, kv_got):
    caps, half, d = kv_own.shape
    h2 = d // 2
    t = z.shape[0]

    def body(ids_ref, cnt_ref, z_ref, p_ref, q_ref, g_ref, b_ref, wq_ref, wo_ref, own_ref, got_ref,
             z2_ref, h_ref, cq_ref, att_ref, part_ref, send_ref):
        c = pl.program_id(0)

        @pl.when(c == 0)
        def _():
            def chunk(i):
                sl = rows(i, CHUNK)
                x = z_ref[sl, :].astype(F32) + p_ref[sl, :] + q_ref[sl, :].astype(F32)
                z2_ref[sl, :] = x
                h_ref[sl, :] = norm(x, g_ref[...], b_ref[...]).astype(BF)

            loop(t // CHUNK, chunk, 4)

            cq_ref[...] = nn(h_ref[...], wq_ref[...]).astype(BF)

        limits = patch_limits(ids_ref, cnt_ref, c, half)
        sl = rows(c, SEQ)
        for p in range(h2 // LANES):
            ln = slice(p * LANES, (p + 1) * LANES)
            lv = slice(h2 + p * LANES, h2 + (p + 1) * LANES)
            q2 = two_heads(cq_ref[sl, ln])
            sides = (own_ref, got_ref)
            scores = [below(nt(ref[0, :, ln], q2), limit) for ref, limit in zip(sides, limits)]
            att_ref[sl, ln] = attend(key_softmax(scores), [ref[0, :, lv] for ref in sides]).astype(BF)

        @pl.when(c == pl.num_programs(0) - 1)
        def _():
            part = nn(att_ref[...], wo_ref[...])
            part_ref[...] = part
            send_ref[...] = part.astype(BF)

    blk = ((1, half, d), lambda c, *_: (c, 0, 0))
    ins = [whole(z), whole(a_own), whole(a_got), whole(gain), whole(bias)]
    ins += [(wq, (d, h2), lambda c, ids, *_: (0, ids[0])), (wco, (h2, d), lambda c, ids, *_: (ids[0], 0))]
    ins += [(kv_own,) + blk, (kv_got,) + blk]
    outs = [
        out_whole((t, d), F32),
        out_whole((t, d), BF),
        out_whole((t, h2), BF),
        out_whole((t, h2), BF),
        out_whole((t, d), F32),
        out_whole((t, d), BF),
    ]
    return call(
        "cross_fwd", body, (caps,), [ids, counts], ins, outs, flops=4 * t * d * h2 + 16e8
    )


def cross_grad(ids, counts, grad, n_own, n_got, x3, gain3, cq, wq, wco, kv_own, kv_got):
    caps, half, d = kv_own.shape
    h2 = d // 2
    t = x3.shape[0]

    def body(ids_ref, cnt_ref, gr_ref, p_ref, q_ref, x_ref, g_ref, cq_ref, wq_ref, wo_ref, own_ref, got_ref,
             dz_ref, dc_ref, dcq_ref, down_ref, dgot_ref, dh_ref, dsend_ref, sums_ref, da_ref):
        c = pl.program_id(0)

        @pl.when(c == 0)
        def _():
            sums_ref[...] = jnp.zeros_like(sums_ref)

            def chunk(i):
                sl = rows(i, CHUNK)
                dh = p_ref[sl, :] + q_ref[sl, :].astype(F32)
                dv, dhn = norm_grad(x_ref[sl, :], g_ref[...], dh)
                dz = gr_ref[sl, :].astype(F32) + dv
                dz_ref[sl, :] = dz
                dc_ref[sl, :] = dz.astype(BF)
                sums_ref[0] += fold(dhn)
                sums_ref[1] += fold(dh)

            loop(t // CHUNK, chunk, 4)

            da_ref[...] = nt(dc_ref[...], wo_ref[...]).astype(BF)

        limits = patch_limits(ids_ref, cnt_ref, c, half)
        sl = rows(c, SEQ)
        for p in range(h2 // LANES):
            ln = slice(p * LANES, (p + 1) * LANES)
            lv = slice(h2 + p * LANES, h2 + (p + 1) * LANES)
            sides = (own_ref, got_ref)
            keys, values = [ref[0, :, ln] for ref in sides], [ref[0, :, lv] for ref in sides]
            q2 = two_heads(cq_ref[sl, ln])
            probs = key_softmax([below(nt(k, q2), limit) for k, limit in zip(keys, limits)])
            dq, dk, dv = attend_grad(q2, keys, values, probs, da_ref[sl, ln])
            dcq_ref[sl, ln] = dq.astype(BF)
            for out, a, b in zip((down_ref, dgot_ref), dk, dv):
                out[0, :, ln] = a.astype(BF)
                out[0, :, lv] = b.astype(BF)

        @pl.when(c == pl.num_programs(0) - 1)
        def _():
            part = nt(dcq_ref[...], wq_ref[...])
            dh_ref[...] = part
            dsend_ref[...] = part.astype(BF)

    blk = ((1, half, d), lambda c, *_: (c, 0, 0))
    ins = [whole(grad), whole(n_own), whole(n_got), whole(x3), whole(gain3), whole(cq)]
    ins += [(wq, (d, h2), lambda c, ids, *_: (0, ids[0])), (wco, (h2, d), lambda c, ids, *_: (ids[0], 0))]
    ins += [(kv_own,) + blk, (kv_got,) + blk]
    outs = [
        out_whole((t, d), F32),
        out_whole((t, d), BF),
        out_whole((t, h2), BF),
        ((caps, half, d), BF) + blk,
        ((caps, half, d), BF) + blk,
        out_whole((t, d), F32),
        out_whole((t, d), BF),
        out_whole((2, 8, d), F32),
    ]
    return call(
        "cross_grad", body, (caps,), [ids, counts], ins, outs,
        scratch=[pltpu.VMEM((t, h2), BF)], flops=4 * t * d * h2 + 5e9,
    )


def self_grad(layer, ids, grad, h_own, h_got, x, gain_x, qkv, wqkv, wout):
    t, d = x.shape
    h2 = d // 2

    def body(ids_ref, gr_ref, p_ref, q_ref, x_ref, g_ref, qkv_ref, own, got, o_own, o_got,
             dz_ref, da_ref, dqkv_ref, dh_ref, dsend_ref, sums_ref, datt_ref):
        j = pl.program_id(0)

        @pl.when(j == 0)
        def _():
            sums_ref[...] = jnp.zeros_like(sums_ref)

            def chunk(i):
                sl = rows(i, CHUNK)
                dh = p_ref[sl, :] + q_ref[sl, :].astype(F32)
                dv, dhn = norm_grad(x_ref[sl, :].astype(F32), g_ref[...], dh)
                dz = gr_ref[sl, :].astype(F32) + dv
                dz_ref[sl, :] = dz
                da_ref[sl, :] = dz.astype(BF)
                sums_ref[0] += fold(dhn)
                sums_ref[1] += fold(dh)

            loop(t // CHUNK, chunk, 4)
            wo = pick(ids_ref, layer, o_own, o_got)

            datt_ref[...] = nt(da_ref[...], wo).astype(BF)

            def block(i):
                units = [
                    (rows(2 * i + c, SEQ), slice(p * LANES, (p + 1) * LANES))
                    for c in range(2) for p in range(h2 // LANES)
                ]
                loaded = [[qkv_ref[m, sl, ln] for m in range(3)] + [datt_ref[sl, ln]] for sl, ln in units]
                done = []
                for q, k, v, go in loaded:
                    q2 = two_heads(q)
                    probs = key_softmax([causal(nt(k, q2))])
                    dq, dk, dv = attend_grad(q2, [k], [v], probs, go)
                    done.append((dq, dk[0], dv[0]))
                for (sl, ln), grads in zip(units, done):
                    for m in range(3):
                        dqkv_ref[m, sl, ln] = grads[m].astype(BF)

            loop(t // (2 * SEQ), block)

        w = pick(ids_ref, layer, own, got)
        part = nt(dqkv_ref[j], w)

        @pl.when(j == 0)
        def _():
            dh_ref[...] = part

        @pl.when(j > 0)
        def _():
            total = dh_ref[...] + part
            dh_ref[...] = total
            dsend_ref[...] = total.astype(BF)

    ins = [whole(grad), whole(h_own), whole(h_got), whole(x), whole(gain_x), whole(qkv)]
    ins += wqkv.cols(lambda j, s: 2 * j + s) + wout.rowblocks(lambda j, s: s)
    outs = [
        out_whole((t, d), F32),
        out_whole((t, d), BF),
        out_whole((3, t, h2), BF),
        out_whole((t, d), F32),
        out_whole((t, d), BF),
        out_whole((2, 8, d), F32),
    ]
    return call(
        f"self_grad_{layer}", body, (3,), [ids], ins, outs,
        scratch=[pltpu.VMEM((t, h2), BF)], flops=2 * t * d * 4 * h2 + 5e8,
    )


def text_grad(ids, grad, h_own, h_got, x, gain, dz):
    t, d = x.shape

    def body(ids_ref, gr_ref, p_ref, q_ref, x_ref, g_ref, dz_ref, dx_ref, sums_ref):
        sums_ref[...] = jnp.zeros_like(sums_ref)

        def chunk(i):
            sl = rows(i, CHUNK)
            dh = p_ref[sl, :] + q_ref[sl, :].astype(F32)
            dv, dhn = norm_grad(x_ref[sl, :].astype(F32), g_ref[...], dh)
            dx_ref[sl, :] = jnp.where(ids_ref[0] == 0, gr_ref[sl, :] + dv, dz_ref[sl, :].astype(F32))
            sums_ref[0] += fold(dhn)
            sums_ref[1] += fold(dh)

        loop(t // CHUNK, chunk, 4)

    ins = [whole(a) for a in (grad, h_own, h_got, x, gain, dz)]
    outs = [out_whole((t, d), F32), out_whole((2, 8, d), F32)]
    return call("text_grad", body, (1,), [ids], ins, outs)


def paths(count, turn):
    bits = list(range(count.bit_length() - 1))
    near, far = bits[:3], bits[3:]
    return [near[k % 3 :] + near[: k % 3] + far for k in (turn, turn + 1)]


def route(s, me, count, turn):
    first, second = paths(count, turn)
    bits = [jnp.where(s == 0, a, b) for a, b in zip(first, second)]
    return jnp.stack([s, me] + bits).astype(jnp.int32)


def tie(value, *after):
    return lax.optimization_barrier((value, *after))[0]


class Sum:
    def __init__(self, parts, count, turn):
        self.parts, self.count, self.paths = parts, count, paths(count, turn)
        self.arrived, self.result = [], None
        self.send(parts[0])

    def send(self, value):
        self.outgoing = value
        step, n = len(self.arrived), self.count
        perm = [(s * n + i, s * n + (i ^ (1 << self.paths[s][step]))) for s in range(2) for i in range(n)]
        self.flight = lax.ppermute(value, ("section", "dp"), perm)

    def land(self, *after):
        if self.result is not None:
            return
        self.arrived.append(tie(self.flight, *after) if after else self.flight)
        step = len(self.arrived)
        low = self.count >> (step + 1)
        high = max(2 * low, 1)
        total = self.parts[step].astype(F32)
        for a in self.arrived:
            total = total + a[low:high].astype(F32)
        if step < len(self.parts) - 1:
            self.send(total.astype(self.parts[0].dtype))
        else:
            self.result = self.outgoing = total[0]


def finish(sums):
    while any(x.result is None for x in sums):
        for x in sums:
            x.land()


def slots(outs, scr, sems):
    copies, high = [], scr.shape[0]
    for i, out in enumerate(outs):
        low = high // 2 if i < len(outs) - 1 else 0
        copies.append(pltpu.make_async_copy(scr.at[low:high], out, sems.at[i]))
        high = low
    for c in copies:
        c.start()
    for c in copies:
        c.wait()


def putter(ids_ref, scr):
    def put(dest, first, block):
        rel, slot = dest ^ ids_ref[1], 0
        for k in range(scr.shape[0].bit_length() - 1):
            slot = slot * 2 + ((rel >> ids_ref[2 + k]) & 1)
        scr[slot, pl.ds(first, block.shape[0]), :] = block.astype(scr.dtype)

    return put


def slot_outs(count, row_count, cols):
    steps = count.bit_length() - 1
    sizes = [count >> k for k in range(1, steps + 1)] + [1]
    return [((n, row_count, cols), BF, ANY, None) for n in sizes]


def slot_scratch(count, row_count, cols):
    return [pltpu.VMEM((count, row_count, cols), BF), pltpu.SemaphoreType.DMA((count.bit_length(),))]


def up_down_weights(layer, ids, normed, du, act_own, act_got, dm, count):
    t, d = normed.shape
    fh = du.shape[1]
    h2 = d // 2
    up_rows, down_rows = d // count, 2 * fh // count
    units = fh // h2
    per = h2 // down_rows
    row_count = units * up_rows + down_rows

    def body(ids_ref, n_ref, du_ref, own_ref, got_ref, dm_ref, *refs):
        outs, (scr, sems, turned) = refs[:-3], refs[-3:]
        j = pl.program_id(0)
        put = putter(ids_ref, scr)

        @pl.when(j == 0)
        def _():
            turned[...] = n_ref[...].T

        w = nn(turned[...], du_ref[...])
        for dest in range(count):
            put(dest, pl.multiple_of(j * up_rows, up_rows), w[dest * up_rows : (dest + 1) * up_rows])
        s = ids_ref[0]
        dm_half = dm_ref[:, lane(s * h2, h2)]
        for ref, side in ((own_ref, s), (got_ref, 1 - s)):
            w = tn(ref[...], dm_half)
            for i in range(per):
                put(
                    side * (count // 2) + j * per + i, units * up_rows,
                    w[i * down_rows : (i + 1) * down_rows],
                )

        @pl.when(j == units - 1)
        def _():
            slots(outs, scr, sems)

    block = ((t, h2), lambda j, *_: (0, j))
    ins = [whole(normed), (du,) + block, (act_own,) + block, (act_got,) + block, whole(dm)]
    return call(
        f"mlp_weights_{layer}", body, (units,), [ids], ins, slot_outs(count, row_count, h2),
        scratch=slot_scratch(count, row_count, h2) + [pltpu.VMEM((d, t), BF)], flops=4 * t * d * fh,
    )


def self_weights(layer, ids, h, dqkv, att_own, att_got, da, count, before=None):
    t, d = h.shape
    h2 = d // 2
    each = d // count
    first = 0 if before is None else before.shape[1]
    row_count = first + 4 * each

    def body(ids_ref, h_ref, dqkv_ref, own_ref, got_ref, da_ref, *refs):
        (scr, sems, turned), refs = refs[-3:], refs[:-3]
        outs = refs if before is None else refs[1:]
        j = pl.program_id(0)
        put = putter(ids_ref, scr)

        @pl.when(j == 0)
        def _():
            turned[...] = h_ref[...].T
            if before is not None:

                def copy(i):
                    scr[i, :first] = refs[0][i]

                loop(count, copy)

        w = nn(turned[...], dqkv_ref[0])
        at = pl.multiple_of(first + j * each, each)
        for dest in range(count):
            put(dest, at, w[dest * each : (dest + 1) * each])

        @pl.when(j == 2)
        def _():
            s = ids_ref[0]
            da_half = da_ref[:, lane(s * h2, h2)]
            for ref, side in ((own_ref, s), (got_ref, 1 - s)):
                w = tn(ref[...], da_half)
                for i in range(count // 2):
                    put(side * (count // 2) + i, first + 3 * each, w[i * each : (i + 1) * each])
            slots(outs, scr, sems)

    ins = [whole(h), (dqkv, (1, t, h2), lambda j, *_: (j, 0, 0))] + [whole(a) for a in (att_own, att_got, da)]
    if before is not None:
        ins.append(whole(before))
    return call(
        f"self_weights_{layer}", body, (3,), [ids], ins, slot_outs(count, row_count, h2),
        scratch=slot_scratch(count, row_count, h2) + [pltpu.VMEM((d, t), BF)], flops=8 * t * d * h2,
    )


def cross_weights(ids, h, dcq, att_own, att_got, dc, r_own, r_got, g_own, g_got, count):
    caps, half, d = r_own.shape
    h2 = d // 2
    each = h2 // count
    per = 2

    def body(ids_ref, h_ref, dcq_ref, own_ref, got_ref, dc_ref, ro, rg, go, gg, out, acc):
        c = pl.program_id(0)
        flat = lambda ref: ref[...].reshape(per * half, d)
        step = tn(
            jnp.concatenate([flat(ro), flat(rg)], 0), jnp.concatenate([flat(go), flat(gg)], 0)
        )

        @pl.when(c == 0)
        def _():
            acc[...] = step

        @pl.when(c > 0)
        def _():
            acc[...] += step

        @pl.when(c == pl.num_programs(0) - 1)
        def _():
            put = putter(ids_ref, out)

            def place(kind, low, high):
                for dest in range(count):
                    sl = slice(dest * each, (dest + 1) * each)
                    put(dest, kind * 2 * each, jnp.concatenate([low[sl], high[sl]], 0))

            w = tn(h_ref[...], dcq_ref[...])
            place(0, w[:h2], w[h2:])
            s = ids_ref[0]
            dc_half = dc_ref[:, lane(s * h2, h2)]
            own, got = tn(own_ref[...], dc_half), tn(got_ref[...], dc_half)
            place(1, jnp.where(s == 0, own, got), jnp.where(s == 0, got, own))
            for kind in range(2):
                cols = slice(kind * h2, (kind + 1) * h2)
                place(2 + kind, acc[:h2, cols], acc[h2:, cols])

    blk = ((per, half, d), lambda c, *_: (c, 0, 0))
    ins = [whole(a) for a in (h, dcq, att_own, att_got, dc)]
    ins += [(a,) + blk for a in (r_own, r_got, g_own, g_got)]
    return call(
        "cross_weights", body, (caps // per,), [ids], ins, [out_whole((count, 8 * each, h2), BF)],
        scratch=[pltpu.VMEM((d, d), F32)], flops=4 * caps * half * d * d,
    )[0]


def pack_vectors(vectors):
    width = sum(v.shape[1] for v in vectors)

    def body(*refs):
        at = 0
        for ref in refs[:-1]:
            refs[-1][:, at : at + ref.shape[1]] = ref[...]
            at += ref.shape[1]

    return call("pack_vectors", body, (1,), [], [whole(v) for v in vectors], [out_whole((1, width), F32)])[0]


def choose_vectors(ids, own, got, d, fh):
    def body(ids_ref, own_ref, got_ref, *outs):
        s = ids_ref[0]
        for layer in range(2):
            pick_one = lambda a, b: jnp.where(s == layer, own_ref[:, a:b], got_ref[:, a:b])
            for i in range(5):
                outs[6 * layer + i][...] = pick_one(i * d, (i + 1) * d)
            low, high = pick_one(5 * d, 5 * d + fh), pick_one(5 * d + fh, 5 * d + 2 * fh)
            outs[6 * layer + 5][...] = jnp.where(s == 0, low, high)

    outs = [out_whole((1, n), F32) for _ in range(2) for n in [d] * 5 + [fh]]
    got = call("choose_vectors", body, (1,), [ids], [whole(own), whole(got)], outs)
    return got[:6], got[6:]


def pack_sums(ids, layers, cross, bup_own, bup_got):
    d, fh = layers[0][0][0].shape[2], bup_own.shape[1]
    arrays = [x[0] for pair in layers for x in pair] + [x[0] for x in cross] + [bup_own, bup_got]
    width = (len(layers) + len(cross)) * d + 2 * fh

    def body(ids_ref, *refs):
        out, s = refs[-1], ids_ref[0]
        total = lambda v: jnp.sum(v, 0, keepdims=True)
        at = 0
        for i, pair in enumerate(layers):
            a, b = [refs[2 * i + k][pair[k][1]] for k in range(2)]
            out[:, at : at + d] = total(jnp.where(s == 0, a, b))
            at += d
        for i, x in enumerate(cross):
            out[:, at : at + d] = total(refs[2 * len(layers) + i][x[1]])
            at += d
        own, got = total(refs[-3][...]), total(refs[-2][...])
        out[:, at : at + fh] = jnp.where(s == 0, own, got)
        out[:, at + fh :] = jnp.where(s == 0, got, own)

    return call("pack_sums", body, (1,), [ids], [whole(a) for a in arrays], [out_whole((1, width), F32)])[0]


def assemble(name, ids, own, got, plans):
    h2 = own[0].shape[1]
    n = len(own)

    def body(ids_ref, *refs):
        s = ids_ref[0]
        mine = refs[0][...] if n == 1 else jnp.where(s == 0, refs[0][...], refs[1][...])
        theirs = refs[n][...]
        sides = jnp.where(s == 0, mine, theirs), jnp.where(s == 0, theirs, mine)
        for out, (size, where) in zip(refs[n + 1 :], plans):
            for side, i, first in where:
                out[:, i * h2 : (i + 1) * h2] = sides[side][first : first + size]

    outs = [out_whole((size, len(where) * h2), F32) for size, where in plans]
    return call(name, body, (1,), [ids], [whole(a) for a in own + [got]], outs)


def plain_sums(s, count, mlp2, cross, attn2, mlp1, image, attn1):
    scatter = lambda g: lax.psum_scatter(g, "dp", scatter_dimension=0, tiled=True)

    def full(act):
        come = swap(act)
        return jnp.concatenate([jnp.where(s == 0, act, come), jnp.where(s == 0, come, act)], 1)

    def side(grad):
        h2 = grad.shape[1] // 2
        return lax.dynamic_slice(grad, (0, s * h2), (grad.shape[0], h2))

    def stacked(w, h2):
        return jnp.concatenate([w[:, i : i + h2] for i in range(0, w.shape[1], h2)], 0)

    def by_section(w):
        parts = w.reshape(2, count, -1, w.shape[1]).swapaxes(0, 1)
        return scatter(parts.reshape(w.shape))

    def mlp(n, du, act, dm):
        return jnp.concatenate(
            [stacked(scatter(tn(n, du)), n.shape[1] // 2), scatter(tn(full(act), side(dm)))], 0
        )

    def attn(h, dqkv, att, da):
        return jnp.concatenate(
            [scatter(tn(h, dqkv[j])) for j in range(3)] + [scatter(tn(full(att), side(da)))], 0
        )

    h, dcq, att, dc = cross
    r_own, r_got, g_own, g_got = [x.reshape(-1, x.shape[-1]) for x in image]
    w_kv = tn(r_own, g_own) + tn(r_got, g_got)
    h2 = dcq.shape[1]
    c = jnp.concatenate([by_section(tn(h, dcq)), by_section(tn(full(att), side(dc)))], 0)
    kv = jnp.concatenate([by_section(w_kv[:, :h2]), by_section(w_kv[:, h2:])], 0)
    return mlp(*mlp2), c, attn(*attn2), mlp(*mlp1), kv, attn(*attn1)


def swap(value):
    return lax.ppermute(value, "section", [(0, 1), (1, 0)])


def on_device(
    text, image, image_counts, cotangent,
    attn_norm_gain, attn_norm_bias, qkv_weight, attn_out_weight, mlp_norm_gain, mlp_norm_bias,
    up_weight, up_bias, down_weight, down_bias,
    cross_norm_gain, cross_norm_bias, cross_query, cross_key_value, cross_out,
):
    s = lax.axis_index("section")
    me = lax.axis_index("dp")
    count = lax.axis_size("dp")
    ids = jnp.stack([s, me]).astype(jnp.int32)
    t, d = text.shape
    h2 = d // 2
    caps, half = image.shape[:2]
    ff = up_bias.shape[1]
    fh = ff // 2
    other = 1 - s

    fast = d // count == 48
    w_qkv, w_out, w_up, w_down = qkv_weight[0], attn_out_weight[0], up_weight[0], down_weight[0]
    vec_own = pack_vectors(
        [attn_norm_gain, attn_norm_bias, mlp_norm_gain, mlp_norm_bias, down_bias, up_bias]
    )
    vec_got = swap(vec_own)
    got_qkv, got_out, got_up, got_down = swap(w_qkv), swap(w_out), swap(w_up), swap(w_down)
    vectors = choose_vectors(ids, vec_own, vec_got, d, fh)
    halves = []
    for layer in range(2):
        halves.append(
            (
                Half(layer, w_qkv, got_qkv, h2),
                Half(layer, w_out, got_out, h2),
                Half(layer, w_up, got_up, fh // 3),
                Half(layer, w_down, got_down, fh // 3),
            )
        )
    gain_i, gain_t = cross_norm_gain[0:1], cross_norm_gain[1:2]
    bias_i, bias_t = cross_norm_bias[0:1], cross_norm_bias[1:2]

    r_own, kv_own, kv_send = key_value(ids, image, gain_i, bias_i, cross_key_value)
    kv_got = swap(kv_send)
    r_got = swap(r_own)

    ag1, ab1, mg1, mb1, bd1, bu1 = vectors[0]
    qw1, ow1, uw1, dw1 = halves[0]
    ag2, ab2, mg2, mb2, bd2, bu2 = vectors[1]
    qw2, ow2, uw2, dw2 = halves[1]

    h1, qkv1, att1, part, send = self_fwd(0, ids, [text], ag1, ab1, qw1, ow1)
    x1, n1, part, send = mlp_fwd(0, ids, text, part, swap(send), mg1, mb1, uw1, bu1, dw1, bd1)
    h2n, qkv2, att2, part, send, z = self_fwd(1, ids, [x1, part, swap(send)], ag2, ab2, qw2, ow2)
    z2, ch, cq, catt, part, send = cross_fwd(
        ids, image_counts, z, part, swap(send), gain_t, bias_t, cross_query, cross_out, kv_own, kv_got
    )
    (act2, du2, dpart, dsend, sums_m2, bup2, z3, n2, mpart, msend) = mlp_grad(
        1, ids, [z2, part, swap(send), cotangent], mg2, mb2, uw2, bu2, dw2, bd2
    )
    turned = [route(s, me, count, turn) for turn in range(3)] if fast else None
    if fast:
        m2 = Sum(up_down_weights(1, turned[0], n2, du2, act2, swap(act2), cotangent, count), count, 0)
        dsend = tie(swap(dsend), m2.outgoing)
    else:
        dsend = swap(dsend)
    (dz3, dc, dcq, dkv_own, dkv_send, cpart, csend, sums_n2) = cross_grad(
        ids, image_counts, cotangent, dpart, dsend, z3, mg2, cq, cross_query, cross_out, kv_own, kv_got,
    )
    dkv_mine, csend = swap(dkv_send), swap(csend)
    if fast:
        ck = cross_weights(
            turned[1], ch, dcq, catt, swap(catt), dc, r_own, r_got, dkv_own, dkv_send, count
        )
        m2.land(ck)
        csend = tie(csend, m2.outgoing)
    dz2, da2, dqkv2, hpart, hsend, sums_c = self_grad(
        1, ids, dz3, cpart, csend, z2, gain_t, qkv2, qw2, ow2
    )
    hsend = swap(hsend)
    if fast:
        m2.land(sums_c)
        ca = Sum(
            self_weights(1, turned[1], tie(h2n, m2.outgoing), dqkv2, att2, swap(att2), da2, count, ck), count, 1
        )
        hsend = tie(hsend, ca.outgoing)
    act1, du1, npart, nsend, sums_a2, bup1, dz = mlp_grad(
        0, ids, [dz2, hpart, hsend, z, ag2, n1], mg1, mb1, uw1, bu1, dw1, bd1
    )
    nsend = swap(nsend)
    bup_got = swap(jnp.where(s == 0, bup2, bup1))
    if fast:
        m2.land(sums_a2)
        m1 = Sum(
            up_down_weights(0, turned[0], tie(n1, m2.outgoing), du1, act1, swap(act1), dz, count), count, 0
        )
        ca.land(m1.outgoing)
        nsend = tie(nsend, ca.outgoing)
    dx1, da1, dqkv1, hpart, hsend, sums_n1 = self_grad(
        0, ids, dz, npart, nsend, x1, mg1, qkv1, qw1, ow1
    )
    hsend = swap(hsend)
    if fast:
        m2.land(sums_n1)
        ca.land(sums_n1)
        a1 = Sum(
            self_weights(0, turned[2], tie(h1, ca.outgoing), dqkv1, att1, swap(att1), da1, count), count, 2
        )
        m1.land(a1.outgoing)
        hsend = tie(hsend, m1.outgoing)
    input_grad, sums_a1 = text_grad(ids, dx1, hpart, hsend, text, ag1, dz)
    got = list(key_value_grad(ids, image, gain_i, dkv_own, tie(dkv_mine, sums_a1), cross_key_value))
    if fast:
        ca.land(got[1])
        a1.land(got[1])
        got[1] = tie(got[1], ca.outgoing, a1.outgoing)
    image_grad, sums_i = key_value_grad(ids, image, gain_i, dkv_own, dkv_mine, cross_key_value, got)
    bup_own = jnp.where(s == 0, bup1, bup2)
    packed = pack_sums(
        ids,
        [
            [(sums_a1, 0), (sums_a2, 0)], [(sums_a1, 1), (sums_a2, 1)],
            [(sums_n1, 0), (sums_n2, 0)], [(sums_n1, 1), (sums_n2, 1)],
            [(sums_a2, 2), (sums_m2, 2)],
        ],
        [(sums_c, 0), (sums_c, 1), (sums_i, 0), (sums_i, 1)], bup_own, bup_got,
    )
    if fast:
        m1.land(sums_i)
        a1.land(sums_i)
        packed = tie(packed, m1.outgoing, a1.outgoing)
        for k in range(count.bit_length() - 1):
            packed = packed + lax.ppermute(packed, "dp", [(i, i ^ (1 << k)) for i in range(count)])
            if k == 1:
                m1.land(packed)
                a1.land(packed)
                packed = tie(packed, m1.outgoing, a1.outgoing)
        finish([m2, ca, m1, a1])
        m2, ca, m1, a1 = [x.result for x in (m2, ca, m1, a1)]
        half_rows = ca.shape[0] // 2
        ckv, a2 = ca[:half_rows], ca[half_rows:]
    else:
        packed = lax.psum(packed, "dp")
        m2, c2, a2, m1, kv, a1 = plain_sums(
            s, count, (n2, du2, act2, cotangent), (ch, dcq, catt, dc), (h2n, dqkv2, att2, da2),
            (n1, du1, act1, dz), (r_own, r_got, dkv_own, dkv_send), (h1, dqkv1, att1, da1),
        )
        ckv = jnp.concatenate([c2, kv], 0)
    y = z3 + mpart + swap(msend).astype(F32)
    layer_out = jnp.where(s == 0, z, y.astype(BF))

    each = d // count
    small = each // 2
    units = fh // h2
    wide = ff // count
    m_got = swap(jnp.where(s == 0, m2, m1))
    a_got = swap(jnp.where(s == 0, a2, a1))
    cross = ckv.reshape(4, 2, small, h2)
    keep = lax.dynamic_index_in_dim(cross, s, 1, False).reshape(4 * small, h2)
    come = swap(lax.dynamic_index_in_dim(cross, other, 1, False).reshape(4 * small, h2))
    pairs = lambda starts: [(side, 2 * i + side, at) for i, at in enumerate(starts) for side in range(2)]
    g_up, g_down = assemble(
        "assemble_mlp", ids, [m1, m2], m_got,
        [
            (each, [(side, side * units + i, i * each) for side in range(2) for i in range(units)]),
            (wide, pairs([units * each])),
        ],
    )
    g_qkv, g_out = assemble(
        "assemble_self", ids, [a1, a2], a_got,
        [(each, pairs([i * each for i in range(3)])), (each, pairs([3 * each]))],
    )
    g_cq, g_co, g_kv = assemble(
        "assemble_cross", ids, [keep], come,
        [(small, pairs([0])), (small, pairs([small])), (small, pairs([2 * small, 3 * small]))],
    )
    image_sums = packed[:, 7 * d : 9 * d]
    image_sums = image_sums + swap(image_sums)
    mine = lambda i: lax.dynamic_slice(packed, (0, i * d + me * each), (1, each))
    at = s * (d // 2) + me * small
    text_part = lambda i: lax.dynamic_slice(packed, (0, (5 + i) * d + at), (1, small))
    image_part = lambda i: lax.dynamic_slice(image_sums, (0, i * d + at), (1, small))
    g_bup = lax.dynamic_slice(packed, (0, 9 * d + me * wide), (1, wide))
    return (
        layer_out[None], input_grad[None], image_grad,
        mine(0), mine(1), g_qkv[None], g_out[None], mine(2), mine(3),
        g_up[None], g_bup, g_down[None], mine(4),
        jnp.concatenate([image_part(0), text_part(0)], 0), jnp.concatenate([image_part(1), text_part(1)], 0),
        g_cq, g_kv, g_co,
    )


def solution(mesh):
    placed = (
        P("dp", None), P("dp", "section", None), P("dp"), P("dp", None),
        P("section", None), P("section", None), P("section", None, None), P("section", None, None),
        P("section", None), P("section", None), P("section", None, None), P("section", None),
        P("section", None, None), P("section", None), P(), P(), P(), P(), P(),
    )
    two, three = P("section", "dp"), P("section", "dp", None)
    last = P(("section", "dp"), None)
    return jax.shard_map(
        on_device,
        mesh=mesh,
        in_specs=placed,
        out_specs=(
            three, three, P("dp", "section", None), two, two, three, three, two, two, three, two,
            three, two, P(None, ("section", "dp")), P(None, ("section", "dp")), last, last, last,
        ),
        check_vma=False,
    )
```

```python
import jax
import jax.numpy as jnp
from jax import lax
from jax.experimental import pallas as pl
from jax.experimental.pallas import tpu as pltpu
from jax.sharding import PartitionSpec as P

HEAD_DIM = 64
SEQ = 64
LANES = 128
CHUNK = 32
ANY = pl.ANY
MT = 256
EPS = 1e-05
NEG = -1e30
SCALE = HEAD_DIM**-0.5
BF = jnp.bfloat16
F32 = jnp.float32


def nn(a, b):
    return lax.dot_general(a, b, (((1,), (0,)), ((), ())), preferred_element_type=F32)


def nt(a, b):
    return lax.dot_general(a, b, (((1,), (1,)), ((), ())), preferred_element_type=F32)


def tn(a, b):
    return lax.dot_general(a, b, (((0,), (0,)), ((), ())), preferred_element_type=F32)


def normalized(v):
    c = v - jnp.mean(v, -1, keepdims=True)
    inv = lax.rsqrt(jnp.mean(c * c, -1, keepdims=True) + EPS)
    return c * inv, inv


def norm(v, g, b):
    return normalized(v)[0] * g + b


def norm_grad(v, g, dh):
    nh, inv = normalized(v)
    e = dh * g
    dv = (e - jnp.mean(e, -1, keepdims=True) - nh * jnp.mean(e * nh, -1, keepdims=True)) * inv
    return dv, dh * nh


def fold(v):
    return jnp.sum(v.reshape(v.shape[0] // 8, 8, v.shape[1]), 0)


def gelu_pair(u):
    k = 0.7978845608028654
    t = jnp.tanh(k * (u + 0.044715 * u * u * u))
    g = 0.5 * u * (1.0 + t)
    dg = 0.5 * (1.0 + t) + 0.5 * u * (1.0 - t * t) * (k * (1.0 + 3 * 0.044715 * u * u))
    return g, dg


def gelu(u):
    k = 0.7978845608028654
    return 0.5 * u * (1.0 + jnp.tanh(k * (u + 0.044715 * u * u * u)))


def two_heads(v):
    low = lax.broadcasted_iota(jnp.int32, v.shape, 1) < HEAD_DIM
    zero = jnp.zeros_like(v)
    return jnp.concatenate([jnp.where(low, v, zero), jnp.where(low, zero, v)], 0)


def join_heads(v):
    half = v.shape[0] // 2
    low = lax.broadcasted_iota(jnp.int32, (half, LANES), 1) < HEAD_DIM
    return jnp.where(low, v[:half], v[half:])


def key_softmax(scores):
    top = jnp.max(scores[0], 0, keepdims=True)
    for s in scores[1:]:
        top = jnp.maximum(top, jnp.max(s, 0, keepdims=True))
    e = [jnp.exp((s - top) * SCALE) for s in scores]
    scale = 1.0 / sum(jnp.sum(x, 0, keepdims=True) for x in e)
    return [x * scale for x in e]


def causal(s):
    key = lax.broadcasted_iota(jnp.int32, s.shape, 0)
    query = lax.broadcasted_iota(jnp.int32, s.shape, 1) % SEQ
    return jnp.where(key <= query, s, NEG)


def below(s, limit):
    return jnp.where(lax.broadcasted_iota(jnp.int32, s.shape, 0) < limit, s, NEG)


def attend(probs, values):
    return join_heads(sum(tn(p.astype(BF), v) for p, v in zip(probs, values)))


def attend_grad(q2, keys, values, probs, go):
    go2 = two_heads(go)
    dp = [nt(v, go2) for v in values]
    mean = sum(jnp.sum(p * d, 0, keepdims=True) for p, d in zip(probs, dp))
    ds = [(p * (d - mean)).astype(BF) for p, d in zip(probs, dp)]
    dq = join_heads(sum(tn(x, k) for x, k in zip(ds, keys))) * SCALE
    dk = [nn(x, q2) * SCALE for x in ds]
    dv = [nn(p.astype(BF), go2) for p in probs]
    return dq, dk, dv


def loop(count, body, unroll=1):
    def step(i, carry):
        for u in range(unroll):
            body(i * unroll + u)
        return carry

    if count == unroll:
        step(0, 0)
    else:
        lax.fori_loop(0, count // unroll, step, 0)


def rows(i, size):
    start = i * size
    return pl.ds(start if isinstance(start, int) else pl.multiple_of(start, size), size)


def lane(start, size):
    return pl.ds(start if isinstance(start, int) else pl.multiple_of(start, LANES), size)


def call(name, body, grid, scalars, ins, outs, scratch=(), flops=0, alias={}):
    def spec(shape, item):
        block, index = item
        if block is ANY:
            return pl.BlockSpec(memory_space=ANY)
        if block is None:
            block = shape
        if index is None:
            index = lambda *_, n=len(shape): (0,) * n
        return pl.BlockSpec(block, index)

    shapes = [jax.ShapeDtypeStruct(o[0], o[1]) for o in outs]
    moved = sum(a[0].size * a[0].dtype.itemsize for a in ins)
    moved += sum(s.size * s.dtype.itemsize for s in shapes)
    return pl.pallas_call(
        body,
        name=name,
        out_shape=shapes,
        input_output_aliases=alias,
        grid_spec=pltpu.PrefetchScalarGridSpec(
            num_scalar_prefetch=len(scalars),
            grid=grid,
            in_specs=[spec(a[0].shape, a[1:]) for a in ins],
            out_specs=[spec(o[0], o[2:]) for o in outs],
            scratch_shapes=list(scratch),
        ),
        compiler_params=pltpu.CompilerParams(vmem_limit_bytes=40 << 20),
        cost_estimate=pl.CostEstimate(flops=int(flops), bytes_accessed=int(moved), transcendentals=0),
    )(*scalars, *[a[0] for a in ins])


def whole(a):
    return (a, None, None)


def out_whole(shape, dtype):
    return (shape, dtype, None, None)


class Half:
    def __init__(self, layer, own, got, width):
        self.layer, self.own, self.got, self.width = layer, own, got, width

    def cols(self, per):
        layer, width = self.layer, self.width
        d = self.own.shape[0]

        def own_map(j, ids, *_):
            return (0, jnp.where(ids[0] == layer, per(j, ids[0]), 0))

        def got_map(j, ids, *_):
            return (0, jnp.where(ids[0] == layer, 0, per(j, ids[0])))

        return [(self.own, (d, width), own_map), (self.got, (d, width), got_map)]

    def rowblocks(self, per):
        layer, width = self.layer, self.width
        d = self.own.shape[1]

        def own_map(j, ids, *_):
            return (jnp.where(ids[0] == layer, per(j, ids[0]), 0), 0)

        def got_map(j, ids, *_):
            return (jnp.where(ids[0] == layer, 0, per(j, ids[0])), 0)

        return [(self.own, (width, d), own_map), (self.got, (width, d), got_map)]


def pick(ids, layer, own_ref, got_ref):
    return jnp.where(ids[0] == layer, own_ref[...], got_ref[...])


def self_fwd(layer, ids, stream, gain, bias, wqkv, wout):
    first = len(stream) == 1
    t, d = stream[0].shape
    h2 = d // 2
    n_in = len(stream)

    def body(ids_ref, *refs):
        xs, refs = refs[:n_in], refs[n_in:]
        g_ref, b_ref, own, got, o_own, o_got = refs[:6]
        outs = refs[6:]
        h_ref, qkv_ref, att_ref, part_ref, send_ref = outs[:5]
        j = pl.program_id(0)

        @pl.when(j == 0)
        def _():
            def chunk(i):
                sl = rows(i, CHUNK)
                if first:
                    x = xs[0][sl, :].astype(F32)
                else:
                    z = (xs[0][sl, :] + xs[1][sl, :] + xs[2][sl, :].astype(F32)).astype(BF)
                    outs[5][sl, :] = z
                    x = z.astype(F32)
                h_ref[sl, :] = norm(x, g_ref[...], b_ref[...]).astype(BF)

            loop(t // CHUNK, chunk, 4)

        w = pick(ids_ref, layer, own, got)

        qkv_ref[j] = nn(h_ref[...], w).astype(BF)

        @pl.when(j == 2)
        def _():
            def block(i):
                units = [
                    (rows(2 * i + c, SEQ), slice(p * LANES, (p + 1) * LANES))
                    for c in range(2) for p in range(h2 // LANES)
                ]
                loaded = [[qkv_ref[m, sl, ln] for m in range(3)] for sl, ln in units]
                scores = [causal(nt(k, two_heads(q))) for q, k, v in loaded]
                probs = [key_softmax([s]) for s in scores]
                done = [attend(p, [x[2]]) for p, x in zip(probs, loaded)]
                for (sl, ln), o in zip(units, done):
                    att_ref[sl, ln] = o.astype(BF)

            loop(t // (2 * SEQ), block)
            wo = pick(ids_ref, layer, o_own, o_got)
            part = nn(att_ref[...], wo)
            part_ref[...] = part
            send_ref[...] = part.astype(BF)

    outs = [
        out_whole((t, d), BF),
        out_whole((3, t, h2), BF),
        out_whole((t, h2), BF),
        out_whole((t, d), F32),
        out_whole((t, d), BF),
    ]
    if not first:
        outs.append(out_whole((t, d), BF))
    ins = [whole(x) for x in stream] + [whole(gain), whole(bias)]
    ins += wqkv.cols(lambda j, s: 2 * j + s) + wout.rowblocks(lambda j, s: s)
    return call(
        f"self_fwd_{layer}", body, (3,), [ids], ins, outs, flops=2 * t * d * 4 * h2 + 2e8
    )


def mlp_fwd(layer, ids, x, a_own, a_got, gain, bias, wup, b_up, wdown, b_down):
    t, d = x.shape
    fh = b_up.shape[1]
    width = wup.width

    def body(ids_ref, x_ref, p_ref, q_ref, g_ref, b_ref, u_own, u_got, bu_ref, d_own, d_got, bd_ref,
             x1_ref, n_ref, part_ref, send_ref):
        j = pl.program_id(0)

        @pl.when(j == 0)
        def _():
            def chunk(i):
                sl = rows(i, CHUNK)
                x1 = x_ref[sl, :].astype(F32) + p_ref[sl, :] + q_ref[sl, :].astype(F32)
                x1_ref[sl, :] = x1
                n_ref[sl, :] = norm(x1, g_ref[...], b_ref[...]).astype(BF)
                part_ref[sl, :] = jnp.broadcast_to(
                    jnp.where(ids_ref[0] == 0, bd_ref[...], 0.0), (CHUNK, d)
                )

            loop(t // CHUNK, chunk, 4)

        up = pick(ids_ref, layer, u_own, u_got)
        down = pick(ids_ref, layer, d_own, d_got)

        def tile(i):
            sl = rows(i, MT)
            u = nn(n_ref[sl, :], up) + bu_ref[...]
            part_ref[sl, :] += nn(gelu(u).astype(BF), down)

        loop(t // MT, tile, t // MT)

        @pl.when(j == pl.num_programs(0) - 1)
        def _():
            def chunk(i):
                sl = rows(i, CHUNK)
                send_ref[sl, :] = part_ref[sl, :].astype(BF)

            loop(t // CHUNK, chunk, 4)

    per = fh // width
    ins = [whole(x), whole(a_own), whole(a_got), whole(gain), whole(bias)]
    ins += wup.cols(lambda j, s: s * per + j)
    ins += [(b_up, (1, width), lambda j, *_: (0, j))]
    ins += wdown.rowblocks(lambda j, s: s * per + j)
    ins += [whole(b_down)]
    outs = [
        out_whole((t, d), F32),
        out_whole((t, d), BF),
        out_whole((t, d), F32),
        out_whole((t, d), BF),
    ]
    return call(f"mlp_fwd_{layer}", body, (per,), [ids], ins, outs, flops=4 * t * d * fh)


def mlp_grad(layer, ids, lead, gain, bias, wup, b_up, wdown, b_down):
    second = layer == 1
    t, d = lead[0].shape
    fh = b_up.shape[1]
    width = wup.width
    n_in = len(lead)

    def body(ids_ref, *refs):
        lead_refs, refs = refs[:n_in], refs[n_in:]
        g_ref, b_ref, u_own, u_got, bu_ref, d_own, d_got, bd_ref = refs[:8]
        outs = refs[8:]
        act_ref, du_ref, dn_ref, dsend_ref, sums_ref, bup_ref = outs[:6]
        extra = outs[6:]
        j = pl.program_id(0)

        @pl.when(j == 0)
        def _():
            sums_ref[...] = jnp.zeros_like(sums_ref)

            def chunk(i):
                sl = rows(i, CHUNK)
                if second:
                    x_ref, p_ref, q_ref, cot_ref = lead_refs
                    x = x_ref[sl, :] + p_ref[sl, :] + q_ref[sl, :].astype(F32)
                    extra[0][sl, :] = x
                    extra[1][sl, :] = norm(x, g_ref[...], b_ref[...]).astype(BF)
                    extra[2][sl, :] = jnp.broadcast_to(
                        jnp.where(ids_ref[0] == 0, bd_ref[...], 0.0), (CHUNK, d)
                    )
                    sums_ref[2] += fold(cot_ref[sl, :].astype(F32))
                else:
                    grad_ref, p_ref, q_ref, z_ref, zg_ref, n_ref = lead_refs
                    dh = p_ref[sl, :] + q_ref[sl, :].astype(F32)
                    dv, dhn = norm_grad(z_ref[sl, :].astype(F32), zg_ref[...], dh)
                    dz = (grad_ref[sl, :] + dv).astype(BF)
                    extra[0][sl, :] = dz
                    sums_ref[0] += fold(dhn)
                    sums_ref[1] += fold(dh)
                    sums_ref[2] += fold(dz.astype(F32))
                dn_ref[sl, :] = jnp.zeros((CHUNK, d), F32)

            loop(t // CHUNK, chunk, 4)

        up = pick(ids_ref, layer, u_own, u_got)
        down = pick(ids_ref, layer, d_own, d_got)
        bup_ref[...] = jnp.zeros_like(bup_ref)
        n_src = extra[1] if second else lead_refs[5]
        dm_src = lead_refs[3] if second else extra[0]

        def tile(i):
            sl = rows(i, MT)
            u = nn(n_src[sl, :], up) + bu_ref[...]
            g, dg = gelu_pair(u)
            g = g.astype(BF)
            act_ref[sl, :] = g
            du = (nt(dm_src[sl, :], down) * dg).astype(BF)
            du_ref[sl, :] = du
            bup_ref[...] += fold(du.astype(F32))
            dn_ref[sl, :] += nt(du, up)
            if second:
                extra[2][sl, :] += nn(g, down)

        loop(t // MT, tile, t // MT)

        @pl.when(j == pl.num_programs(0) - 1)
        def _():
            def chunk(i):
                sl = rows(i, CHUNK)
                dsend_ref[sl, :] = dn_ref[sl, :].astype(BF)
                if second:
                    extra[3][sl, :] = extra[2][sl, :].astype(BF)

            loop(t // CHUNK, chunk, 4)

    per = fh // width
    ins = [whole(a) for a in lead] + [whole(gain), whole(bias)]
    ins += wup.cols(lambda j, s: s * per + j)
    ins += [(b_up, (1, width), lambda j, *_: (0, j))]
    ins += wdown.rowblocks(lambda j, s: s * per + j)
    ins += [whole(b_down)]
    outs = [
        ((t, fh), BF, (t, width), lambda j, *_: (0, j)),
        ((t, fh), BF, (t, width), lambda j, *_: (0, j)),
        out_whole((t, d), F32),
        out_whole((t, d), BF),
        out_whole((3, 8, d), F32),
        ((8, fh), F32, (8, width), lambda j, *_: (0, j)),
    ]
    if second:
        outs += [
            out_whole((t, d), F32),
            out_whole((t, d), BF),
            out_whole((t, d), F32),
            out_whole((t, d), BF),
        ]
    else:
        outs += [out_whole((t, d), BF)]
    return call(
        f"mlp_grad_{layer}", body, (per,), [ids], ins, outs,
        flops=(8 if second else 6) * t * d * fh,
    )


def key_value(ids, image, gain, bias, w):
    caps, half, d = image.shape
    h2 = d // 2
    per = 2

    def body(ids_ref, im_ref, g_ref, b_ref, w_ref, r_ref, own_ref, oth_ref):
        for c in range(per):

            def chunk(i, c=c):
                sl = rows(i, 32)
                r_ref[c, sl, :] = norm(im_ref[c, sl, :].astype(F32), g_ref[...], b_ref[...]).astype(BF)

            loop(half // 32, chunk, 3)
        r = r_ref[...].reshape(per * half, d)
        first = ids_ref[0] == 0
        for i in range(2):
            x = nn(r, w_ref[:, i * d : (i + 1) * d]).astype(BF).reshape(per, half, d)
            low, high = x[:, :, :h2], x[:, :, h2:]
            own_ref[:, :, i * h2 : (i + 1) * h2] = jnp.where(first, low, high)
            oth_ref[:, :, i * h2 : (i + 1) * h2] = jnp.where(first, high, low)

    blk = ((per, half, d), lambda c, *_: (c, 0, 0))
    ins = [(image,) + blk, whole(gain), whole(bias), whole(w)]
    outs = [((caps, half, d), BF) + blk] * 3
    return call("key_value", body, (caps // per,), [ids], ins, outs, flops=4 * caps * half * d * d)


def key_value_grad(ids, image, gain, g_own, g_oth, w, before=None):
    caps, half, d = image.shape
    h2 = d // 2
    per = 2
    steps = caps // per // 2
    first_step = 0 if before is None else steps

    def body(ids_ref, im_ref, g_ref, own_ref, oth_ref, w_ref, *refs):
        dx_ref, sums_ref, dr_ref = refs[-3:]

        @pl.when(pl.program_id(0) == 0)
        def _():
            sums_ref[...] = jnp.zeros_like(sums_ref) if before is None else refs[1][...]

        own = own_ref[...].reshape(per * half, d)
        oth = oth_ref[...].reshape(per * half, d)
        first = ids_ref[0] == 0
        low, high = jnp.where(first, own, oth), jnp.where(first, oth, own)
        g = [x[:, i * h2 : (i + 1) * h2] for i in range(2) for x in (low, high)]
        dr_ref[...] = nt(jnp.concatenate(g, 1), w_ref[...]).reshape(per, half, d)
        for c in range(per):

            def chunk(i, c=c):
                sl = rows(i, 32)
                dr = dr_ref[c, sl, :]
                dv, dhn = norm_grad(im_ref[c, sl, :].astype(F32), g_ref[...], dr)
                dx_ref[c, sl, :] = dv
                sums_ref[0] += fold(dhn)
                sums_ref[1] += fold(dr)

            loop(half // 32, chunk, 3)

    blk = ((per, half, d), lambda c, *_: (c + first_step, 0, 0))
    ins = [(image,) + blk, whole(gain), (g_own,) + blk, (g_oth,) + blk, whole(w)]
    alias = {}
    if before is not None:
        ins += [(before[0], ANY, None), whole(before[1])]
        alias = {6: 0}
    outs = [((caps, half, d), F32) + blk, out_whole((2, 8, d), F32)]
    return call(
        "key_value_grad", body, (steps,), [ids], ins, outs, alias=alias,
        scratch=[pltpu.VMEM((per, half, d), F32)], flops=2 * caps * half * d * d,
    )


def patch_limits(ids_ref, counts_ref, c, half):
    s = ids_ref[0]
    return counts_ref[c] - s * half, counts_ref[c] - (1 - s) * half


def cross_fwd(ids, counts, z, a_own, a_got, gain, bias, wq, wco, kv_own, kv_got):
    caps, half, d = kv_own.shape
    h2 = d // 2
    t = z.shape[0]

    def body(ids_ref, cnt_ref, z_ref, p_ref, q_ref, g_ref, b_ref, wq_ref, wo_ref, own_ref, got_ref,
             z2_ref, h_ref, cq_ref, att_ref, part_ref, send_ref):
        c = pl.program_id(0)

        @pl.when(c == 0)
        def _():
            def chunk(i):
                sl = rows(i, CHUNK)
                x = z_ref[sl, :].astype(F32) + p_ref[sl, :] + q_ref[sl, :].astype(F32)
                z2_ref[sl, :] = x
                h_ref[sl, :] = norm(x, g_ref[...], b_ref[...]).astype(BF)

            loop(t // CHUNK, chunk, 4)

            cq_ref[...] = nn(h_ref[...], wq_ref[...]).astype(BF)

        limits = patch_limits(ids_ref, cnt_ref, c, half)
        sl = rows(c, SEQ)
        for p in range(h2 // LANES):
            ln = slice(p * LANES, (p + 1) * LANES)
            lv = slice(h2 + p * LANES, h2 + (p + 1) * LANES)
            q2 = two_heads(cq_ref[sl, ln])
            sides = (own_ref, got_ref)
            scores = [below(nt(ref[0, :, ln], q2), limit) for ref, limit in zip(sides, limits)]
            att_ref[sl, ln] = attend(key_softmax(scores), [ref[0, :, lv] for ref in sides]).astype(BF)

        @pl.when(c == pl.num_programs(0) - 1)
        def _():
            part = nn(att_ref[...], wo_ref[...])
            part_ref[...] = part
            send_ref[...] = part.astype(BF)

    blk = ((1, half, d), lambda c, *_: (c, 0, 0))
    ins = [whole(z), whole(a_own), whole(a_got), whole(gain), whole(bias)]
    ins += [(wq, (d, h2), lambda c, ids, *_: (0, ids[0])), (wco, (h2, d), lambda c, ids, *_: (ids[0], 0))]
    ins += [(kv_own,) + blk, (kv_got,) + blk]
    outs = [
        out_whole((t, d), F32),
        out_whole((t, d), BF),
        out_whole((t, h2), BF),
        out_whole((t, h2), BF),
        out_whole((t, d), F32),
        out_whole((t, d), BF),
    ]
    return call(
        "cross_fwd", body, (caps,), [ids, counts], ins, outs, flops=4 * t * d * h2 + 16e8
    )


def cross_grad(ids, counts, grad, n_own, n_got, x3, gain3, cq, wq, wco, kv_own, kv_got):
    caps, half, d = kv_own.shape
    h2 = d // 2
    t = x3.shape[0]

    def body(ids_ref, cnt_ref, gr_ref, p_ref, q_ref, x_ref, g_ref, cq_ref, wq_ref, wo_ref, own_ref, got_ref,
             dz_ref, dc_ref, dcq_ref, down_ref, dgot_ref, dh_ref, dsend_ref, sums_ref, da_ref):
        c = pl.program_id(0)

        @pl.when(c == 0)
        def _():
            sums_ref[...] = jnp.zeros_like(sums_ref)

            def chunk(i):
                sl = rows(i, CHUNK)
                dh = p_ref[sl, :] + q_ref[sl, :].astype(F32)
                dv, dhn = norm_grad(x_ref[sl, :], g_ref[...], dh)
                dz = gr_ref[sl, :].astype(F32) + dv
                dz_ref[sl, :] = dz
                dc_ref[sl, :] = dz.astype(BF)
                sums_ref[0] += fold(dhn)
                sums_ref[1] += fold(dh)

            loop(t // CHUNK, chunk, 4)

            da_ref[...] = nt(dc_ref[...], wo_ref[...]).astype(BF)

        limits = patch_limits(ids_ref, cnt_ref, c, half)
        sl = rows(c, SEQ)
        for p in range(h2 // LANES):
            ln = slice(p * LANES, (p + 1) * LANES)
            lv = slice(h2 + p * LANES, h2 + (p + 1) * LANES)
            sides = (own_ref, got_ref)
            keys, values = [ref[0, :, ln] for ref in sides], [ref[0, :, lv] for ref in sides]
            q2 = two_heads(cq_ref[sl, ln])
            probs = key_softmax([below(nt(k, q2), limit) for k, limit in zip(keys, limits)])
            dq, dk, dv = attend_grad(q2, keys, values, probs, da_ref[sl, ln])
            dcq_ref[sl, ln] = dq.astype(BF)
            for out, a, b in zip((down_ref, dgot_ref), dk, dv):
                out[0, :, ln] = a.astype(BF)
                out[0, :, lv] = b.astype(BF)

        @pl.when(c == pl.num_programs(0) - 1)
        def _():
            part = nt(dcq_ref[...], wq_ref[...])
            dh_ref[...] = part
            dsend_ref[...] = part.astype(BF)

    blk = ((1, half, d), lambda c, *_: (c, 0, 0))
    ins = [whole(grad), whole(n_own), whole(n_got), whole(x3), whole(gain3), whole(cq)]
    ins += [(wq, (d, h2), lambda c, ids, *_: (0, ids[0])), (wco, (h2, d), lambda c, ids, *_: (ids[0], 0))]
    ins += [(kv_own,) + blk, (kv_got,) + blk]
    outs = [
        out_whole((t, d), F32),
        out_whole((t, d), BF),
        out_whole((t, h2), BF),
        ((caps, half, d), BF) + blk,
        ((caps, half, d), BF) + blk,
        out_whole((t, d), F32),
        out_whole((t, d), BF),
        out_whole((2, 8, d), F32),
    ]
    return call(
        "cross_grad", body, (caps,), [ids, counts], ins, outs,
        scratch=[pltpu.VMEM((t, h2), BF)], flops=4 * t * d * h2 + 5e9,
    )


def self_grad(layer, ids, grad, h_own, h_got, x, gain_x, qkv, wqkv, wout):
    t, d = x.shape
    h2 = d // 2

    def body(ids_ref, gr_ref, p_ref, q_ref, x_ref, g_ref, qkv_ref, own, got, o_own, o_got,
             dz_ref, da_ref, dqkv_ref, dh_ref, dsend_ref, sums_ref, datt_ref):
        j = pl.program_id(0)

        @pl.when(j == 0)
        def _():
            sums_ref[...] = jnp.zeros_like(sums_ref)

            def chunk(i):
                sl = rows(i, CHUNK)
                dh = p_ref[sl, :] + q_ref[sl, :].astype(F32)
                dv, dhn = norm_grad(x_ref[sl, :].astype(F32), g_ref[...], dh)
                dz = gr_ref[sl, :].astype(F32) + dv
                dz_ref[sl, :] = dz
                da_ref[sl, :] = dz.astype(BF)
                sums_ref[0] += fold(dhn)
                sums_ref[1] += fold(dh)

            loop(t // CHUNK, chunk, 4)
            wo = pick(ids_ref, layer, o_own, o_got)

            datt_ref[...] = nt(da_ref[...], wo).astype(BF)

            def block(i):
                units = [
                    (rows(2 * i + c, SEQ), slice(p * LANES, (p + 1) * LANES))
                    for c in range(2) for p in range(h2 // LANES)
                ]
                loaded = [[qkv_ref[m, sl, ln] for m in range(3)] + [datt_ref[sl, ln]] for sl, ln in units]
                done = []
                for q, k, v, go in loaded:
                    q2 = two_heads(q)
                    probs = key_softmax([causal(nt(k, q2))])
                    dq, dk, dv = attend_grad(q2, [k], [v], probs, go)
                    done.append((dq, dk[0], dv[0]))
                for (sl, ln), grads in zip(units, done):
                    for m in range(3):
                        dqkv_ref[m, sl, ln] = grads[m].astype(BF)

            loop(t // (2 * SEQ), block)

        w = pick(ids_ref, layer, own, got)
        part = nt(dqkv_ref[j], w)

        @pl.when(j == 0)
        def _():
            dh_ref[...] = part

        @pl.when(j > 0)
        def _():
            total = dh_ref[...] + part
            dh_ref[...] = total
            dsend_ref[...] = total.astype(BF)

    ins = [whole(grad), whole(h_own), whole(h_got), whole(x), whole(gain_x), whole(qkv)]
    ins += wqkv.cols(lambda j, s: 2 * j + s) + wout.rowblocks(lambda j, s: s)
    outs = [
        out_whole((t, d), F32),
        out_whole((t, d), BF),
        out_whole((3, t, h2), BF),
        out_whole((t, d), F32),
        out_whole((t, d), BF),
        out_whole((2, 8, d), F32),
    ]
    return call(
        f"self_grad_{layer}", body, (3,), [ids], ins, outs,
        scratch=[pltpu.VMEM((t, h2), BF)], flops=2 * t * d * 4 * h2 + 5e8,
    )


def text_grad(ids, grad, h_own, h_got, x, gain, dz):
    t, d = x.shape

    def body(ids_ref, gr_ref, p_ref, q_ref, x_ref, g_ref, dz_ref, dx_ref, sums_ref):
        sums_ref[...] = jnp.zeros_like(sums_ref)

        def chunk(i):
            sl = rows(i, CHUNK)
            dh = p_ref[sl, :] + q_ref[sl, :].astype(F32)
            dv, dhn = norm_grad(x_ref[sl, :].astype(F32), g_ref[...], dh)
            dx_ref[sl, :] = jnp.where(ids_ref[0] == 0, gr_ref[sl, :] + dv, dz_ref[sl, :].astype(F32))
            sums_ref[0] += fold(dhn)
            sums_ref[1] += fold(dh)

        loop(t // CHUNK, chunk, 4)

    ins = [whole(a) for a in (grad, h_own, h_got, x, gain, dz)]
    outs = [out_whole((t, d), F32), out_whole((2, 8, d), F32)]
    return call("text_grad", body, (1,), [ids], ins, outs)


def paths(count, turn):
    bits = list(range(count.bit_length() - 1))
    near, far = bits[:3], bits[3:]
    return [near[k % 3 :] + near[: k % 3] + far for k in (turn, turn + 1)]


def route(s, me, count, turn):
    first, second = paths(count, turn)
    bits = [jnp.where(s == 0, a, b) for a, b in zip(first, second)]
    return jnp.stack([s, me] + bits).astype(jnp.int32)


def tie(value, *after):
    return lax.optimization_barrier((value, *after))[0]


class Sum:
    def __init__(self, parts, count, turn):
        self.parts, self.count, self.paths = parts, count, paths(count, turn)
        self.arrived, self.result = [], None
        self.send(parts[0])

    def send(self, value):
        self.outgoing = value
        step, n = len(self.arrived), self.count
        perm = [(s * n + i, s * n + (i ^ (1 << self.paths[s][step]))) for s in range(2) for i in range(n)]
        self.flight = lax.ppermute(value, ("section", "dp"), perm)

    def land(self, *after):
        if self.result is not None:
            return
        self.arrived.append(tie(self.flight, *after) if after else self.flight)
        step = len(self.arrived)
        low = self.count >> (step + 1)
        high = max(2 * low, 1)
        total = self.parts[step].astype(F32)
        for a in self.arrived:
            total = total + a[low:high].astype(F32)
        if step < len(self.parts) - 1:
            self.send(total.astype(self.parts[0].dtype))
        else:
            self.result = self.outgoing = total[0]


def finish(sums):
    while any(x.result is None for x in sums):
        for x in sums:
            x.land()


def slots(outs, scr, sems):
    copies, high = [], scr.shape[0]
    for i, out in enumerate(outs):
        low = high // 2 if i < len(outs) - 1 else 0
        copies.append(pltpu.make_async_copy(scr.at[low:high], out, sems.at[i]))
        high = low
    for c in copies:
        c.start()
    for c in copies:
        c.wait()


def putter(ids_ref, scr):
    def put(dest, first, block):
        rel, slot = dest ^ ids_ref[1], 0
        for k in range(scr.shape[0].bit_length() - 1):
            slot = slot * 2 + ((rel >> ids_ref[2 + k]) & 1)
        scr[slot, pl.ds(first, block.shape[0]), :] = block.astype(scr.dtype)

    return put


def slot_outs(count, row_count, cols):
    steps = count.bit_length() - 1
    sizes = [count >> k for k in range(1, steps + 1)] + [1]
    return [((n, row_count, cols), BF, ANY, None) for n in sizes]


def slot_scratch(count, row_count, cols):
    return [pltpu.VMEM((count, row_count, cols), BF), pltpu.SemaphoreType.DMA((count.bit_length(),))]


def up_down_weights(layer, ids, normed, du, act_own, act_got, dm, count):
    t, d = normed.shape
    fh = du.shape[1]
    h2 = d // 2
    up_rows, down_rows = d // count, 2 * fh // count
    units = fh // h2
    per = h2 // down_rows
    row_count = units * up_rows + down_rows

    def body(ids_ref, n_ref, du_ref, own_ref, got_ref, dm_ref, *refs):
        outs, (scr, sems, turned) = refs[:-3], refs[-3:]
        j = pl.program_id(0)
        put = putter(ids_ref, scr)

        @pl.when(j == 0)
        def _():
            turned[...] = n_ref[...].T

        w = nn(turned[...], du_ref[...])
        for dest in range(count):
            put(dest, pl.multiple_of(j * up_rows, up_rows), w[dest * up_rows : (dest + 1) * up_rows])
        s = ids_ref[0]
        dm_half = dm_ref[:, lane(s * h2, h2)]
        for ref, side in ((own_ref, s), (got_ref, 1 - s)):
            w = tn(ref[...], dm_half)
            for i in range(per):
                put(
                    side * (count // 2) + j * per + i, units * up_rows,
                    w[i * down_rows : (i + 1) * down_rows],
                )

        @pl.when(j == units - 1)
        def _():
            slots(outs, scr, sems)

    block = ((t, h2), lambda j, *_: (0, j))
    ins = [whole(normed), (du,) + block, (act_own,) + block, (act_got,) + block, whole(dm)]
    return call(
        f"mlp_weights_{layer}", body, (units,), [ids], ins, slot_outs(count, row_count, h2),
        scratch=slot_scratch(count, row_count, h2) + [pltpu.VMEM((d, t), BF)], flops=4 * t * d * fh,
    )


def self_weights(layer, ids, h, dqkv, att_own, att_got, da, count, before=None):
    t, d = h.shape
    h2 = d // 2
    each = d // count
    first = 0 if before is None else before.shape[1]
    row_count = first + 4 * each

    def body(ids_ref, h_ref, dqkv_ref, own_ref, got_ref, da_ref, *refs):
        (scr, sems, turned), refs = refs[-3:], refs[:-3]
        outs = refs if before is None else refs[1:]
        j = pl.program_id(0)
        put = putter(ids_ref, scr)

        @pl.when(j == 0)
        def _():
            turned[...] = h_ref[...].T
            if before is not None:

                def copy(i):
                    scr[i, :first] = refs[0][i]

                loop(count, copy)

        w = nn(turned[...], dqkv_ref[0])
        at = pl.multiple_of(first + j * each, each)
        for dest in range(count):
            put(dest, at, w[dest * each : (dest + 1) * each])

        @pl.when(j == 2)
        def _():
            s = ids_ref[0]
            da_half = da_ref[:, lane(s * h2, h2)]
            for ref, side in ((own_ref, s), (got_ref, 1 - s)):
                w = tn(ref[...], da_half)
                for i in range(count // 2):
                    put(side * (count // 2) + i, first + 3 * each, w[i * each : (i + 1) * each])
            slots(outs, scr, sems)

    ins = [whole(h), (dqkv, (1, t, h2), lambda j, *_: (j, 0, 0))] + [whole(a) for a in (att_own, att_got, da)]
    if before is not None:
        ins.append(whole(before))
    return call(
        f"self_weights_{layer}", body, (3,), [ids], ins, slot_outs(count, row_count, h2),
        scratch=slot_scratch(count, row_count, h2) + [pltpu.VMEM((d, t), BF)], flops=8 * t * d * h2,
    )


def cross_weights(ids, h, dcq, att_own, att_got, dc, r_own, r_got, g_own, g_got, count):
    caps, half, d = r_own.shape
    h2 = d // 2
    each = h2 // count
    per = 2

    def body(ids_ref, h_ref, dcq_ref, own_ref, got_ref, dc_ref, ro, rg, go, gg, out, acc):
        c = pl.program_id(0)
        flat = lambda ref: ref[...].reshape(per * half, d)
        step = tn(
            jnp.concatenate([flat(ro), flat(rg)], 0), jnp.concatenate([flat(go), flat(gg)], 0)
        )

        @pl.when(c == 0)
        def _():
            acc[...] = step

        @pl.when(c > 0)
        def _():
            acc[...] += step

        @pl.when(c == pl.num_programs(0) - 1)
        def _():
            put = putter(ids_ref, out)

            def place(kind, low, high):
                for dest in range(count):
                    sl = slice(dest * each, (dest + 1) * each)
                    put(dest, kind * 2 * each, jnp.concatenate([low[sl], high[sl]], 0))

            w = tn(h_ref[...], dcq_ref[...])
            place(0, w[:h2], w[h2:])
            s = ids_ref[0]
            dc_half = dc_ref[:, lane(s * h2, h2)]
            own, got = tn(own_ref[...], dc_half), tn(got_ref[...], dc_half)
            place(1, jnp.where(s == 0, own, got), jnp.where(s == 0, got, own))
            for kind in range(2):
                cols = slice(kind * h2, (kind + 1) * h2)
                place(2 + kind, acc[:h2, cols], acc[h2:, cols])

    blk = ((per, half, d), lambda c, *_: (c, 0, 0))
    ins = [whole(a) for a in (h, dcq, att_own, att_got, dc)]
    ins += [(a,) + blk for a in (r_own, r_got, g_own, g_got)]
    return call(
        "cross_weights", body, (caps // per,), [ids], ins, [out_whole((count, 8 * each, h2), BF)],
        scratch=[pltpu.VMEM((d, d), F32)], flops=4 * caps * half * d * d,
    )[0]


def pack_vectors(vectors):
    width = sum(v.shape[1] for v in vectors)

    def body(*refs):
        at = 0
        for ref in refs[:-1]:
            refs[-1][:, at : at + ref.shape[1]] = ref[...]
            at += ref.shape[1]

    return call("pack_vectors", body, (1,), [], [whole(v) for v in vectors], [out_whole((1, width), F32)])[0]


def choose_vectors(ids, own, got, d, fh):
    def body(ids_ref, own_ref, got_ref, *outs):
        s = ids_ref[0]
        for layer in range(2):
            pick_one = lambda a, b: jnp.where(s == layer, own_ref[:, a:b], got_ref[:, a:b])
            for i in range(5):
                outs[6 * layer + i][...] = pick_one(i * d, (i + 1) * d)
            low, high = pick_one(5 * d, 5 * d + fh), pick_one(5 * d + fh, 5 * d + 2 * fh)
            outs[6 * layer + 5][...] = jnp.where(s == 0, low, high)

    outs = [out_whole((1, n), F32) for _ in range(2) for n in [d] * 5 + [fh]]
    got = call("choose_vectors", body, (1,), [ids], [whole(own), whole(got)], outs)
    return got[:6], got[6:]


def pack_sums(ids, layers, cross, bup_own, bup_got):
    d, fh = layers[0][0][0].shape[2], bup_own.shape[1]
    arrays = [x[0] for pair in layers for x in pair] + [x[0] for x in cross] + [bup_own, bup_got]
    width = (len(layers) + len(cross)) * d + 2 * fh

    def body(ids_ref, *refs):
        out, s = refs[-1], ids_ref[0]
        total = lambda v: jnp.sum(v, 0, keepdims=True)
        at = 0
        for i, pair in enumerate(layers):
            a, b = [refs[2 * i + k][pair[k][1]] for k in range(2)]
            out[:, at : at + d] = total(jnp.where(s == 0, a, b))
            at += d
        for i, x in enumerate(cross):
            out[:, at : at + d] = total(refs[2 * len(layers) + i][x[1]])
            at += d
        own, got = total(refs[-3][...]), total(refs[-2][...])
        out[:, at : at + fh] = jnp.where(s == 0, own, got)
        out[:, at + fh :] = jnp.where(s == 0, got, own)

    return call("pack_sums", body, (1,), [ids], [whole(a) for a in arrays], [out_whole((1, width), F32)])[0]


def assemble(name, ids, own, got, plans):
    h2 = own[0].shape[1]
    n = len(own)

    def body(ids_ref, *refs):
        s = ids_ref[0]
        mine = refs[0][...] if n == 1 else jnp.where(s == 0, refs[0][...], refs[1][...])
        theirs = refs[n][...]
        sides = jnp.where(s == 0, mine, theirs), jnp.where(s == 0, theirs, mine)
        for out, (size, where) in zip(refs[n + 1 :], plans):
            for side, i, first in where:
                out[:, i * h2 : (i + 1) * h2] = sides[side][first : first + size]

    outs = [out_whole((size, len(where) * h2), F32) for size, where in plans]
    return call(name, body, (1,), [ids], [whole(a) for a in own + [got]], outs)


def plain_sums(s, count, mlp2, cross, attn2, mlp1, image, attn1):
    scatter = lambda g: lax.psum_scatter(g, "dp", scatter_dimension=0, tiled=True)

    def full(act):
        come = swap(act)
        return jnp.concatenate([jnp.where(s == 0, act, come), jnp.where(s == 0, come, act)], 1)

    def side(grad):
        h2 = grad.shape[1] // 2
        return lax.dynamic_slice(grad, (0, s * h2), (grad.shape[0], h2))

    def stacked(w, h2):
        return jnp.concatenate([w[:, i : i + h2] for i in range(0, w.shape[1], h2)], 0)

    def by_section(w):
        parts = w.reshape(2, count, -1, w.shape[1]).swapaxes(0, 1)
        return scatter(parts.reshape(w.shape))

    def mlp(n, du, act, dm):
        return jnp.concatenate(
            [stacked(scatter(tn(n, du)), n.shape[1] // 2), scatter(tn(full(act), side(dm)))], 0
        )

    def attn(h, dqkv, att, da):
        return jnp.concatenate(
            [scatter(tn(h, dqkv[j])) for j in range(3)] + [scatter(tn(full(att), side(da)))], 0
        )

    h, dcq, att, dc = cross
    r_own, r_got, g_own, g_got = [x.reshape(-1, x.shape[-1]) for x in image]
    w_kv = tn(r_own, g_own) + tn(r_got, g_got)
    h2 = dcq.shape[1]
    c = jnp.concatenate([by_section(tn(h, dcq)), by_section(tn(full(att), side(dc)))], 0)
    kv = jnp.concatenate([by_section(w_kv[:, :h2]), by_section(w_kv[:, h2:])], 0)
    return mlp(*mlp2), c, attn(*attn2), mlp(*mlp1), kv, attn(*attn1)


def swap(value):
    return lax.ppermute(value, "section", [(0, 1), (1, 0)])


def on_device(
    text, image, image_counts, cotangent,
    attn_norm_gain, attn_norm_bias, qkv_weight, attn_out_weight, mlp_norm_gain, mlp_norm_bias,
    up_weight, up_bias, down_weight, down_bias,
    cross_norm_gain, cross_norm_bias, cross_query, cross_key_value, cross_out,
):
    s = lax.axis_index("section")
    me = lax.axis_index("dp")
    count = lax.axis_size("dp")
    ids = jnp.stack([s, me]).astype(jnp.int32)
    t, d = text.shape
    h2 = d // 2
    caps, half = image.shape[:2]
    ff = up_bias.shape[1]
    fh = ff // 2
    other = 1 - s

    fast = d // count == 48
    w_qkv, w_out, w_up, w_down = qkv_weight[0], attn_out_weight[0], up_weight[0], down_weight[0]
    vec_own = pack_vectors(
        [attn_norm_gain, attn_norm_bias, mlp_norm_gain, mlp_norm_bias, down_bias, up_bias]
    )
    vec_got = swap(vec_own)
    got_qkv, got_out, got_up, got_down = swap(w_qkv), swap(w_out), swap(w_up), swap(w_down)
    vectors = choose_vectors(ids, vec_own, vec_got, d, fh)
    halves = []
    for layer in range(2):
        halves.append(
            (
                Half(layer, w_qkv, got_qkv, h2),
                Half(layer, w_out, got_out, h2),
                Half(layer, w_up, got_up, fh // 3),
                Half(layer, w_down, got_down, fh // 3),
            )
        )
    gain_i, gain_t = cross_norm_gain[0:1], cross_norm_gain[1:2]
    bias_i, bias_t = cross_norm_bias[0:1], cross_norm_bias[1:2]

    r_own, kv_own, kv_send = key_value(ids, image, gain_i, bias_i, cross_key_value)
    kv_got = swap(kv_send)
    r_got = swap(r_own)

    ag1, ab1, mg1, mb1, bd1, bu1 = vectors[0]
    qw1, ow1, uw1, dw1 = halves[0]
    ag2, ab2, mg2, mb2, bd2, bu2 = vectors[1]
    qw2, ow2, uw2, dw2 = halves[1]

    h1, qkv1, att1, part, send = self_fwd(0, ids, [text], ag1, ab1, qw1, ow1)
    x1, n1, part, send = mlp_fwd(0, ids, text, part, swap(send), mg1, mb1, uw1, bu1, dw1, bd1)
    h2n, qkv2, att2, part, send, z = self_fwd(1, ids, [x1, part, swap(send)], ag2, ab2, qw2, ow2)
    z2, ch, cq, catt, part, send = cross_fwd(
        ids, image_counts, z, part, swap(send), gain_t, bias_t, cross_query, cross_out, kv_own, kv_got
    )
    (act2, du2, dpart, dsend, sums_m2, bup2, z3, n2, mpart, msend) = mlp_grad(
        1, ids, [z2, part, swap(send), cotangent], mg2, mb2, uw2, bu2, dw2, bd2
    )
    turned = [route(s, me, count, turn) for turn in range(3)] if fast else None
    if fast:
        m2 = Sum(up_down_weights(1, turned[0], n2, du2, act2, swap(act2), cotangent, count), count, 0)
        dsend = tie(swap(dsend), m2.outgoing)
    else:
        dsend = swap(dsend)
    (dz3, dc, dcq, dkv_own, dkv_send, cpart, csend, sums_n2) = cross_grad(
        ids, image_counts, cotangent, dpart, dsend, z3, mg2, cq, cross_query, cross_out, kv_own, kv_got,
    )
    dkv_mine, csend = swap(dkv_send), swap(csend)
    if fast:
        ck = cross_weights(
            turned[0], ch, dcq, catt, swap(catt), dc, r_own, r_got, dkv_own, dkv_send, count
        )
        m2.land(ck)
        csend = tie(csend, m2.outgoing)
    dz2, da2, dqkv2, hpart, hsend, sums_c = self_grad(
        1, ids, dz3, cpart, csend, z2, gain_t, qkv2, qw2, ow2
    )
    hsend = swap(hsend)
    if fast:
        m2.land(sums_c)
        ca = Sum(
            self_weights(1, turned[0], tie(h2n, m2.outgoing), dqkv2, att2, swap(att2), da2, count, ck), count, 0
        )
        hsend = tie(hsend, ca.outgoing)
    act1, du1, npart, nsend, sums_a2, bup1, dz = mlp_grad(
        0, ids, [dz2, hpart, hsend, z, ag2, n1], mg1, mb1, uw1, bu1, dw1, bd1
    )
    nsend = swap(nsend)
    bup_got = swap(jnp.where(s == 0, bup2, bup1))
    if fast:
        m1 = Sum(
            up_down_weights(0, turned[0], n1, du1, act1, swap(act1), dz, count), count, 0
        )
        ca.land(m1.outgoing)
        nsend = tie(nsend, ca.outgoing)
    dx1, da1, dqkv1, hpart, hsend, sums_n1 = self_grad(
        0, ids, dz, npart, nsend, x1, mg1, qkv1, qw1, ow1
    )
    hsend = swap(hsend)
    if fast:
        m2.land(sums_n1)
        ca.land(sums_n1)
        a1 = Sum(
            self_weights(0, turned[0], tie(h1, ca.outgoing), dqkv1, att1, swap(att1), da1, count), count, 0
        )
        m1.land(a1.outgoing)
        hsend = tie(hsend, m1.outgoing)
    input_grad, sums_a1 = text_grad(ids, dx1, hpart, hsend, text, ag1, dz)
    got = list(key_value_grad(ids, image, gain_i, dkv_own, tie(dkv_mine, sums_a1), cross_key_value))
    if fast:
        for x in (m2, ca, m1, a1):
            x.land(got[1])
        got[1] = tie(got[1], ca.outgoing, m1.outgoing, a1.outgoing)
    image_grad, sums_i = key_value_grad(ids, image, gain_i, dkv_own, dkv_mine, cross_key_value, got)
    bup_own = jnp.where(s == 0, bup1, bup2)
    packed = pack_sums(
        ids,
        [
            [(sums_a1, 0), (sums_a2, 0)], [(sums_a1, 1), (sums_a2, 1)],
            [(sums_n1, 0), (sums_n2, 0)], [(sums_n1, 1), (sums_n2, 1)],
            [(sums_a2, 2), (sums_m2, 2)],
        ],
        [(sums_c, 0), (sums_c, 1), (sums_i, 0), (sums_i, 1)], bup_own, bup_got,
    )
    if fast:
        for x in (m1, a1, ca):
            x.land(sums_i)
        packed = tie(packed, m1.outgoing, a1.outgoing)
        for k in reversed(range(count.bit_length() - 1)):
            packed = packed + lax.ppermute(packed, "dp", [(i, i ^ (1 << k)) for i in range(count)])
            if k == 2:
                a1.land(packed)
                packed = tie(packed, a1.outgoing)
        finish([m2, ca, m1, a1])
        m2, ca, m1, a1 = [x.result for x in (m2, ca, m1, a1)]
        half_rows = ca.shape[0] // 2
        ckv, a2 = ca[:half_rows], ca[half_rows:]
    else:
        packed = lax.psum(packed, "dp")
        m2, c2, a2, m1, kv, a1 = plain_sums(
            s, count, (n2, du2, act2, cotangent), (ch, dcq, catt, dc), (h2n, dqkv2, att2, da2),
            (n1, du1, act1, dz), (r_own, r_got, dkv_own, dkv_send), (h1, dqkv1, att1, da1),
        )
        ckv = jnp.concatenate([c2, kv], 0)
    y = z3 + mpart + swap(msend).astype(F32)
    layer_out = jnp.where(s == 0, z, y.astype(BF))

    each = d // count
    small = each // 2
    units = fh // h2
    wide = ff // count
    m_got = swap(jnp.where(s == 0, m2, m1))
    a_got = swap(jnp.where(s == 0, a2, a1))
    cross = ckv.reshape(4, 2, small, h2)
    keep = lax.dynamic_index_in_dim(cross, s, 1, False).reshape(4 * small, h2)
    come = swap(lax.dynamic_index_in_dim(cross, other, 1, False).reshape(4 * small, h2))
    pairs = lambda starts: [(side, 2 * i + side, at) for i, at in enumerate(starts) for side in range(2)]
    g_up, g_down = assemble(
        "assemble_mlp", ids, [m1, m2], m_got,
        [
            (each, [(side, side * units + i, i * each) for side in range(2) for i in range(units)]),
            (wide, pairs([units * each])),
        ],
    )
    g_qkv, g_out = assemble(
        "assemble_self", ids, [a1, a2], a_got,
        [(each, pairs([i * each for i in range(3)])), (each, pairs([3 * each]))],
    )
    g_cq, g_co, g_kv = assemble(
        "assemble_cross", ids, [keep], come,
        [(small, pairs([0])), (small, pairs([small])), (small, pairs([2 * small, 3 * small]))],
    )
    image_sums = packed[:, 7 * d : 9 * d]
    image_sums = image_sums + swap(image_sums)
    mine = lambda i: lax.dynamic_slice(packed, (0, i * d + me * each), (1, each))
    at = s * (d // 2) + me * small
    text_part = lambda i: lax.dynamic_slice(packed, (0, (5 + i) * d + at), (1, small))
    image_part = lambda i: lax.dynamic_slice(image_sums, (0, i * d + at), (1, small))
    g_bup = lax.dynamic_slice(packed, (0, 9 * d + me * wide), (1, wide))
    return (
        layer_out[None], input_grad[None], image_grad,
        mine(0), mine(1), g_qkv[None], g_out[None], mine(2), mine(3),
        g_up[None], g_bup, g_down[None], mine(4),
        jnp.concatenate([image_part(0), text_part(0)], 0), jnp.concatenate([image_part(1), text_part(1)], 0),
        g_cq, g_kv, g_co,
    )


def solution(mesh):
    placed = (
        P("dp", None), P("dp", "section", None), P("dp"), P("dp", None),
        P("section", None), P("section", None), P("section", None, None), P("section", None, None),
        P("section", None), P("section", None), P("section", None, None), P("section", None),
        P("section", None, None), P("section", None), P(), P(), P(), P(), P(),
    )
    two, three = P("section", "dp"), P("section", "dp", None)
    last = P(("section", "dp"), None)
    return jax.shard_map(
        on_device,
        mesh=mesh,
        in_specs=placed,
        out_specs=(
            three, three, P("dp", "section", None), two, two, three, three, two, two, three, two,
            three, two, P(None, ("section", "dp")), P(None, ("section", "dp")), last, last, last,
        ),
        check_vma=False,
    )
```

```python
import jax
import jax.numpy as jnp
from jax import lax
from jax.experimental import pallas as pl
from jax.experimental.pallas import tpu as pltpu
from jax.sharding import PartitionSpec as P

HEAD_DIM = 64
SEQ = 64
LANES = 128
CHUNK = 32
ANY = pl.ANY
MT = 256
EPS = 1e-05
NEG = -1e30
SCALE = HEAD_DIM**-0.5
BF = jnp.bfloat16
F32 = jnp.float32


def nn(a, b):
    return lax.dot_general(a, b, (((1,), (0,)), ((), ())), preferred_element_type=F32)


def nt(a, b):
    return lax.dot_general(a, b, (((1,), (1,)), ((), ())), preferred_element_type=F32)


def tn(a, b):
    return lax.dot_general(a, b, (((0,), (0,)), ((), ())), preferred_element_type=F32)


def normalized(v):
    c = v - jnp.mean(v, -1, keepdims=True)
    inv = lax.rsqrt(jnp.mean(c * c, -1, keepdims=True) + EPS)
    return c * inv, inv


def norm(v, g, b):
    return normalized(v)[0] * g + b


def norm_grad(v, g, dh):
    nh, inv = normalized(v)
    e = dh * g
    dv = (e - jnp.mean(e, -1, keepdims=True) - nh * jnp.mean(e * nh, -1, keepdims=True)) * inv
    return dv, dh * nh


def fold(v):
    return jnp.sum(v.reshape(v.shape[0] // 8, 8, v.shape[1]), 0)


def gelu_pair(u):
    k = 0.7978845608028654
    t = jnp.tanh(k * (u + 0.044715 * u * u * u))
    g = 0.5 * u * (1.0 + t)
    dg = 0.5 * (1.0 + t) + 0.5 * u * (1.0 - t * t) * (k * (1.0 + 3 * 0.044715 * u * u))
    return g, dg


def gelu(u):
    k = 0.7978845608028654
    return 0.5 * u * (1.0 + jnp.tanh(k * (u + 0.044715 * u * u * u)))


def two_heads(v):
    low = lax.broadcasted_iota(jnp.int32, v.shape, 1) < HEAD_DIM
    zero = jnp.zeros_like(v)
    return jnp.concatenate([jnp.where(low, v, zero), jnp.where(low, zero, v)], 0)


def join_heads(v):
    half = v.shape[0] // 2
    low = lax.broadcasted_iota(jnp.int32, (half, LANES), 1) < HEAD_DIM
    return jnp.where(low, v[:half], v[half:])


def key_softmax(scores):
    top = jnp.max(scores[0], 0, keepdims=True)
    for s in scores[1:]:
        top = jnp.maximum(top, jnp.max(s, 0, keepdims=True))
    e = [jnp.exp((s - top) * SCALE) for s in scores]
    scale = 1.0 / sum(jnp.sum(x, 0, keepdims=True) for x in e)
    return [x * scale for x in e]


def causal(s):
    key = lax.broadcasted_iota(jnp.int32, s.shape, 0)
    query = lax.broadcasted_iota(jnp.int32, s.shape, 1) % SEQ
    return jnp.where(key <= query, s, NEG)


def below(s, limit):
    return jnp.where(lax.broadcasted_iota(jnp.int32, s.shape, 0) < limit, s, NEG)


def attend(probs, values):
    return join_heads(sum(tn(p.astype(BF), v) for p, v in zip(probs, values)))


def attend_grad(q2, keys, values, probs, go):
    go2 = two_heads(go)
    dp = [nt(v, go2) for v in values]
    mean = sum(jnp.sum(p * d, 0, keepdims=True) for p, d in zip(probs, dp))
    ds = [(p * (d - mean)).astype(BF) for p, d in zip(probs, dp)]
    dq = join_heads(sum(tn(x, k) for x, k in zip(ds, keys))) * SCALE
    dk = [nn(x, q2) * SCALE for x in ds]
    dv = [nn(p.astype(BF), go2) for p in probs]
    return dq, dk, dv


def loop(count, body, unroll=1):
    def step(i, carry):
        for u in range(unroll):
            body(i * unroll + u)
        return carry

    if count == unroll:
        step(0, 0)
    else:
        lax.fori_loop(0, count // unroll, step, 0)


def rows(i, size):
    start = i * size
    return pl.ds(start if isinstance(start, int) else pl.multiple_of(start, size), size)


def lane(start, size):
    return pl.ds(start if isinstance(start, int) else pl.multiple_of(start, LANES), size)


def call(name, body, grid, scalars, ins, outs, scratch=(), flops=0, alias={}):
    def spec(shape, item):
        block, index = item
        if block is ANY:
            return pl.BlockSpec(memory_space=ANY)
        if block is None:
            block = shape
        if index is None:
            index = lambda *_, n=len(shape): (0,) * n
        return pl.BlockSpec(block, index)

    shapes = [jax.ShapeDtypeStruct(o[0], o[1]) for o in outs]

    def held(shape, dtype, block):
        if block is ANY:
            return 0
        dims = list(shape if block is None else block)
        dims[-2] = max(dims[-2], 8)
        size = jnp.dtype(dtype).itemsize
        for n in dims:
            size *= n
        return 2 * size

    room = 16 << 20
    room += sum(held(a[0].shape, a[0].dtype, a[1]) for a in ins)
    room += sum(held(o[0], o[1], o[2]) for o in outs)
    room += sum(held(x.shape, x.dtype, None) // 2 for x in scratch if len(x.shape) > 1)
    moved = sum(a[0].size * a[0].dtype.itemsize for a in ins)
    moved += sum(s.size * s.dtype.itemsize for s in shapes)
    return pl.pallas_call(
        body,
        name=name,
        out_shape=shapes,
        input_output_aliases=alias,
        grid_spec=pltpu.PrefetchScalarGridSpec(
            num_scalar_prefetch=len(scalars),
            grid=grid,
            in_specs=[spec(a[0].shape, a[1:]) for a in ins],
            out_specs=[spec(o[0], o[2:]) for o in outs],
            scratch_shapes=list(scratch),
        ),
        compiler_params=pltpu.CompilerParams(vmem_limit_bytes=room),
        cost_estimate=pl.CostEstimate(flops=int(flops), bytes_accessed=int(moved), transcendentals=0),
    )(*scalars, *[a[0] for a in ins])


def whole(a):
    return (a, None, None)


def out_whole(shape, dtype):
    return (shape, dtype, None, None)


class Half:
    def __init__(self, layer, own, got, width):
        self.layer, self.own, self.got, self.width = layer, own, got, width

    def cols(self, per):
        layer, width = self.layer, self.width
        d = self.own.shape[0]

        def own_map(j, ids, *_):
            return (0, jnp.where(ids[0] == layer, per(j, ids[0]), 0))

        def got_map(j, ids, *_):
            return (0, jnp.where(ids[0] == layer, 0, per(j, ids[0])))

        return [(self.own, (d, width), own_map), (self.got, (d, width), got_map)]

    def rowblocks(self, per):
        layer, width = self.layer, self.width
        d = self.own.shape[1]

        def own_map(j, ids, *_):
            return (jnp.where(ids[0] == layer, per(j, ids[0]), 0), 0)

        def got_map(j, ids, *_):
            return (jnp.where(ids[0] == layer, 0, per(j, ids[0])), 0)

        return [(self.own, (width, d), own_map), (self.got, (width, d), got_map)]


def pick(ids, layer, own_ref, got_ref):
    return jnp.where(ids[0] == layer, own_ref[...], got_ref[...])


def self_fwd(layer, ids, stream, gain, bias, wqkv, wout):
    first = len(stream) == 1
    t, d = stream[0].shape
    h2 = d // 2
    n_in = len(stream)

    def body(ids_ref, *refs):
        xs, refs = refs[:n_in], refs[n_in:]
        g_ref, b_ref, own, got, o_own, o_got = refs[:6]
        outs = refs[6:]
        h_ref, qkv_ref, att_ref, send_ref = outs[:4]
        j = pl.program_id(0)

        @pl.when(j == 0)
        def _():
            def chunk(i):
                sl = rows(i, CHUNK)
                if first:
                    x = xs[0][sl, :].astype(F32)
                else:
                    z = (xs[0][sl, :] + xs[1][sl, :].astype(F32) + xs[2][sl, :].astype(F32)).astype(BF)
                    outs[4][sl, :] = z
                    x = z.astype(F32)
                h_ref[sl, :] = norm(x, g_ref[...], b_ref[...]).astype(BF)

            loop(t // CHUNK, chunk, 4)

        w = pick(ids_ref, layer, own, got)

        qkv_ref[j] = nn(h_ref[...], w).astype(BF)

        @pl.when(j == 2)
        def _():
            def block(i):
                units = [
                    (rows(2 * i + c, SEQ), slice(p * LANES, (p + 1) * LANES))
                    for c in range(2) for p in range(h2 // LANES)
                ]
                loaded = [[qkv_ref[m, sl, ln] for m in range(3)] for sl, ln in units]
                scores = [causal(nt(k, two_heads(q))) for q, k, v in loaded]
                probs = [key_softmax([s]) for s in scores]
                done = [attend(p, [x[2]]) for p, x in zip(probs, loaded)]
                for (sl, ln), o in zip(units, done):
                    att_ref[sl, ln] = o.astype(BF)

            loop(t // (2 * SEQ), block)
            wo = pick(ids_ref, layer, o_own, o_got)
            send_ref[...] = nn(att_ref[...], wo).astype(BF)

    outs = [
        out_whole((t, d), BF),
        out_whole((3, t, h2), BF),
        out_whole((t, h2), BF),
        out_whole((t, d), BF),
    ]
    if not first:
        outs.append(out_whole((t, d), BF))
    ins = [whole(x) for x in stream] + [whole(gain), whole(bias)]
    ins += wqkv.cols(lambda j, s: 2 * j + s) + wout.rowblocks(lambda j, s: s)
    return call(
        f"self_fwd_{layer}", body, (3,), [ids], ins, outs, flops=2 * t * d * 4 * h2 + 2e8
    )


def mlp_fwd(layer, ids, x, a_own, a_got, gain, bias, wup, b_up, wdown, b_down):
    t, d = x.shape
    fh = b_up.shape[1]
    width = wup.width

    def body(ids_ref, x_ref, p_ref, q_ref, g_ref, b_ref, u_own, u_got, bu_ref, d_own, d_got, bd_ref,
             x1_ref, n_ref, send_ref, part_ref):
        j = pl.program_id(0)

        @pl.when(j == 0)
        def _():
            def chunk(i):
                sl = rows(i, CHUNK)
                x1 = x_ref[sl, :].astype(F32) + p_ref[sl, :].astype(F32) + q_ref[sl, :].astype(F32)
                x1_ref[sl, :] = x1
                n_ref[sl, :] = norm(x1, g_ref[...], b_ref[...]).astype(BF)
                part_ref[sl, :] = jnp.broadcast_to(
                    jnp.where(ids_ref[0] == 0, bd_ref[...], 0.0), (CHUNK, d)
                )

            loop(t // CHUNK, chunk, 4)

        up = pick(ids_ref, layer, u_own, u_got)
        down = pick(ids_ref, layer, d_own, d_got)

        def tile(i):
            sl = rows(i, MT)
            u = nn(n_ref[sl, :], up) + bu_ref[...]
            part_ref[sl, :] += nn(gelu(u).astype(BF), down)

        loop(t // MT, tile, t // MT)

        @pl.when(j == pl.num_programs(0) - 1)
        def _():
            def chunk(i):
                sl = rows(i, CHUNK)
                send_ref[sl, :] = part_ref[sl, :].astype(BF)

            loop(t // CHUNK, chunk, 4)

    per = fh // width
    ins = [whole(x), whole(a_own), whole(a_got), whole(gain), whole(bias)]
    ins += wup.cols(lambda j, s: s * per + j)
    ins += [(b_up, (1, width), lambda j, *_: (0, j))]
    ins += wdown.rowblocks(lambda j, s: s * per + j)
    ins += [whole(b_down)]
    outs = [out_whole((t, d), F32), out_whole((t, d), BF), out_whole((t, d), BF)]
    return call(
        f"mlp_fwd_{layer}", body, (per,), [ids], ins, outs, scratch=[pltpu.VMEM((t, d), F32)],
        flops=4 * t * d * fh,
    )


def mlp_grad(layer, ids, lead, gain, bias, wup, b_up, wdown, b_down):
    second = layer == 1
    t, d = lead[0].shape
    fh = b_up.shape[1]
    width = wup.width
    n_in = len(lead)

    def body(ids_ref, *refs):
        lead_refs, refs = refs[:n_in], refs[n_in:]
        g_ref, b_ref, u_own, u_got, bu_ref, d_own, d_got, bd_ref = refs[:8]
        outs, scr = refs[8 : 16 if second else 14], refs[16 if second else 14 :]
        act_ref, du_ref, dsend_ref, sums_ref, bup_ref = outs[:5]
        extra, dn_ref = outs[5:], scr[0]
        j = pl.program_id(0)

        @pl.when(j == 0)
        def _():
            sums_ref[...] = jnp.zeros_like(sums_ref)

            def chunk(i):
                sl = rows(i, CHUNK)
                if second:
                    x_ref, p_ref, q_ref, cot_ref = lead_refs
                    x = x_ref[sl, :] + p_ref[sl, :].astype(F32) + q_ref[sl, :].astype(F32)
                    extra[0][sl, :] = x
                    extra[1][sl, :] = norm(x, g_ref[...], b_ref[...]).astype(BF)
                    scr[1][sl, :] = jnp.broadcast_to(
                        jnp.where(ids_ref[0] == 0, bd_ref[...], 0.0), (CHUNK, d)
                    )
                    sums_ref[2] += fold(cot_ref[sl, :].astype(F32))
                else:
                    grad_ref, p_ref, q_ref, z_ref, zg_ref, n_ref = lead_refs
                    dh = p_ref[sl, :].astype(F32) + q_ref[sl, :].astype(F32)
                    dv, dhn = norm_grad(z_ref[sl, :].astype(F32), zg_ref[...], dh)
                    dz = (grad_ref[sl, :] + dv).astype(BF)
                    extra[0][sl, :] = dz
                    sums_ref[0] += fold(dhn)
                    sums_ref[1] += fold(dh)
                    sums_ref[2] += fold(dz.astype(F32))
                dn_ref[sl, :] = jnp.zeros((CHUNK, d), F32)

            loop(t // CHUNK, chunk, 4)

        up = pick(ids_ref, layer, u_own, u_got)
        down = pick(ids_ref, layer, d_own, d_got)
        bup_ref[...] = jnp.zeros_like(bup_ref)
        n_src = extra[1] if second else lead_refs[5]
        dm_src = lead_refs[3] if second else extra[0]

        def tile(i):
            sl = rows(i, MT)
            u = nn(n_src[sl, :], up) + bu_ref[...]
            g, dg = gelu_pair(u)
            g = g.astype(BF)
            act_ref[sl, :] = g
            du = (nt(dm_src[sl, :], down) * dg).astype(BF)
            du_ref[sl, :] = du
            bup_ref[...] += fold(du.astype(F32))
            dn_ref[sl, :] += nt(du, up)
            if second:
                scr[1][sl, :] += nn(g, down)

        loop(t // MT, tile, t // MT)

        @pl.when(j == pl.num_programs(0) - 1)
        def _():
            def chunk(i):
                sl = rows(i, CHUNK)
                dsend_ref[sl, :] = dn_ref[sl, :].astype(BF)
                if second:
                    extra[2][sl, :] = scr[1][sl, :].astype(BF)

            loop(t // CHUNK, chunk, 4)

    per = fh // width
    ins = [whole(a) for a in lead] + [whole(gain), whole(bias)]
    ins += wup.cols(lambda j, s: s * per + j)
    ins += [(b_up, (1, width), lambda j, *_: (0, j))]
    ins += wdown.rowblocks(lambda j, s: s * per + j)
    ins += [whole(b_down)]
    outs = [
        ((t, fh), BF, (t, width), lambda j, *_: (0, j)),
        ((t, fh), BF, (t, width), lambda j, *_: (0, j)),
        out_whole((t, d), BF),
        out_whole((3, 8, d), F32),
        ((8, fh), F32, (8, width), lambda j, *_: (0, j)),
    ]
    if second:
        outs += [out_whole((t, d), F32), out_whole((t, d), BF), out_whole((t, d), BF)]
    else:
        outs += [out_whole((t, d), BF)]
    return call(
        f"mlp_grad_{layer}", body, (per,), [ids], ins, outs,
        scratch=[pltpu.VMEM((t, d), F32)] * (2 if second else 1),
        flops=(8 if second else 6) * t * d * fh,
    )


def key_value(ids, image, gain, bias, w):
    caps, half, d = image.shape
    h2 = d // 2
    per = 2

    def body(ids_ref, im_ref, g_ref, b_ref, w_ref, r_ref, own_ref, oth_ref):
        for c in range(per):

            def chunk(i, c=c):
                sl = rows(i, 32)
                r_ref[c, sl, :] = norm(im_ref[c, sl, :].astype(F32), g_ref[...], b_ref[...]).astype(BF)

            loop(half // 32, chunk, 3)
        r = r_ref[...].reshape(per * half, d)
        first = ids_ref[0] == 0
        for i in range(2):
            x = nn(r, w_ref[:, i * d : (i + 1) * d]).astype(BF).reshape(per, half, d)
            low, high = x[:, :, :h2], x[:, :, h2:]
            own_ref[:, :, i * h2 : (i + 1) * h2] = jnp.where(first, low, high)
            oth_ref[:, :, i * h2 : (i + 1) * h2] = jnp.where(first, high, low)

    blk = ((per, half, d), lambda c, *_: (c, 0, 0))
    ins = [(image,) + blk, whole(gain), whole(bias), whole(w)]
    outs = [((caps, half, d), BF) + blk] * 3
    return call("key_value", body, (caps // per,), [ids], ins, outs, flops=4 * caps * half * d * d)


def key_value_grad(ids, image, gain, g_own, g_oth, w, before=None):
    caps, half, d = image.shape
    h2 = d // 2
    per = 2
    steps = caps // per // 2
    first_step = 0 if before is None else steps

    def body(ids_ref, im_ref, g_ref, own_ref, oth_ref, w_ref, *refs):
        dx_ref, sums_ref, dr_ref = refs[-3:]

        @pl.when(pl.program_id(0) == 0)
        def _():
            sums_ref[...] = jnp.zeros_like(sums_ref) if before is None else refs[1][...]

        own = own_ref[...].reshape(per * half, d)
        oth = oth_ref[...].reshape(per * half, d)
        first = ids_ref[0] == 0
        low, high = jnp.where(first, own, oth), jnp.where(first, oth, own)
        g = [x[:, i * h2 : (i + 1) * h2] for i in range(2) for x in (low, high)]
        dr_ref[...] = nt(jnp.concatenate(g, 1), w_ref[...]).reshape(per, half, d)
        for c in range(per):

            def chunk(i, c=c):
                sl = rows(i, 32)
                dr = dr_ref[c, sl, :]
                dv, dhn = norm_grad(im_ref[c, sl, :].astype(F32), g_ref[...], dr)
                dx_ref[c, sl, :] = dv
                sums_ref[0] += fold(dhn)
                sums_ref[1] += fold(dr)

            loop(half // 32, chunk, 3)

    blk = ((per, half, d), lambda c, *_: (c + first_step, 0, 0))
    ins = [(image,) + blk, whole(gain), (g_own,) + blk, (g_oth,) + blk, whole(w)]
    alias = {}
    if before is not None:
        ins += [(before[0], ANY, None), whole(before[1])]
        alias = {6: 0}
    outs = [((caps, half, d), F32) + blk, out_whole((2, 8, d), F32)]
    return call(
        "key_value_grad", body, (steps,), [ids], ins, outs, alias=alias,
        scratch=[pltpu.VMEM((per, half, d), F32)], flops=2 * caps * half * d * d,
    )


def patch_limits(ids_ref, counts_ref, c, half):
    s = ids_ref[0]
    return counts_ref[c] - s * half, counts_ref[c] - (1 - s) * half


def cross_fwd(ids, counts, z, a_own, a_got, gain, bias, wq, wco, kv_own, kv_got):
    caps, half, d = kv_own.shape
    h2 = d // 2
    t = z.shape[0]

    def body(ids_ref, cnt_ref, z_ref, p_ref, q_ref, g_ref, b_ref, wq_ref, wo_ref, own_ref, got_ref,
             z2_ref, h_ref, cq_ref, att_ref, send_ref):
        c = pl.program_id(0)

        @pl.when(c == 0)
        def _():
            def chunk(i):
                sl = rows(i, CHUNK)
                x = z_ref[sl, :].astype(F32) + p_ref[sl, :].astype(F32) + q_ref[sl, :].astype(F32)
                z2_ref[sl, :] = x
                h_ref[sl, :] = norm(x, g_ref[...], b_ref[...]).astype(BF)

            loop(t // CHUNK, chunk, 4)

            cq_ref[...] = nn(h_ref[...], wq_ref[...]).astype(BF)

        limits = patch_limits(ids_ref, cnt_ref, c, half)
        sl = rows(c, SEQ)
        for p in range(h2 // LANES):
            ln = slice(p * LANES, (p + 1) * LANES)
            lv = slice(h2 + p * LANES, h2 + (p + 1) * LANES)
            q2 = two_heads(cq_ref[sl, ln])
            sides = (own_ref, got_ref)
            scores = [below(nt(ref[0, :, ln], q2), limit) for ref, limit in zip(sides, limits)]
            att_ref[sl, ln] = attend(key_softmax(scores), [ref[0, :, lv] for ref in sides]).astype(BF)

        @pl.when(c == pl.num_programs(0) - 1)
        def _():
            send_ref[...] = nn(att_ref[...], wo_ref[...]).astype(BF)

    blk = ((1, half, d), lambda c, *_: (c, 0, 0))
    ins = [whole(z), whole(a_own), whole(a_got), whole(gain), whole(bias)]
    ins += [(wq, (d, h2), lambda c, ids, *_: (0, ids[0])), (wco, (h2, d), lambda c, ids, *_: (ids[0], 0))]
    ins += [(kv_own,) + blk, (kv_got,) + blk]
    outs = [
        out_whole((t, d), F32),
        out_whole((t, d), BF),
        out_whole((t, h2), BF),
        out_whole((t, h2), BF),
        out_whole((t, d), BF),
    ]
    return call(
        "cross_fwd", body, (caps,), [ids, counts], ins, outs, flops=4 * t * d * h2 + 16e8
    )


def cross_grad(ids, counts, grad, n_own, n_got, x3, gain3, cq, wq, wco, kv_own, kv_got):
    caps, half, d = kv_own.shape
    h2 = d // 2
    t = x3.shape[0]

    def body(ids_ref, cnt_ref, gr_ref, p_ref, q_ref, x_ref, g_ref, cq_ref, wq_ref, wo_ref, own_ref, got_ref,
             dz_ref, dc_ref, dcq_ref, down_ref, dgot_ref, dsend_ref, sums_ref, da_ref):
        c = pl.program_id(0)

        @pl.when(c == 0)
        def _():
            sums_ref[...] = jnp.zeros_like(sums_ref)

            def chunk(i):
                sl = rows(i, CHUNK)
                dh = p_ref[sl, :].astype(F32) + q_ref[sl, :].astype(F32)
                dv, dhn = norm_grad(x_ref[sl, :], g_ref[...], dh)
                dz = gr_ref[sl, :].astype(F32) + dv
                dz_ref[sl, :] = dz
                dc_ref[sl, :] = dz.astype(BF)
                sums_ref[0] += fold(dhn)
                sums_ref[1] += fold(dh)

            loop(t // CHUNK, chunk, 4)

            da_ref[...] = nt(dc_ref[...], wo_ref[...]).astype(BF)

        limits = patch_limits(ids_ref, cnt_ref, c, half)
        sl = rows(c, SEQ)
        for p in range(h2 // LANES):
            ln = slice(p * LANES, (p + 1) * LANES)
            lv = slice(h2 + p * LANES, h2 + (p + 1) * LANES)
            sides = (own_ref, got_ref)
            keys, values = [ref[0, :, ln] for ref in sides], [ref[0, :, lv] for ref in sides]
            q2 = two_heads(cq_ref[sl, ln])
            probs = key_softmax([below(nt(k, q2), limit) for k, limit in zip(keys, limits)])
            dq, dk, dv = attend_grad(q2, keys, values, probs, da_ref[sl, ln])
            dcq_ref[sl, ln] = dq.astype(BF)
            for out, a, b in zip((down_ref, dgot_ref), dk, dv):
                out[0, :, ln] = a.astype(BF)
                out[0, :, lv] = b.astype(BF)

        @pl.when(c == pl.num_programs(0) - 1)
        def _():
            dsend_ref[...] = nt(dcq_ref[...], wq_ref[...]).astype(BF)

    blk = ((1, half, d), lambda c, *_: (c, 0, 0))
    ins = [whole(grad), whole(n_own), whole(n_got), whole(x3), whole(gain3), whole(cq)]
    ins += [(wq, (d, h2), lambda c, ids, *_: (0, ids[0])), (wco, (h2, d), lambda c, ids, *_: (ids[0], 0))]
    ins += [(kv_own,) + blk, (kv_got,) + blk]
    outs = [
        out_whole((t, d), F32),
        out_whole((t, d), BF),
        out_whole((t, h2), BF),
        ((caps, half, d), BF) + blk,
        ((caps, half, d), BF) + blk,
        out_whole((t, d), BF),
        out_whole((2, 8, d), F32),
    ]
    return call(
        "cross_grad", body, (caps,), [ids, counts], ins, outs,
        scratch=[pltpu.VMEM((t, h2), BF)], flops=4 * t * d * h2 + 5e9,
    )


def self_grad(layer, ids, grad, h_own, h_got, x, gain_x, qkv, wqkv, wout):
    t, d = x.shape
    h2 = d // 2

    def body(ids_ref, gr_ref, p_ref, q_ref, x_ref, g_ref, qkv_ref, own, got, o_own, o_got,
             dz_ref, da_ref, dqkv_ref, dsend_ref, sums_ref, datt_ref, dh_ref):
        j = pl.program_id(0)

        @pl.when(j == 0)
        def _():
            sums_ref[...] = jnp.zeros_like(sums_ref)

            def chunk(i):
                sl = rows(i, CHUNK)
                dh = p_ref[sl, :].astype(F32) + q_ref[sl, :].astype(F32)
                dv, dhn = norm_grad(x_ref[sl, :].astype(F32), g_ref[...], dh)
                dz = gr_ref[sl, :].astype(F32) + dv
                dz_ref[sl, :] = dz
                da_ref[sl, :] = dz.astype(BF)
                sums_ref[0] += fold(dhn)
                sums_ref[1] += fold(dh)

            loop(t // CHUNK, chunk, 4)
            wo = pick(ids_ref, layer, o_own, o_got)

            datt_ref[...] = nt(da_ref[...], wo).astype(BF)

            def block(i):
                units = [
                    (rows(2 * i + c, SEQ), slice(p * LANES, (p + 1) * LANES))
                    for c in range(2) for p in range(h2 // LANES)
                ]
                loaded = [[qkv_ref[m, sl, ln] for m in range(3)] + [datt_ref[sl, ln]] for sl, ln in units]
                done = []
                for q, k, v, go in loaded:
                    q2 = two_heads(q)
                    probs = key_softmax([causal(nt(k, q2))])
                    dq, dk, dv = attend_grad(q2, [k], [v], probs, go)
                    done.append((dq, dk[0], dv[0]))
                for (sl, ln), grads in zip(units, done):
                    for m in range(3):
                        dqkv_ref[m, sl, ln] = grads[m].astype(BF)

            loop(t // (2 * SEQ), block)

        w = pick(ids_ref, layer, own, got)
        part = nt(dqkv_ref[j], w)

        @pl.when(j == 0)
        def _():
            dh_ref[...] = part

        @pl.when(j == 1)
        def _():
            dh_ref[...] += part

        @pl.when(j == 2)
        def _():
            dsend_ref[...] = (dh_ref[...] + part).astype(BF)

    ins = [whole(grad), whole(h_own), whole(h_got), whole(x), whole(gain_x), whole(qkv)]
    ins += wqkv.cols(lambda j, s: 2 * j + s) + wout.rowblocks(lambda j, s: s)
    outs = [
        out_whole((t, d), F32),
        out_whole((t, d), BF),
        out_whole((3, t, h2), BF),
        out_whole((t, d), BF),
        out_whole((2, 8, d), F32),
    ]
    return call(
        f"self_grad_{layer}", body, (3,), [ids], ins, outs,
        scratch=[pltpu.VMEM((t, h2), BF), pltpu.VMEM((t, d), F32)], flops=2 * t * d * 4 * h2 + 5e8,
    )


def text_grad(ids, grad, h_own, h_got, x, gain, dz):
    t, d = x.shape

    def body(ids_ref, gr_ref, p_ref, q_ref, x_ref, g_ref, dz_ref, dx_ref, sums_ref):
        sums_ref[...] = jnp.zeros_like(sums_ref)

        def chunk(i):
            sl = rows(i, CHUNK)
            dh = p_ref[sl, :].astype(F32) + q_ref[sl, :].astype(F32)
            dv, dhn = norm_grad(x_ref[sl, :].astype(F32), g_ref[...], dh)
            dx_ref[sl, :] = jnp.where(ids_ref[0] == 0, gr_ref[sl, :] + dv, dz_ref[sl, :].astype(F32))
            sums_ref[0] += fold(dhn)
            sums_ref[1] += fold(dh)

        loop(t // CHUNK, chunk, 4)

    ins = [whole(a) for a in (grad, h_own, h_got, x, gain, dz)]
    outs = [out_whole((t, d), F32), out_whole((2, 8, d), F32)]
    return call("text_grad", body, (1,), [ids], ins, outs)


def paths(count, turn):
    bits = list(range(count.bit_length() - 1))
    near, far = bits[:3], bits[3:]
    return [near[k % 3 :] + near[: k % 3] + far for k in (turn, turn + 1)]


def route(s, me, count, turn):
    first, second = paths(count, turn)
    bits = [jnp.where(s == 0, a, b) for a, b in zip(first, second)]
    return jnp.stack([s, me] + bits).astype(jnp.int32)


def tie(value, *after):
    return lax.optimization_barrier((value, *after))[0]


class Sum:
    def __init__(self, parts, count, turn):
        self.parts, self.count, self.paths = parts, count, paths(count, turn)
        self.arrived, self.result = [], None
        self.send(parts[0])

    def send(self, value):
        self.outgoing = value
        step, n = len(self.arrived), self.count
        perm = [(s * n + i, s * n + (i ^ (1 << self.paths[s][step]))) for s in range(2) for i in range(n)]
        self.flight = lax.ppermute(value, ("section", "dp"), perm)

    def land(self, *after):
        if self.result is not None:
            return
        self.arrived.append(tie(self.flight, *after) if after else self.flight)
        step = len(self.arrived)
        low = self.count >> (step + 1)
        high = max(2 * low, 1)
        total = self.parts[step].astype(F32)
        for a in self.arrived:
            total = total + a[low:high].astype(F32)
        if step < len(self.parts) - 1:
            self.send(total.astype(self.parts[0].dtype))
        else:
            self.result = self.outgoing = total[0]


def finish(sums):
    while any(x.result is None for x in sums):
        for x in sums:
            x.land()


def slots(outs, scr, sems):
    copies, high = [], scr.shape[0]
    for i, out in enumerate(outs):
        low = high // 2 if i < len(outs) - 1 else 0
        copies.append(pltpu.make_async_copy(scr.at[low:high], out, sems.at[i]))
        high = low
    for c in copies:
        c.start()
    for c in copies:
        c.wait()


def putter(ids_ref, scr):
    def put(dest, first, block):
        rel, slot = dest ^ ids_ref[1], 0
        for k in range(scr.shape[0].bit_length() - 1):
            slot = slot * 2 + ((rel >> ids_ref[2 + k]) & 1)
        scr[slot, pl.ds(first, block.shape[0]), :] = block.astype(scr.dtype)

    return put


def slot_outs(count, row_count, cols):
    steps = count.bit_length() - 1
    sizes = [count >> k for k in range(1, steps + 1)] + [1]
    return [((n, row_count, cols), BF, ANY, None) for n in sizes]


def slot_scratch(count, row_count, cols):
    return [pltpu.VMEM((count, row_count, cols), BF), pltpu.SemaphoreType.DMA((count.bit_length(),))]


def up_down_weights(layer, ids, normed, du, act_own, act_got, dm, count):
    t, d = normed.shape
    fh = du.shape[1]
    h2 = d // 2
    up_rows, down_rows = d // count, 2 * fh // count
    units = fh // h2
    per = h2 // down_rows
    row_count = units * up_rows + down_rows

    def body(ids_ref, n_ref, du_ref, own_ref, got_ref, dm_ref, *refs):
        outs, (scr, sems, turned) = refs[:-3], refs[-3:]
        j = pl.program_id(0)
        put = putter(ids_ref, scr)

        @pl.when(j == 0)
        def _():
            turned[...] = n_ref[...].T

        w = nn(turned[...], du_ref[...])
        for dest in range(count):
            put(dest, pl.multiple_of(j * up_rows, up_rows), w[dest * up_rows : (dest + 1) * up_rows])
        s = ids_ref[0]
        dm_half = dm_ref[:, lane(s * h2, h2)]
        for ref, side in ((own_ref, s), (got_ref, 1 - s)):
            w = tn(ref[...], dm_half)
            for i in range(per):
                put(
                    side * (count // 2) + j * per + i, units * up_rows,
                    w[i * down_rows : (i + 1) * down_rows],
                )

        @pl.when(j == units - 1)
        def _():
            slots(outs, scr, sems)

    block = ((t, h2), lambda j, *_: (0, j))
    ins = [whole(normed), (du,) + block, (act_own,) + block, (act_got,) + block, whole(dm)]
    return call(
        f"mlp_weights_{layer}", body, (units,), [ids], ins, slot_outs(count, row_count, h2),
        scratch=slot_scratch(count, row_count, h2) + [pltpu.VMEM((d, t), BF)], flops=4 * t * d * fh,
    )


def self_weights(layer, ids, h, dqkv, att_own, att_got, da, count, before=None):
    t, d = h.shape
    h2 = d // 2
    each = d // count
    first = 0 if before is None else before.shape[1]
    row_count = first + 4 * each

    def body(ids_ref, h_ref, dqkv_ref, own_ref, got_ref, da_ref, *refs):
        (scr, sems, turned), refs = refs[-3:], refs[:-3]
        outs = refs if before is None else refs[1:]
        j = pl.program_id(0)
        put = putter(ids_ref, scr)

        @pl.when(j == 0)
        def _():
            turned[...] = h_ref[...].T
            if before is not None:

                def copy(i):
                    scr[i, :first] = refs[0][i]

                loop(count, copy)

        w = nn(turned[...], dqkv_ref[0])
        at = pl.multiple_of(first + j * each, each)
        for dest in range(count):
            put(dest, at, w[dest * each : (dest + 1) * each])

        @pl.when(j == 2)
        def _():
            s = ids_ref[0]
            da_half = da_ref[:, lane(s * h2, h2)]
            for ref, side in ((own_ref, s), (got_ref, 1 - s)):
                w = tn(ref[...], da_half)
                for i in range(count // 2):
                    put(side * (count // 2) + i, first + 3 * each, w[i * each : (i + 1) * each])
            slots(outs, scr, sems)

    ins = [whole(h), (dqkv, (1, t, h2), lambda j, *_: (j, 0, 0))] + [whole(a) for a in (att_own, att_got, da)]
    if before is not None:
        ins.append(whole(before))
    return call(
        f"self_weights_{layer}", body, (3,), [ids], ins, slot_outs(count, row_count, h2),
        scratch=slot_scratch(count, row_count, h2) + [pltpu.VMEM((d, t), BF)], flops=8 * t * d * h2,
    )


def cross_weights(ids, h, dcq, att_own, att_got, dc, r_own, r_got, g_own, g_got, count):
    caps, half, d = r_own.shape
    h2 = d // 2
    each = h2 // count
    per = 2

    def body(ids_ref, h_ref, dcq_ref, own_ref, got_ref, dc_ref, ro, rg, go, gg, out, acc):
        c = pl.program_id(0)
        flat = lambda ref: ref[...].reshape(per * half, d)
        step = tn(
            jnp.concatenate([flat(ro), flat(rg)], 0), jnp.concatenate([flat(go), flat(gg)], 0)
        )

        @pl.when(c == 0)
        def _():
            acc[...] = step

        @pl.when(c > 0)
        def _():
            acc[...] += step

        @pl.when(c == pl.num_programs(0) - 1)
        def _():
            put = putter(ids_ref, out)

            def place(kind, low, high):
                for dest in range(count):
                    sl = slice(dest * each, (dest + 1) * each)
                    put(dest, kind * 2 * each, jnp.concatenate([low[sl], high[sl]], 0))

            w = tn(h_ref[...], dcq_ref[...])
            place(0, w[:h2], w[h2:])
            s = ids_ref[0]
            dc_half = dc_ref[:, lane(s * h2, h2)]
            own, got = tn(own_ref[...], dc_half), tn(got_ref[...], dc_half)
            place(1, jnp.where(s == 0, own, got), jnp.where(s == 0, got, own))
            for kind in range(2):
                cols = slice(kind * h2, (kind + 1) * h2)
                place(2 + kind, acc[:h2, cols], acc[h2:, cols])

    blk = ((per, half, d), lambda c, *_: (c, 0, 0))
    ins = [whole(a) for a in (h, dcq, att_own, att_got, dc)]
    ins += [(a,) + blk for a in (r_own, r_got, g_own, g_got)]
    return call(
        "cross_weights", body, (caps // per,), [ids], ins, [out_whole((count, 8 * each, h2), BF)],
        scratch=[pltpu.VMEM((d, d), F32)], flops=4 * caps * half * d * d,
    )[0]


def pack_vectors(vectors):
    width = sum(v.shape[1] for v in vectors)

    def body(*refs):
        at = 0
        for ref in refs[:-1]:
            refs[-1][:, at : at + ref.shape[1]] = ref[...]
            at += ref.shape[1]

    return call("pack_vectors", body, (1,), [], [whole(v) for v in vectors], [out_whole((1, width), F32)])[0]


def choose_vectors(ids, own, got, d, fh):
    def body(ids_ref, own_ref, got_ref, *outs):
        s = ids_ref[0]
        for layer in range(2):
            pick_one = lambda a, b: jnp.where(s == layer, own_ref[:, a:b], got_ref[:, a:b])
            for i in range(5):
                outs[6 * layer + i][...] = pick_one(i * d, (i + 1) * d)
            low, high = pick_one(5 * d, 5 * d + fh), pick_one(5 * d + fh, 5 * d + 2 * fh)
            outs[6 * layer + 5][...] = jnp.where(s == 0, low, high)

    outs = [out_whole((1, n), F32) for _ in range(2) for n in [d] * 5 + [fh]]
    got = call("choose_vectors", body, (1,), [ids], [whole(own), whole(got)], outs)
    return got[:6], got[6:]


def pack_sums(ids, layers, cross, bup_own, bup_got):
    d, fh = layers[0][0][0].shape[2], bup_own.shape[1]
    arrays = [x[0] for pair in layers for x in pair] + [x[0] for x in cross] + [bup_own, bup_got]
    width = (len(layers) + len(cross)) * d + 2 * fh

    def body(ids_ref, *refs):
        out, s = refs[-1], ids_ref[0]
        total = lambda v: jnp.sum(v, 0, keepdims=True)
        at = 0
        for i, pair in enumerate(layers):
            a, b = [refs[2 * i + k][pair[k][1]] for k in range(2)]
            out[:, at : at + d] = total(jnp.where(s == 0, a, b))
            at += d
        for i, x in enumerate(cross):
            out[:, at : at + d] = total(refs[2 * len(layers) + i][x[1]])
            at += d
        own, got = total(refs[-3][...]), total(refs[-2][...])
        out[:, at : at + fh] = jnp.where(s == 0, own, got)
        out[:, at + fh :] = jnp.where(s == 0, got, own)

    return call("pack_sums", body, (1,), [ids], [whole(a) for a in arrays], [out_whole((1, width), F32)])[0]


def assemble(name, ids, own, got, plans):
    h2 = own[0].shape[1]
    n = len(own)

    def body(ids_ref, *refs):
        s = ids_ref[0]
        mine = refs[0][...] if n == 1 else jnp.where(s == 0, refs[0][...], refs[1][...])
        theirs = refs[n][...]
        sides = jnp.where(s == 0, mine, theirs), jnp.where(s == 0, theirs, mine)
        for out, (size, where) in zip(refs[n + 1 :], plans):
            for side, i, first in where:
                out[:, i * h2 : (i + 1) * h2] = sides[side][first : first + size]

    outs = [out_whole((size, len(where) * h2), F32) for size, where in plans]
    return call(name, body, (1,), [ids], [whole(a) for a in own + [got]], outs)


def plain_sums(s, count, mlp2, cross, attn2, mlp1, image, attn1):
    scatter = lambda g: lax.psum_scatter(g, "dp", scatter_dimension=0, tiled=True)

    def full(act):
        come = swap(act)
        return jnp.concatenate([jnp.where(s == 0, act, come), jnp.where(s == 0, come, act)], 1)

    def side(grad):
        h2 = grad.shape[1] // 2
        return lax.dynamic_slice(grad, (0, s * h2), (grad.shape[0], h2))

    def stacked(w, h2):
        return jnp.concatenate([w[:, i : i + h2] for i in range(0, w.shape[1], h2)], 0)

    def by_section(w):
        parts = w.reshape(2, count, -1, w.shape[1]).swapaxes(0, 1)
        return scatter(parts.reshape(w.shape))

    def mlp(n, du, act, dm):
        return jnp.concatenate(
            [stacked(scatter(tn(n, du)), n.shape[1] // 2), scatter(tn(full(act), side(dm)))], 0
        )

    def attn(h, dqkv, att, da):
        return jnp.concatenate(
            [scatter(tn(h, dqkv[j])) for j in range(3)] + [scatter(tn(full(att), side(da)))], 0
        )

    h, dcq, att, dc = cross
    r_own, r_got, g_own, g_got = [x.reshape(-1, x.shape[-1]) for x in image]
    w_kv = tn(r_own, g_own) + tn(r_got, g_got)
    h2 = dcq.shape[1]
    c = jnp.concatenate([by_section(tn(h, dcq)), by_section(tn(full(att), side(dc)))], 0)
    kv = jnp.concatenate([by_section(w_kv[:, :h2]), by_section(w_kv[:, h2:])], 0)
    return mlp(*mlp2), c, attn(*attn2), mlp(*mlp1), kv, attn(*attn1)


def swap(value):
    return lax.ppermute(value, "section", [(0, 1), (1, 0)])


def on_device(
    text, image, image_counts, cotangent,
    attn_norm_gain, attn_norm_bias, qkv_weight, attn_out_weight, mlp_norm_gain, mlp_norm_bias,
    up_weight, up_bias, down_weight, down_bias,
    cross_norm_gain, cross_norm_bias, cross_query, cross_key_value, cross_out,
):
    s = lax.axis_index("section")
    me = lax.axis_index("dp")
    count = lax.axis_size("dp")
    ids = jnp.stack([s, me]).astype(jnp.int32)
    t, d = text.shape
    h2 = d // 2
    caps, half = image.shape[:2]
    ff = up_bias.shape[1]
    fh = ff // 2
    other = 1 - s

    fast = d // count == 48
    w_qkv, w_out, w_up, w_down = qkv_weight[0], attn_out_weight[0], up_weight[0], down_weight[0]
    vec_own = pack_vectors(
        [attn_norm_gain, attn_norm_bias, mlp_norm_gain, mlp_norm_bias, down_bias, up_bias]
    )
    vec_got = swap(vec_own)
    got_qkv, got_out, got_up, got_down = swap(w_qkv), swap(w_out), swap(w_up), swap(w_down)
    vectors = choose_vectors(ids, vec_own, vec_got, d, fh)
    halves = []
    for layer in range(2):
        halves.append(
            (
                Half(layer, w_qkv, got_qkv, h2),
                Half(layer, w_out, got_out, h2),
                Half(layer, w_up, got_up, fh // 3),
                Half(layer, w_down, got_down, fh // 3),
            )
        )
    gain_i, gain_t = cross_norm_gain[0:1], cross_norm_gain[1:2]
    bias_i, bias_t = cross_norm_bias[0:1], cross_norm_bias[1:2]

    r_own, kv_own, kv_send = key_value(ids, image, gain_i, bias_i, cross_key_value)
    kv_got = swap(kv_send)
    r_got = swap(r_own)

    ag1, ab1, mg1, mb1, bd1, bu1 = vectors[0]
    qw1, ow1, uw1, dw1 = halves[0]
    ag2, ab2, mg2, mb2, bd2, bu2 = vectors[1]
    qw2, ow2, uw2, dw2 = halves[1]

    h1, qkv1, att1, send = self_fwd(0, ids, [text], ag1, ab1, qw1, ow1)
    x1, n1, send = mlp_fwd(0, ids, text, send, swap(send), mg1, mb1, uw1, bu1, dw1, bd1)
    h2n, qkv2, att2, send, z = self_fwd(1, ids, [x1, send, swap(send)], ag2, ab2, qw2, ow2)
    z2, ch, cq, catt, send = cross_fwd(
        ids, image_counts, z, send, swap(send), gain_t, bias_t, cross_query, cross_out, kv_own, kv_got
    )
    act2, du2, dpart, sums_m2, bup2, z3, n2, msend = mlp_grad(
        1, ids, [z2, send, swap(send), cotangent], mg2, mb2, uw2, bu2, dw2, bd2
    )
    turned = [route(s, me, count, turn) for turn in range(3)] if fast else None
    if fast:
        m2 = Sum(up_down_weights(1, turned[0], n2, du2, act2, swap(act2), cotangent, count), count, 0)
        dsend = tie(swap(dpart), m2.outgoing)
    else:
        dsend = swap(dpart)
    dz3, dc, dcq, dkv_own, dkv_send, cpart, sums_n2 = cross_grad(
        ids, image_counts, cotangent, dpart, dsend, z3, mg2, cq, cross_query, cross_out, kv_own, kv_got,
    )
    dkv_mine, csend = swap(dkv_send), swap(cpart)
    if fast:
        ck = cross_weights(
            turned[0], ch, dcq, catt, swap(catt), dc, r_own, r_got, dkv_own, dkv_send, count
        )
        m2.land(ck)
        csend = tie(csend, m2.outgoing)
    dz2, da2, dqkv2, hpart, sums_c = self_grad(
        1, ids, dz3, cpart, csend, z2, gain_t, qkv2, qw2, ow2
    )
    hsend = swap(hpart)
    if fast:
        m2.land(sums_c)
        ca = Sum(
            self_weights(1, turned[0], tie(h2n, m2.outgoing), dqkv2, att2, swap(att2), da2, count, ck), count, 0
        )
        hsend = tie(hsend, ca.outgoing)
    act1, du1, npart, sums_a2, bup1, dz = mlp_grad(
        0, ids, [dz2, hpart, hsend, z, ag2, n1], mg1, mb1, uw1, bu1, dw1, bd1
    )
    nsend = swap(npart)
    bup_got = swap(jnp.where(s == 0, bup2, bup1))
    if fast:
        m1 = Sum(
            up_down_weights(0, turned[0], n1, du1, act1, swap(act1), dz, count), count, 0
        )
        ca.land(m1.outgoing)
        nsend = tie(nsend, ca.outgoing)
    dx1, da1, dqkv1, hpart, sums_n1 = self_grad(
        0, ids, dz, npart, nsend, x1, mg1, qkv1, qw1, ow1
    )
    hsend = swap(hpart)
    if fast:
        m2.land(sums_n1)
        ca.land(sums_n1)
        a1 = Sum(
            self_weights(0, turned[0], tie(h1, ca.outgoing), dqkv1, att1, swap(att1), da1, count), count, 0
        )
        m1.land(a1.outgoing)
        hsend = tie(hsend, m1.outgoing)
    input_grad, sums_a1 = text_grad(ids, dx1, hpart, hsend, text, ag1, dz)
    got = list(key_value_grad(ids, image, gain_i, dkv_own, tie(dkv_mine, sums_a1), cross_key_value))
    if fast:
        for x in (m2, ca, m1, a1):
            x.land(got[1])
        got[1] = tie(got[1], ca.outgoing, m1.outgoing, a1.outgoing)
    image_grad, sums_i = key_value_grad(ids, image, gain_i, dkv_own, dkv_mine, cross_key_value, got)
    bup_own = jnp.where(s == 0, bup1, bup2)
    packed = pack_sums(
        ids,
        [
            [(sums_a1, 0), (sums_a2, 0)], [(sums_a1, 1), (sums_a2, 1)],
            [(sums_n1, 0), (sums_n2, 0)], [(sums_n1, 1), (sums_n2, 1)],
            [(sums_a2, 2), (sums_m2, 2)],
        ],
        [(sums_c, 0), (sums_c, 1), (sums_i, 0), (sums_i, 1)], bup_own, bup_got,
    )
    if fast:
        for x in (m1, a1, ca):
            x.land(sums_i)
        packed = tie(packed, m1.outgoing, a1.outgoing)
        for k in reversed(range(count.bit_length() - 1)):
            packed = packed + lax.ppermute(packed, "dp", [(i, i ^ (1 << k)) for i in range(count)])
            if k == 2:
                a1.land(packed)
                packed = tie(packed, a1.outgoing)
            if k == 1:
                m1.land(packed)
                packed = tie(packed, m1.outgoing)
        finish([m2, ca, m1, a1])
        m2, ca, m1, a1 = [x.result for x in (m2, ca, m1, a1)]
        half_rows = ca.shape[0] // 2
        ckv, a2 = ca[:half_rows], ca[half_rows:]
    else:
        packed = lax.psum(packed, "dp")
        m2, c2, a2, m1, kv, a1 = plain_sums(
            s, count, (n2, du2, act2, cotangent), (ch, dcq, catt, dc), (h2n, dqkv2, att2, da2),
            (n1, du1, act1, dz), (r_own, r_got, dkv_own, dkv_send), (h1, dqkv1, att1, da1),
        )
        ckv = jnp.concatenate([c2, kv], 0)
    y = z3 + msend.astype(F32) + swap(msend).astype(F32)
    layer_out = jnp.where(s == 0, z, y.astype(BF))

    each = d // count
    small = each // 2
    units = fh // h2
    wide = ff // count
    m_got = swap(jnp.where(s == 0, m2, m1))
    a_got = swap(jnp.where(s == 0, a2, a1))
    cross = ckv.reshape(4, 2, small, h2)
    keep = lax.dynamic_index_in_dim(cross, s, 1, False).reshape(4 * small, h2)
    come = swap(lax.dynamic_index_in_dim(cross, other, 1, False).reshape(4 * small, h2))
    pairs = lambda starts: [(side, 2 * i + side, at) for i, at in enumerate(starts) for side in range(2)]
    g_up, g_down = assemble(
        "assemble_mlp", ids, [m1, m2], m_got,
        [
            (each, [(side, side * units + i, i * each) for side in range(2) for i in range(units)]),
            (wide, pairs([units * each])),
        ],
    )
    g_qkv, g_out = assemble(
        "assemble_self", ids, [a1, a2], a_got,
        [(each, pairs([i * each for i in range(3)])), (each, pairs([3 * each]))],
    )
    g_cq, g_co, g_kv = assemble(
        "assemble_cross", ids, [keep], come,
        [(small, pairs([0])), (small, pairs([small])), (small, pairs([2 * small, 3 * small]))],
    )
    image_sums = packed[:, 7 * d : 9 * d]
    image_sums = image_sums + swap(image_sums)
    mine = lambda i: lax.dynamic_slice(packed, (0, i * d + me * each), (1, each))
    at = s * (d // 2) + me * small
    text_part = lambda i: lax.dynamic_slice(packed, (0, (5 + i) * d + at), (1, small))
    image_part = lambda i: lax.dynamic_slice(image_sums, (0, i * d + at), (1, small))
    g_bup = lax.dynamic_slice(packed, (0, 9 * d + me * wide), (1, wide))
    return (
        layer_out[None], input_grad[None], image_grad,
        mine(0), mine(1), g_qkv[None], g_out[None], mine(2), mine(3),
        g_up[None], g_bup, g_down[None], mine(4),
        jnp.concatenate([image_part(0), text_part(0)], 0), jnp.concatenate([image_part(1), text_part(1)], 0),
        g_cq, g_kv, g_co,
    )


def solution(mesh):
    placed = (
        P("dp", None), P("dp", "section", None), P("dp"), P("dp", None),
        P("section", None), P("section", None), P("section", None, None), P("section", None, None),
        P("section", None), P("section", None), P("section", None, None), P("section", None),
        P("section", None, None), P("section", None), P(), P(), P(), P(), P(),
    )
    two, three = P("section", "dp"), P("section", "dp", None)
    last = P(("section", "dp"), None)
    return jax.shard_map(
        on_device,
        mesh=mesh,
        in_specs=placed,
        out_specs=(
            three, three, P("dp", "section", None), two, two, three, three, two, two, three, two,
            three, two, P(None, ("section", "dp")), P(None, ("section", "dp")), last, last, last,
        ),
        check_vma=False,
    )
```

```python
import jax
import jax.numpy as jnp
from jax import lax
from jax.experimental import pallas as pl
from jax.experimental.pallas import tpu as pltpu
from jax.sharding import PartitionSpec as P

HEAD_DIM = 64
SEQ = 64
LANES = 128
CHUNK = 32
ANY = pl.ANY
MT = 256
EPS = 1e-05
NEG = -1e30
SCALE = HEAD_DIM**-0.5
LOG2E = 1.4426950408889634
BF = jnp.bfloat16
F32 = jnp.float32


def nn(a, b):
    return lax.dot_general(a, b, (((1,), (0,)), ((), ())), preferred_element_type=F32)


def nt(a, b):
    return lax.dot_general(a, b, (((1,), (1,)), ((), ())), preferred_element_type=F32)


def tn(a, b):
    return lax.dot_general(a, b, (((0,), (0,)), ((), ())), preferred_element_type=F32)


def normalized(v):
    c = v - jnp.mean(v, -1, keepdims=True)
    inv = lax.rsqrt(jnp.mean(c * c, -1, keepdims=True) + EPS)
    return c * inv, inv


def norm(v, g, b):
    return normalized(v)[0] * g + b


def norm_grad(v, g, dh):
    nh, inv = normalized(v)
    e = dh * g
    dv = (e - jnp.mean(e, -1, keepdims=True) - nh * jnp.mean(e * nh, -1, keepdims=True)) * inv
    return dv, dh * nh


def fold(v):
    return jnp.sum(v.reshape(v.shape[0] // 8, 8, v.shape[1]), 0)


def gelu_pair(u):
    k = 0.7978845608028654
    t = jnp.tanh(k * (u + 0.044715 * u * u * u))
    g = 0.5 * u * (1.0 + t)
    dg = 0.5 * (1.0 + t) + 0.5 * u * (1.0 - t * t) * (k * (1.0 + 3 * 0.044715 * u * u))
    return g, dg


def gelu(u):
    k = 0.7978845608028654
    return 0.5 * u * (1.0 + jnp.tanh(k * (u + 0.044715 * u * u * u)))


def two_heads(v):
    low = lax.broadcasted_iota(jnp.int32, v.shape, 1) < HEAD_DIM
    zero = jnp.zeros_like(v)
    return jnp.concatenate([jnp.where(low, v, zero), jnp.where(low, zero, v)], 0)


def join_heads(v):
    half = v.shape[0] // 2
    low = lax.broadcasted_iota(jnp.int32, (half, LANES), 1) < HEAD_DIM
    return jnp.where(low, v[:half], v[half:])


def key_softmax(scores):
    top = jnp.max(scores[0], 0, keepdims=True)
    for s in scores[1:]:
        top = jnp.maximum(top, jnp.max(s, 0, keepdims=True))
    e = [jnp.exp2((s - top) * (SCALE * LOG2E)) for s in scores]
    scale = 1.0 / sum(jnp.sum(x, 0, keepdims=True) for x in e)
    return [x * scale for x in e]


def causal(s):
    key = lax.broadcasted_iota(jnp.int32, s.shape, 0)
    query = lax.broadcasted_iota(jnp.int32, s.shape, 1) % SEQ
    return jnp.where(key <= query, s, NEG)


def below(s, limit):
    return jnp.where(lax.broadcasted_iota(jnp.int32, s.shape, 0) < limit, s, NEG)


def attend(probs, values):
    return join_heads(sum(tn(p.astype(BF), v) for p, v in zip(probs, values)))


def attend_grad(q2, keys, values, probs, go):
    go2 = two_heads(go)
    dp = [nt(v, go2) for v in values]
    mean = sum(jnp.sum(p * d, 0, keepdims=True) for p, d in zip(probs, dp))
    ds = [(p * (d - mean)).astype(BF) for p, d in zip(probs, dp)]
    dq = join_heads(sum(tn(x, k) for x, k in zip(ds, keys))) * SCALE
    dk = [nn(x, q2) * SCALE for x in ds]
    dv = [nn(p.astype(BF), go2) for p in probs]
    return dq, dk, dv


def loop(count, body, unroll=1):
    def step(i, carry):
        for u in range(unroll):
            body(i * unroll + u)
        return carry

    if count == unroll:
        step(0, 0)
    else:
        lax.fori_loop(0, count // unroll, step, 0)


def rows(i, size):
    start = i * size
    return pl.ds(start if isinstance(start, int) else pl.multiple_of(start, size), size)


def lane(start, size):
    return pl.ds(start if isinstance(start, int) else pl.multiple_of(start, LANES), size)


def call(name, body, grid, scalars, ins, outs, scratch=(), flops=0, alias={}):
    def spec(shape, item):
        block, index = item
        if block is ANY:
            return pl.BlockSpec(memory_space=ANY)
        if block is None:
            block = shape
        if index is None:
            index = lambda *_, n=len(shape): (0,) * n
        return pl.BlockSpec(block, index)

    shapes = [jax.ShapeDtypeStruct(o[0], o[1]) for o in outs]

    def held(shape, dtype, block):
        if block is ANY:
            return 0
        dims = list(shape if block is None else block)
        dims[-2] = max(dims[-2], 8)
        size = jnp.dtype(dtype).itemsize
        for n in dims:
            size *= n
        return 2 * size

    room = 16 << 20
    room += sum(held(a[0].shape, a[0].dtype, a[1]) for a in ins)
    room += sum(held(o[0], o[1], o[2]) for o in outs)
    room += sum(held(x.shape, x.dtype, None) // 2 for x in scratch if len(x.shape) > 1)
    moved = sum(a[0].size * a[0].dtype.itemsize for a in ins)
    moved += sum(s.size * s.dtype.itemsize for s in shapes)
    return pl.pallas_call(
        body,
        name=name,
        out_shape=shapes,
        input_output_aliases=alias,
        grid_spec=pltpu.PrefetchScalarGridSpec(
            num_scalar_prefetch=len(scalars),
            grid=grid,
            in_specs=[spec(a[0].shape, a[1:]) for a in ins],
            out_specs=[spec(o[0], o[2:]) for o in outs],
            scratch_shapes=list(scratch),
        ),
        compiler_params=pltpu.CompilerParams(vmem_limit_bytes=room),
        cost_estimate=pl.CostEstimate(flops=int(flops), bytes_accessed=int(moved), transcendentals=0),
    )(*scalars, *[a[0] for a in ins])


def whole(a):
    return (a, None, None)


def out_whole(shape, dtype):
    return (shape, dtype, None, None)


class Half:
    def __init__(self, layer, own, got, width):
        self.layer, self.own, self.got, self.width = layer, own, got, width

    def cols(self, per):
        layer, width = self.layer, self.width
        d = self.own.shape[0]

        def own_map(j, ids, *_):
            return (0, jnp.where(ids[0] == layer, per(j, ids[0]), 0))

        def got_map(j, ids, *_):
            return (0, jnp.where(ids[0] == layer, 0, per(j, ids[0])))

        return [(self.own, (d, width), own_map), (self.got, (d, width), got_map)]

    def rowblocks(self, per):
        layer, width = self.layer, self.width
        d = self.own.shape[1]

        def own_map(j, ids, *_):
            return (jnp.where(ids[0] == layer, per(j, ids[0]), 0), 0)

        def got_map(j, ids, *_):
            return (jnp.where(ids[0] == layer, 0, per(j, ids[0])), 0)

        return [(self.own, (width, d), own_map), (self.got, (width, d), got_map)]


def pick(ids, layer, own_ref, got_ref):
    return jnp.where(ids[0] == layer, own_ref[...], got_ref[...])


def self_fwd(layer, ids, stream, gain, bias, wqkv, wout):
    first = len(stream) == 1
    t, d = stream[0].shape
    h2 = d // 2
    n_in = len(stream)

    def body(ids_ref, *refs):
        xs, refs = refs[:n_in], refs[n_in:]
        g_ref, b_ref, own, got, o_own, o_got = refs[:6]
        outs = refs[6:]
        h_ref, qkv_ref, att_ref, send_ref = outs[:4]
        j = pl.program_id(0)

        @pl.when(j == 0)
        def _():
            def chunk(i):
                sl = rows(i, CHUNK)
                if first:
                    x = xs[0][sl, :].astype(F32)
                else:
                    z = (xs[0][sl, :] + xs[1][sl, :].astype(F32) + xs[2][sl, :].astype(F32)).astype(BF)
                    outs[4][sl, :] = z
                    x = z.astype(F32)
                h_ref[sl, :] = norm(x, g_ref[...], b_ref[...]).astype(BF)

            loop(t // CHUNK, chunk, 4)

        w = pick(ids_ref, layer, own, got)

        qkv_ref[j] = nn(h_ref[...], w).astype(BF)

        @pl.when(j == 2)
        def _():
            def block(i):
                units = [
                    (rows(2 * i + c, SEQ), slice(p * LANES, (p + 1) * LANES))
                    for c in range(2) for p in range(h2 // LANES)
                ]
                loaded = [[qkv_ref[m, sl, ln] for m in range(3)] for sl, ln in units]
                scores = [causal(nt(k, two_heads(q))) for q, k, v in loaded]
                probs = [key_softmax([s]) for s in scores]
                done = [attend(p, [x[2]]) for p, x in zip(probs, loaded)]
                for (sl, ln), o in zip(units, done):
                    att_ref[sl, ln] = o.astype(BF)

            loop(t // (2 * SEQ), block)
            wo = pick(ids_ref, layer, o_own, o_got)
            send_ref[...] = nn(att_ref[...], wo).astype(BF)

    outs = [
        out_whole((t, d), BF),
        out_whole((3, t, h2), BF),
        out_whole((t, h2), BF),
        out_whole((t, d), BF),
    ]
    if not first:
        outs.append(out_whole((t, d), BF))
    ins = [whole(x) for x in stream] + [whole(gain), whole(bias)]
    ins += wqkv.cols(lambda j, s: 2 * j + s) + wout.rowblocks(lambda j, s: s)
    return call(
        f"self_fwd_{layer}", body, (3,), [ids], ins, outs, flops=2 * t * d * 4 * h2 + 2e8
    )


def mlp_fwd(layer, ids, x, a_own, a_got, gain, bias, wup, b_up, wdown, b_down):
    t, d = x.shape
    fh = b_up.shape[1]
    width = wup.width

    def body(ids_ref, x_ref, p_ref, q_ref, g_ref, b_ref, u_own, u_got, bu_ref, d_own, d_got, bd_ref,
             x1_ref, n_ref, send_ref, part_ref):
        j = pl.program_id(0)

        @pl.when(j == 0)
        def _():
            def chunk(i):
                sl = rows(i, CHUNK)
                x1 = x_ref[sl, :].astype(F32) + p_ref[sl, :].astype(F32) + q_ref[sl, :].astype(F32)
                x1_ref[sl, :] = x1
                n_ref[sl, :] = norm(x1, g_ref[...], b_ref[...]).astype(BF)
                part_ref[sl, :] = jnp.broadcast_to(
                    jnp.where(ids_ref[0] == 0, bd_ref[...], 0.0), (CHUNK, d)
                )

            loop(t // CHUNK, chunk, 4)

        up = pick(ids_ref, layer, u_own, u_got)
        down = pick(ids_ref, layer, d_own, d_got)

        def tile(i):
            sl = rows(i, MT)
            u = nn(n_ref[sl, :], up) + bu_ref[...]
            part_ref[sl, :] += nn(gelu(u).astype(BF), down)

        loop(t // MT, tile, t // MT)

        @pl.when(j == pl.num_programs(0) - 1)
        def _():
            def chunk(i):
                sl = rows(i, CHUNK)
                send_ref[sl, :] = part_ref[sl, :].astype(BF)

            loop(t // CHUNK, chunk, 4)

    per = fh // width
    ins = [whole(x), whole(a_own), whole(a_got), whole(gain), whole(bias)]
    ins += wup.cols(lambda j, s: s * per + j)
    ins += [(b_up, (1, width), lambda j, *_: (0, j))]
    ins += wdown.rowblocks(lambda j, s: s * per + j)
    ins += [whole(b_down)]
    outs = [out_whole((t, d), F32), out_whole((t, d), BF), out_whole((t, d), BF)]
    return call(
        f"mlp_fwd_{layer}", body, (per,), [ids], ins, outs, scratch=[pltpu.VMEM((t, d), F32)],
        flops=4 * t * d * fh,
    )


def mlp_grad(layer, ids, lead, gain, bias, wup, b_up, wdown, b_down):
    second = layer == 1
    t, d = lead[0].shape
    fh = b_up.shape[1]
    width = wup.width
    n_in = len(lead)

    def body(ids_ref, *refs):
        lead_refs, refs = refs[:n_in], refs[n_in:]
        g_ref, b_ref, u_own, u_got, bu_ref, d_own, d_got, bd_ref = refs[:8]
        outs, scr = refs[8 : 16 if second else 14], refs[16 if second else 14 :]
        act_ref, du_ref, dsend_ref, sums_ref, bup_ref = outs[:5]
        extra, dn_ref = outs[5:], scr[0]
        j = pl.program_id(0)

        @pl.when(j == 0)
        def _():
            sums_ref[...] = jnp.zeros_like(sums_ref)

            def chunk(i):
                sl = rows(i, CHUNK)
                if second:
                    x_ref, p_ref, q_ref, cot_ref = lead_refs
                    x = x_ref[sl, :] + p_ref[sl, :].astype(F32) + q_ref[sl, :].astype(F32)
                    extra[0][sl, :] = x
                    extra[1][sl, :] = norm(x, g_ref[...], b_ref[...]).astype(BF)
                    scr[1][sl, :] = jnp.broadcast_to(
                        jnp.where(ids_ref[0] == 0, bd_ref[...], 0.0), (CHUNK, d)
                    )
                    sums_ref[2] += fold(cot_ref[sl, :].astype(F32))
                else:
                    grad_ref, p_ref, q_ref, z_ref, zg_ref, n_ref = lead_refs
                    dh = p_ref[sl, :].astype(F32) + q_ref[sl, :].astype(F32)
                    dv, dhn = norm_grad(z_ref[sl, :].astype(F32), zg_ref[...], dh)
                    dz = (grad_ref[sl, :] + dv).astype(BF)
                    extra[0][sl, :] = dz
                    sums_ref[0] += fold(dhn)
                    sums_ref[1] += fold(dh)
                    sums_ref[2] += fold(dz.astype(F32))
                dn_ref[sl, :] = jnp.zeros((CHUNK, d), F32)

            loop(t // CHUNK, chunk, 4)

        up = pick(ids_ref, layer, u_own, u_got)
        down = pick(ids_ref, layer, d_own, d_got)
        bup_ref[...] = jnp.zeros_like(bup_ref)
        n_src = extra[1] if second else lead_refs[5]
        dm_src = lead_refs[3] if second else extra[0]

        def tile(i):
            sl = rows(i, MT)
            u = nn(n_src[sl, :], up) + bu_ref[...]
            g, dg = gelu_pair(u)
            g = g.astype(BF)
            act_ref[sl, :] = g
            du = (nt(dm_src[sl, :], down) * dg).astype(BF)
            du_ref[sl, :] = du
            bup_ref[...] += fold(du.astype(F32))
            dn_ref[sl, :] += nt(du, up)
            if second:
                scr[1][sl, :] += nn(g, down)

        loop(t // MT, tile, t // MT)

        @pl.when(j == pl.num_programs(0) - 1)
        def _():
            def chunk(i):
                sl = rows(i, CHUNK)
                dsend_ref[sl, :] = dn_ref[sl, :].astype(BF)
                if second:
                    extra[2][sl, :] = scr[1][sl, :].astype(BF)

            loop(t // CHUNK, chunk, 4)

    per = fh // width
    ins = [whole(a) for a in lead] + [whole(gain), whole(bias)]
    ins += wup.cols(lambda j, s: s * per + j)
    ins += [(b_up, (1, width), lambda j, *_: (0, j))]
    ins += wdown.rowblocks(lambda j, s: s * per + j)
    ins += [whole(b_down)]
    outs = [
        ((t, fh), BF, (t, width), lambda j, *_: (0, j)),
        ((t, fh), BF, (t, width), lambda j, *_: (0, j)),
        out_whole((t, d), BF),
        out_whole((3, 8, d), F32),
        ((8, fh), F32, (8, width), lambda j, *_: (0, j)),
    ]
    if second:
        outs += [out_whole((t, d), F32), out_whole((t, d), BF), out_whole((t, d), BF)]
    else:
        outs += [out_whole((t, d), BF)]
    return call(
        f"mlp_grad_{layer}", body, (per,), [ids], ins, outs,
        scratch=[pltpu.VMEM((t, d), F32)] * (2 if second else 1),
        flops=(8 if second else 6) * t * d * fh,
    )


def key_value(ids, image, gain, bias, w):
    caps, half, d = image.shape
    h2 = d // 2
    per = 2

    def body(ids_ref, im_ref, g_ref, b_ref, w_ref, r_ref, own_ref, oth_ref):
        for c in range(per):

            def chunk(i, c=c):
                sl = rows(i, 32)
                r_ref[c, sl, :] = norm(im_ref[c, sl, :].astype(F32), g_ref[...], b_ref[...]).astype(BF)

            loop(half // 32, chunk, 3)
        r = r_ref[...].reshape(per * half, d)
        first = ids_ref[0] == 0
        for i in range(2):
            x = nn(r, w_ref[:, i * d : (i + 1) * d]).astype(BF).reshape(per, half, d)
            low, high = x[:, :, :h2], x[:, :, h2:]
            own_ref[:, :, i * h2 : (i + 1) * h2] = jnp.where(first, low, high)
            oth_ref[:, :, i * h2 : (i + 1) * h2] = jnp.where(first, high, low)

    blk = ((per, half, d), lambda c, *_: (c, 0, 0))
    ins = [(image,) + blk, whole(gain), whole(bias), whole(w)]
    outs = [((caps, half, d), BF) + blk] * 3
    return call("key_value", body, (caps // per,), [ids], ins, outs, flops=4 * caps * half * d * d)


def key_value_grad(ids, image, gain, g_own, g_oth, w, before=None):
    caps, half, d = image.shape
    h2 = d // 2
    per = 2
    steps = caps // per // 2
    first_step = 0 if before is None else steps

    def body(ids_ref, im_ref, g_ref, own_ref, oth_ref, w_ref, *refs):
        dx_ref, sums_ref, dr_ref = refs[-3:]

        @pl.when(pl.program_id(0) == 0)
        def _():
            sums_ref[...] = jnp.zeros_like(sums_ref) if before is None else refs[1][...]

        own = own_ref[...].reshape(per * half, d)
        oth = oth_ref[...].reshape(per * half, d)
        first = ids_ref[0] == 0
        low, high = jnp.where(first, own, oth), jnp.where(first, oth, own)
        g = [x[:, i * h2 : (i + 1) * h2] for i in range(2) for x in (low, high)]
        dr_ref[...] = nt(jnp.concatenate(g, 1), w_ref[...]).reshape(per, half, d)
        for c in range(per):

            def chunk(i, c=c):
                sl = rows(i, 32)
                dr = dr_ref[c, sl, :]
                dv, dhn = norm_grad(im_ref[c, sl, :].astype(F32), g_ref[...], dr)
                dx_ref[c, sl, :] = dv
                sums_ref[0] += fold(dhn)
                sums_ref[1] += fold(dr)

            loop(half // 32, chunk, 3)

    blk = ((per, half, d), lambda c, *_: (c + first_step, 0, 0))
    ins = [(image,) + blk, whole(gain), (g_own,) + blk, (g_oth,) + blk, whole(w)]
    alias = {}
    if before is not None:
        ins += [(before[0], ANY, None), whole(before[1])]
        alias = {6: 0}
    outs = [((caps, half, d), F32) + blk, out_whole((2, 8, d), F32)]
    return call(
        "key_value_grad", body, (steps,), [ids], ins, outs, alias=alias,
        scratch=[pltpu.VMEM((per, half, d), F32)], flops=2 * caps * half * d * d,
    )


def patch_limits(ids_ref, counts_ref, c, half):
    s = ids_ref[0]
    return counts_ref[c] - s * half, counts_ref[c] - (1 - s) * half


def cross_fwd(ids, counts, z, a_own, a_got, gain, bias, wq, wco, kv_own, kv_got):
    caps, half, d = kv_own.shape
    h2 = d // 2
    t = z.shape[0]

    def body(ids_ref, cnt_ref, z_ref, p_ref, q_ref, g_ref, b_ref, wq_ref, wo_ref, own_ref, got_ref,
             z2_ref, h_ref, cq_ref, att_ref, send_ref):
        c = pl.program_id(0)

        @pl.when(c == 0)
        def _():
            def chunk(i):
                sl = rows(i, CHUNK)
                x = z_ref[sl, :].astype(F32) + p_ref[sl, :].astype(F32) + q_ref[sl, :].astype(F32)
                z2_ref[sl, :] = x
                h_ref[sl, :] = norm(x, g_ref[...], b_ref[...]).astype(BF)

            loop(t // CHUNK, chunk, 4)

            cq_ref[...] = nn(h_ref[...], wq_ref[...]).astype(BF)

        limits = patch_limits(ids_ref, cnt_ref, c, half)
        sl = rows(c, SEQ)
        sides = (own_ref, got_ref)
        pairs = h2 // LANES

        def scored(p):
            ln = slice(p * LANES, (p + 1) * LANES)
            q2 = two_heads(cq_ref[sl, ln])
            return [below(nt(ref[0, :, ln], q2), limit) for ref, limit in zip(sides, limits)]

        ahead = scored(0)
        for p in range(pairs):
            scores, ahead = ahead, scored(p + 1) if p + 1 < pairs else None
            lv = slice(h2 + p * LANES, h2 + (p + 1) * LANES)
            out = attend(key_softmax(scores), [ref[0, :, lv] for ref in sides])
            att_ref[sl, p * LANES : (p + 1) * LANES] = out.astype(BF)

        @pl.when(c == pl.num_programs(0) - 1)
        def _():
            send_ref[...] = nn(att_ref[...], wo_ref[...]).astype(BF)

    blk = ((1, half, d), lambda c, *_: (c, 0, 0))
    ins = [whole(z), whole(a_own), whole(a_got), whole(gain), whole(bias)]
    ins += [(wq, (d, h2), lambda c, ids, *_: (0, ids[0])), (wco, (h2, d), lambda c, ids, *_: (ids[0], 0))]
    ins += [(kv_own,) + blk, (kv_got,) + blk]
    outs = [
        out_whole((t, d), F32),
        out_whole((t, d), BF),
        out_whole((t, h2), BF),
        out_whole((t, h2), BF),
        out_whole((t, d), BF),
    ]
    return call(
        "cross_fwd", body, (caps,), [ids, counts], ins, outs, flops=4 * t * d * h2 + 16e8
    )


def cross_grad(ids, counts, grad, n_own, n_got, x3, gain3, cq, wq, wco, kv_own, kv_got):
    caps, half, d = kv_own.shape
    h2 = d // 2
    t = x3.shape[0]

    def body(ids_ref, cnt_ref, gr_ref, p_ref, q_ref, x_ref, g_ref, cq_ref, wq_ref, wo_ref, own_ref, got_ref,
             dz_ref, dc_ref, dcq_ref, down_ref, dgot_ref, dsend_ref, sums_ref, da_ref):
        c = pl.program_id(0)

        @pl.when(c == 0)
        def _():
            sums_ref[...] = jnp.zeros_like(sums_ref)

            def chunk(i):
                sl = rows(i, CHUNK)
                dh = p_ref[sl, :].astype(F32) + q_ref[sl, :].astype(F32)
                dv, dhn = norm_grad(x_ref[sl, :], g_ref[...], dh)
                dz = gr_ref[sl, :].astype(F32) + dv
                dz_ref[sl, :] = dz
                dc_ref[sl, :] = dz.astype(BF)
                sums_ref[0] += fold(dhn)
                sums_ref[1] += fold(dh)

            loop(t // CHUNK, chunk, 4)

            da_ref[...] = nt(dc_ref[...], wo_ref[...]).astype(BF)

        limits = patch_limits(ids_ref, cnt_ref, c, half)
        sl = rows(c, SEQ)
        sides = (own_ref, got_ref)
        pairs = h2 // LANES

        def scored(p):
            ln = slice(p * LANES, (p + 1) * LANES)
            keys = [ref[0, :, ln] for ref in sides]
            q2 = two_heads(cq_ref[sl, ln])
            return q2, keys, [below(nt(k, q2), limit) for k, limit in zip(keys, limits)]

        ahead = scored(0)
        for p in range(pairs):
            ln = slice(p * LANES, (p + 1) * LANES)
            lv = slice(h2 + p * LANES, h2 + (p + 1) * LANES)
            (q2, keys, scores), ahead = ahead, scored(p + 1) if p + 1 < pairs else None
            values = [ref[0, :, lv] for ref in sides]
            dq, dk, dv = attend_grad(q2, keys, values, key_softmax(scores), da_ref[sl, ln])
            dcq_ref[sl, ln] = dq.astype(BF)
            for out, a, b in zip((down_ref, dgot_ref), dk, dv):
                out[0, :, ln] = a.astype(BF)
                out[0, :, lv] = b.astype(BF)

        @pl.when(c == pl.num_programs(0) - 1)
        def _():
            dsend_ref[...] = nt(dcq_ref[...], wq_ref[...]).astype(BF)

    blk = ((1, half, d), lambda c, *_: (c, 0, 0))
    ins = [whole(grad), whole(n_own), whole(n_got), whole(x3), whole(gain3), whole(cq)]
    ins += [(wq, (d, h2), lambda c, ids, *_: (0, ids[0])), (wco, (h2, d), lambda c, ids, *_: (ids[0], 0))]
    ins += [(kv_own,) + blk, (kv_got,) + blk]
    outs = [
        out_whole((t, d), F32),
        out_whole((t, d), BF),
        out_whole((t, h2), BF),
        ((caps, half, d), BF) + blk,
        ((caps, half, d), BF) + blk,
        out_whole((t, d), BF),
        out_whole((2, 8, d), F32),
    ]
    return call(
        "cross_grad", body, (caps,), [ids, counts], ins, outs,
        scratch=[pltpu.VMEM((t, h2), BF)], flops=4 * t * d * h2 + 5e9,
    )


def self_grad(layer, ids, grad, h_own, h_got, x, gain_x, qkv, wqkv, wout):
    t, d = x.shape
    h2 = d // 2

    def body(ids_ref, gr_ref, p_ref, q_ref, x_ref, g_ref, qkv_ref, own, got, o_own, o_got,
             dz_ref, da_ref, dqkv_ref, dsend_ref, sums_ref, datt_ref, dh_ref):
        j = pl.program_id(0)

        @pl.when(j == 0)
        def _():
            sums_ref[...] = jnp.zeros_like(sums_ref)

            def chunk(i):
                sl = rows(i, CHUNK)
                dh = p_ref[sl, :].astype(F32) + q_ref[sl, :].astype(F32)
                dv, dhn = norm_grad(x_ref[sl, :].astype(F32), g_ref[...], dh)
                dz = gr_ref[sl, :].astype(F32) + dv
                dz_ref[sl, :] = dz
                da_ref[sl, :] = dz.astype(BF)
                sums_ref[0] += fold(dhn)
                sums_ref[1] += fold(dh)

            loop(t // CHUNK, chunk, 4)
            wo = pick(ids_ref, layer, o_own, o_got)

            datt_ref[...] = nt(da_ref[...], wo).astype(BF)

            def block(i):
                units = [
                    (rows(2 * i + c, SEQ), slice(p * LANES, (p + 1) * LANES))
                    for c in range(2) for p in range(h2 // LANES)
                ]
                loaded = [[qkv_ref[m, sl, ln] for m in range(3)] + [datt_ref[sl, ln]] for sl, ln in units]
                done = []
                for q, k, v, go in loaded:
                    q2 = two_heads(q)
                    probs = key_softmax([causal(nt(k, q2))])
                    dq, dk, dv = attend_grad(q2, [k], [v], probs, go)
                    done.append((dq, dk[0], dv[0]))
                for (sl, ln), grads in zip(units, done):
                    for m in range(3):
                        dqkv_ref[m, sl, ln] = grads[m].astype(BF)

            loop(t // (2 * SEQ), block)

        w = pick(ids_ref, layer, own, got)
        part = nt(dqkv_ref[j], w)

        @pl.when(j == 0)
        def _():
            dh_ref[...] = part

        @pl.when(j == 1)
        def _():
            dh_ref[...] += part

        @pl.when(j == 2)
        def _():
            dsend_ref[...] = (dh_ref[...] + part).astype(BF)

    ins = [whole(grad), whole(h_own), whole(h_got), whole(x), whole(gain_x), whole(qkv)]
    ins += wqkv.cols(lambda j, s: 2 * j + s) + wout.rowblocks(lambda j, s: s)
    outs = [
        out_whole((t, d), F32),
        out_whole((t, d), BF),
        out_whole((3, t, h2), BF),
        out_whole((t, d), BF),
        out_whole((2, 8, d), F32),
    ]
    return call(
        f"self_grad_{layer}", body, (3,), [ids], ins, outs,
        scratch=[pltpu.VMEM((t, h2), BF), pltpu.VMEM((t, d), F32)], flops=2 * t * d * 4 * h2 + 5e8,
    )


def text_grad(ids, grad, h_own, h_got, x, gain, dz):
    t, d = x.shape

    def body(ids_ref, gr_ref, p_ref, q_ref, x_ref, g_ref, dz_ref, dx_ref, sums_ref):
        sums_ref[...] = jnp.zeros_like(sums_ref)

        def chunk(i):
            sl = rows(i, CHUNK)
            dh = p_ref[sl, :].astype(F32) + q_ref[sl, :].astype(F32)
            dv, dhn = norm_grad(x_ref[sl, :].astype(F32), g_ref[...], dh)
            dx_ref[sl, :] = jnp.where(ids_ref[0] == 0, gr_ref[sl, :] + dv, dz_ref[sl, :].astype(F32))
            sums_ref[0] += fold(dhn)
            sums_ref[1] += fold(dh)

        loop(t // CHUNK, chunk, 4)

    ins = [whole(a) for a in (grad, h_own, h_got, x, gain, dz)]
    outs = [out_whole((t, d), F32), out_whole((2, 8, d), F32)]
    return call("text_grad", body, (1,), [ids], ins, outs)


def paths(count, turn):
    bits = list(range(count.bit_length() - 1))
    near, far = bits[:3], bits[3:]
    return [near[k % 3 :] + near[: k % 3] + far for k in (turn, turn + 1)]


def route(s, me, count, turn):
    first, second = paths(count, turn)
    bits = [jnp.where(s == 0, a, b) for a, b in zip(first, second)]
    return jnp.stack([s, me] + bits).astype(jnp.int32)


def tie(value, *after):
    return lax.optimization_barrier((value, *after))[0]


class Sum:
    def __init__(self, parts, count, turn):
        self.parts, self.count, self.paths = parts, count, paths(count, turn)
        self.arrived, self.result = [], None
        self.send(parts[0])

    def send(self, value):
        self.outgoing = value
        step, n = len(self.arrived), self.count
        perm = [(s * n + i, s * n + (i ^ (1 << self.paths[s][step]))) for s in range(2) for i in range(n)]
        self.flight = lax.ppermute(value, ("section", "dp"), perm)

    def land(self, *after):
        if self.result is not None:
            return
        self.arrived.append(tie(self.flight, *after) if after else self.flight)
        step = len(self.arrived)
        low = self.count >> (step + 1)
        high = max(2 * low, 1)
        total = self.parts[step].astype(F32)
        for a in self.arrived:
            total = total + a[low:high].astype(F32)
        if step < len(self.parts) - 1:
            self.send(total.astype(self.parts[0].dtype))
        else:
            self.result = self.outgoing = total[0]


def finish(sums):
    while any(x.result is None for x in sums):
        for x in sums:
            x.land()


def slots(outs, scr, sems):
    copies, high = [], scr.shape[0]
    for i, out in enumerate(outs):
        low = high // 2 if i < len(outs) - 1 else 0
        copies.append(pltpu.make_async_copy(scr.at[low:high], out, sems.at[i]))
        high = low
    for c in copies:
        c.start()
    for c in copies:
        c.wait()


def putter(ids_ref, scr):
    def put(dest, first, block):
        rel, slot = dest ^ ids_ref[1], 0
        for k in range(scr.shape[0].bit_length() - 1):
            slot = slot * 2 + ((rel >> ids_ref[2 + k]) & 1)
        scr[slot, pl.ds(first, block.shape[0]), :] = block.astype(scr.dtype)

    return put


def slot_outs(count, row_count, cols):
    steps = count.bit_length() - 1
    sizes = [count >> k for k in range(1, steps + 1)] + [1]
    return [((n, row_count, cols), BF, ANY, None) for n in sizes]


def slot_scratch(count, row_count, cols):
    return [pltpu.VMEM((count, row_count, cols), BF), pltpu.SemaphoreType.DMA((count.bit_length(),))]


def up_down_weights(layer, ids, normed, du, act_own, act_got, dm, count):
    t, d = normed.shape
    fh = du.shape[1]
    h2 = d // 2
    up_rows, down_rows = d // count, 2 * fh // count
    units = fh // h2
    per = h2 // down_rows
    row_count = units * up_rows + down_rows

    def body(ids_ref, n_ref, du_ref, own_ref, got_ref, dm_ref, *refs):
        outs, (scr, sems, turned) = refs[:-3], refs[-3:]
        j = pl.program_id(0)
        put = putter(ids_ref, scr)

        @pl.when(j == 0)
        def _():
            turned[...] = n_ref[...].T

        w = nn(turned[...], du_ref[...])
        for dest in range(count):
            put(dest, pl.multiple_of(j * up_rows, up_rows), w[dest * up_rows : (dest + 1) * up_rows])
        s = ids_ref[0]
        dm_half = dm_ref[:, lane(s * h2, h2)]
        for ref, side in ((own_ref, s), (got_ref, 1 - s)):
            w = tn(ref[...], dm_half)
            for i in range(per):
                put(
                    side * (count // 2) + j * per + i, units * up_rows,
                    w[i * down_rows : (i + 1) * down_rows],
                )

        @pl.when(j == units - 1)
        def _():
            slots(outs, scr, sems)

    block = ((t, h2), lambda j, *_: (0, j))
    ins = [whole(normed), (du,) + block, (act_own,) + block, (act_got,) + block, whole(dm)]
    return call(
        f"mlp_weights_{layer}", body, (units,), [ids], ins, slot_outs(count, row_count, h2),
        scratch=slot_scratch(count, row_count, h2) + [pltpu.VMEM((d, t), BF)], flops=4 * t * d * fh,
    )


def self_weights(layer, ids, h, dqkv, att_own, att_got, da, count, before=None):
    t, d = h.shape
    h2 = d // 2
    each = d // count
    first = 0 if before is None else before.shape[1]
    row_count = first + 4 * each

    def body(ids_ref, h_ref, dqkv_ref, own_ref, got_ref, da_ref, *refs):
        (scr, sems, turned), refs = refs[-3:], refs[:-3]
        outs = refs if before is None else refs[1:]
        j = pl.program_id(0)
        put = putter(ids_ref, scr)

        @pl.when(j == 0)
        def _():
            turned[...] = h_ref[...].T
            if before is not None:

                def copy(i):
                    scr[i, :first] = refs[0][i]

                loop(count, copy)

        w = nn(turned[...], dqkv_ref[0])
        at = pl.multiple_of(first + j * each, each)
        for dest in range(count):
            put(dest, at, w[dest * each : (dest + 1) * each])

        @pl.when(j == 2)
        def _():
            s = ids_ref[0]
            da_half = da_ref[:, lane(s * h2, h2)]
            for ref, side in ((own_ref, s), (got_ref, 1 - s)):
                w = tn(ref[...], da_half)
                for i in range(count // 2):
                    put(side * (count // 2) + i, first + 3 * each, w[i * each : (i + 1) * each])
            slots(outs, scr, sems)

    ins = [whole(h), (dqkv, (1, t, h2), lambda j, *_: (j, 0, 0))] + [whole(a) for a in (att_own, att_got, da)]
    if before is not None:
        ins.append(whole(before))
    return call(
        f"self_weights_{layer}", body, (3,), [ids], ins, slot_outs(count, row_count, h2),
        scratch=slot_scratch(count, row_count, h2) + [pltpu.VMEM((d, t), BF)], flops=8 * t * d * h2,
    )


def cross_weights(ids, h, dcq, att_own, att_got, dc, r_own, r_got, g_own, g_got, count):
    caps, half, d = r_own.shape
    h2 = d // 2
    each = h2 // count
    per = 2

    def body(ids_ref, h_ref, dcq_ref, own_ref, got_ref, dc_ref, ro, rg, go, gg, out, acc):
        c = pl.program_id(0)
        flat = lambda ref: ref[...].reshape(per * half, d)
        step = tn(
            jnp.concatenate([flat(ro), flat(rg)], 0), jnp.concatenate([flat(go), flat(gg)], 0)
        )

        @pl.when(c == 0)
        def _():
            acc[...] = step

        @pl.when(c > 0)
        def _():
            acc[...] += step

        @pl.when(c == pl.num_programs(0) - 1)
        def _():
            put = putter(ids_ref, out)

            def place(kind, low, high):
                for dest in range(count):
                    sl = slice(dest * each, (dest + 1) * each)
                    put(dest, kind * 2 * each, jnp.concatenate([low[sl], high[sl]], 0))

            w = tn(h_ref[...], dcq_ref[...])
            place(0, w[:h2], w[h2:])
            s = ids_ref[0]
            dc_half = dc_ref[:, lane(s * h2, h2)]
            own, got = tn(own_ref[...], dc_half), tn(got_ref[...], dc_half)
            place(1, jnp.where(s == 0, own, got), jnp.where(s == 0, got, own))
            for kind in range(2):
                cols = slice(kind * h2, (kind + 1) * h2)
                place(2 + kind, acc[:h2, cols], acc[h2:, cols])

    blk = ((per, half, d), lambda c, *_: (c, 0, 0))
    ins = [whole(a) for a in (h, dcq, att_own, att_got, dc)]
    ins += [(a,) + blk for a in (r_own, r_got, g_own, g_got)]
    return call(
        "cross_weights", body, (caps // per,), [ids], ins, [out_whole((count, 8 * each, h2), BF)],
        scratch=[pltpu.VMEM((d, d), F32)], flops=4 * caps * half * d * d,
    )[0]


def pack_vectors(vectors):
    width = sum(v.shape[1] for v in vectors)

    def body(*refs):
        at = 0
        for ref in refs[:-1]:
            refs[-1][:, at : at + ref.shape[1]] = ref[...]
            at += ref.shape[1]

    return call("pack_vectors", body, (1,), [], [whole(v) for v in vectors], [out_whole((1, width), F32)])[0]


def choose_vectors(ids, own, got, d, fh):
    def body(ids_ref, own_ref, got_ref, *outs):
        s = ids_ref[0]
        for layer in range(2):
            pick_one = lambda a, b: jnp.where(s == layer, own_ref[:, a:b], got_ref[:, a:b])
            for i in range(5):
                outs[6 * layer + i][...] = pick_one(i * d, (i + 1) * d)
            low, high = pick_one(5 * d, 5 * d + fh), pick_one(5 * d + fh, 5 * d + 2 * fh)
            outs[6 * layer + 5][...] = jnp.where(s == 0, low, high)

    outs = [out_whole((1, n), F32) for _ in range(2) for n in [d] * 5 + [fh]]
    got = call("choose_vectors", body, (1,), [ids], [whole(own), whole(got)], outs)
    return got[:6], got[6:]


def pack_sums(ids, layers, cross, bup_own, bup_got):
    d, fh = layers[0][0][0].shape[2], bup_own.shape[1]
    arrays = [x[0] for pair in layers for x in pair] + [x[0] for x in cross] + [bup_own, bup_got]
    width = (len(layers) + len(cross)) * d + 2 * fh

    def body(ids_ref, *refs):
        out, s = refs[-1], ids_ref[0]
        total = lambda v: jnp.sum(v, 0, keepdims=True)
        at = 0
        for i, pair in enumerate(layers):
            a, b = [refs[2 * i + k][pair[k][1]] for k in range(2)]
            out[:, at : at + d] = total(jnp.where(s == 0, a, b))
            at += d
        for i, x in enumerate(cross):
            out[:, at : at + d] = total(refs[2 * len(layers) + i][x[1]])
            at += d
        own, got = total(refs[-3][...]), total(refs[-2][...])
        out[:, at : at + fh] = jnp.where(s == 0, own, got)
        out[:, at + fh :] = jnp.where(s == 0, got, own)

    return call("pack_sums", body, (1,), [ids], [whole(a) for a in arrays], [out_whole((1, width), F32)])[0]


def assemble(name, ids, own, got, plans):
    h2 = own[0].shape[1]
    n = len(own)

    def body(ids_ref, *refs):
        s = ids_ref[0]
        mine = refs[0][...] if n == 1 else jnp.where(s == 0, refs[0][...], refs[1][...])
        theirs = refs[n][...]
        sides = jnp.where(s == 0, mine, theirs), jnp.where(s == 0, theirs, mine)
        for out, (size, where) in zip(refs[n + 1 :], plans):
            for side, i, first in where:
                out[:, i * h2 : (i + 1) * h2] = sides[side][first : first + size]

    outs = [out_whole((size, len(where) * h2), F32) for size, where in plans]
    return call(name, body, (1,), [ids], [whole(a) for a in own + [got]], outs)


def plain_sums(s, count, mlp2, cross, attn2, mlp1, image, attn1):
    scatter = lambda g: lax.psum_scatter(g, "dp", scatter_dimension=0, tiled=True)

    def full(act):
        come = swap(act)
        return jnp.concatenate([jnp.where(s == 0, act, come), jnp.where(s == 0, come, act)], 1)

    def side(grad):
        h2 = grad.shape[1] // 2
        return lax.dynamic_slice(grad, (0, s * h2), (grad.shape[0], h2))

    def stacked(w, h2):
        return jnp.concatenate([w[:, i : i + h2] for i in range(0, w.shape[1], h2)], 0)

    def by_section(w):
        parts = w.reshape(2, count, -1, w.shape[1]).swapaxes(0, 1)
        return scatter(parts.reshape(w.shape))

    def mlp(n, du, act, dm):
        return jnp.concatenate(
            [stacked(scatter(tn(n, du)), n.shape[1] // 2), scatter(tn(full(act), side(dm)))], 0
        )

    def attn(h, dqkv, att, da):
        return jnp.concatenate(
            [scatter(tn(h, dqkv[j])) for j in range(3)] + [scatter(tn(full(att), side(da)))], 0
        )

    h, dcq, att, dc = cross
    r_own, r_got, g_own, g_got = [x.reshape(-1, x.shape[-1]) for x in image]
    w_kv = tn(r_own, g_own) + tn(r_got, g_got)
    h2 = dcq.shape[1]
    c = jnp.concatenate([by_section(tn(h, dcq)), by_section(tn(full(att), side(dc)))], 0)
    kv = jnp.concatenate([by_section(w_kv[:, :h2]), by_section(w_kv[:, h2:])], 0)
    return mlp(*mlp2), c, attn(*attn2), mlp(*mlp1), kv, attn(*attn1)


def swap(value):
    return lax.ppermute(value, "section", [(0, 1), (1, 0)])


def on_device(
    text, image, image_counts, cotangent,
    attn_norm_gain, attn_norm_bias, qkv_weight, attn_out_weight, mlp_norm_gain, mlp_norm_bias,
    up_weight, up_bias, down_weight, down_bias,
    cross_norm_gain, cross_norm_bias, cross_query, cross_key_value, cross_out,
):
    s = lax.axis_index("section")
    me = lax.axis_index("dp")
    count = lax.axis_size("dp")
    ids = jnp.stack([s, me]).astype(jnp.int32)
    t, d = text.shape
    h2 = d // 2
    caps, half = image.shape[:2]
    ff = up_bias.shape[1]
    fh = ff // 2
    other = 1 - s

    fast = d // count == 48
    w_qkv, w_out, w_up, w_down = qkv_weight[0], attn_out_weight[0], up_weight[0], down_weight[0]
    vec_own = pack_vectors(
        [attn_norm_gain, attn_norm_bias, mlp_norm_gain, mlp_norm_bias, down_bias, up_bias]
    )
    vec_got = swap(vec_own)
    got_qkv, got_out, got_up, got_down = swap(w_qkv), swap(w_out), swap(w_up), swap(w_down)
    vectors = choose_vectors(ids, vec_own, vec_got, d, fh)
    halves = []
    for layer in range(2):
        halves.append(
            (
                Half(layer, w_qkv, got_qkv, h2),
                Half(layer, w_out, got_out, h2),
                Half(layer, w_up, got_up, fh // 3),
                Half(layer, w_down, got_down, fh // 3),
            )
        )
    gain_i, gain_t = cross_norm_gain[0:1], cross_norm_gain[1:2]
    bias_i, bias_t = cross_norm_bias[0:1], cross_norm_bias[1:2]

    r_own, kv_own, kv_send = key_value(ids, image, gain_i, bias_i, cross_key_value)
    kv_got = swap(kv_send)
    r_got = swap(r_own)

    ag1, ab1, mg1, mb1, bd1, bu1 = vectors[0]
    qw1, ow1, uw1, dw1 = halves[0]
    ag2, ab2, mg2, mb2, bd2, bu2 = vectors[1]
    qw2, ow2, uw2, dw2 = halves[1]

    h1, qkv1, att1, send = self_fwd(0, ids, [text], ag1, ab1, qw1, ow1)
    x1, n1, send = mlp_fwd(0, ids, text, send, swap(send), mg1, mb1, uw1, bu1, dw1, bd1)
    h2n, qkv2, att2, send, z = self_fwd(1, ids, [x1, send, swap(send)], ag2, ab2, qw2, ow2)
    z2, ch, cq, catt, send = cross_fwd(
        ids, image_counts, z, send, swap(send), gain_t, bias_t, cross_query, cross_out, kv_own, kv_got
    )
    act2, du2, dpart, sums_m2, bup2, z3, n2, msend = mlp_grad(
        1, ids, [z2, send, swap(send), cotangent], mg2, mb2, uw2, bu2, dw2, bd2
    )
    turned = [route(s, me, count, turn) for turn in range(3)] if fast else None
    if fast:
        m2 = Sum(up_down_weights(1, turned[0], n2, du2, act2, swap(act2), cotangent, count), count, 0)
        dsend = tie(swap(dpart), m2.outgoing)
    else:
        dsend = swap(dpart)
    dz3, dc, dcq, dkv_own, dkv_send, cpart, sums_n2 = cross_grad(
        ids, image_counts, cotangent, dpart, dsend, z3, mg2, cq, cross_query, cross_out, kv_own, kv_got,
    )
    dkv_mine, csend = swap(dkv_send), swap(cpart)
    if fast:
        ck = cross_weights(
            turned[0], ch, dcq, catt, swap(catt), dc, r_own, r_got, dkv_own, dkv_send, count
        )
        m2.land(ck)
        csend = tie(csend, m2.outgoing)
    dz2, da2, dqkv2, hpart, sums_c = self_grad(
        1, ids, dz3, cpart, csend, z2, gain_t, qkv2, qw2, ow2
    )
    hsend = swap(hpart)
    if fast:
        m2.land(sums_c)
        ca = Sum(
            self_weights(1, turned[0], tie(h2n, m2.outgoing), dqkv2, att2, swap(att2), da2, count, ck), count, 0
        )
        hsend = tie(hsend, ca.outgoing)
    act1, du1, npart, sums_a2, bup1, dz = mlp_grad(
        0, ids, [dz2, hpart, hsend, z, ag2, n1], mg1, mb1, uw1, bu1, dw1, bd1
    )
    nsend = swap(npart)
    bup_got = swap(jnp.where(s == 0, bup2, bup1))
    if fast:
        m1 = Sum(
            up_down_weights(0, turned[0], n1, du1, act1, swap(act1), dz, count), count, 0
        )
        ca.land(m1.outgoing)
        nsend = tie(nsend, ca.outgoing)
    dx1, da1, dqkv1, hpart, sums_n1 = self_grad(
        0, ids, dz, npart, nsend, x1, mg1, qkv1, qw1, ow1
    )
    hsend = swap(hpart)
    if fast:
        m2.land(sums_n1)
        ca.land(sums_n1)
        a1 = Sum(
            self_weights(0, turned[0], tie(h1, ca.outgoing), dqkv1, att1, swap(att1), da1, count), count, 0
        )
        m1.land(a1.outgoing)
        hsend = tie(hsend, m1.outgoing)
    input_grad, sums_a1 = text_grad(ids, dx1, hpart, hsend, text, ag1, dz)
    got = list(key_value_grad(ids, image, gain_i, dkv_own, tie(dkv_mine, sums_a1), cross_key_value))
    if fast:
        for x in (m2, ca, m1, a1):
            x.land(got[1])
        got[1] = tie(got[1], ca.outgoing, m1.outgoing, a1.outgoing)
    image_grad, sums_i = key_value_grad(ids, image, gain_i, dkv_own, dkv_mine, cross_key_value, got)
    bup_own = jnp.where(s == 0, bup1, bup2)
    packed = pack_sums(
        ids,
        [
            [(sums_a1, 0), (sums_a2, 0)], [(sums_a1, 1), (sums_a2, 1)],
            [(sums_n1, 0), (sums_n2, 0)], [(sums_n1, 1), (sums_n2, 1)],
            [(sums_a2, 2), (sums_m2, 2)],
        ],
        [(sums_c, 0), (sums_c, 1), (sums_i, 0), (sums_i, 1)], bup_own, bup_got,
    )
    if fast:
        for x in (m1, a1, ca):
            x.land(sums_i)
        packed = tie(packed, m1.outgoing, a1.outgoing)
        for k in reversed(range(count.bit_length() - 1)):
            packed = packed + lax.ppermute(packed, "dp", [(i, i ^ (1 << k)) for i in range(count)])
            if k == 2:
                a1.land(packed)
                packed = tie(packed, a1.outgoing)
            if k == 1:
                m1.land(packed)
                packed = tie(packed, m1.outgoing)
        finish([m2, ca, m1, a1])
        m2, ca, m1, a1 = [x.result for x in (m2, ca, m1, a1)]
        half_rows = ca.shape[0] // 2
        ckv, a2 = ca[:half_rows], ca[half_rows:]
    else:
        packed = lax.psum(packed, "dp")
        m2, c2, a2, m1, kv, a1 = plain_sums(
            s, count, (n2, du2, act2, cotangent), (ch, dcq, catt, dc), (h2n, dqkv2, att2, da2),
            (n1, du1, act1, dz), (r_own, r_got, dkv_own, dkv_send), (h1, dqkv1, att1, da1),
        )
        ckv = jnp.concatenate([c2, kv], 0)
    y = z3 + msend.astype(F32) + swap(msend).astype(F32)
    layer_out = jnp.where(s == 0, z, y.astype(BF))

    each = d // count
    small = each // 2
    units = fh // h2
    wide = ff // count
    m_got = swap(jnp.where(s == 0, m2, m1))
    a_got = swap(jnp.where(s == 0, a2, a1))
    cross = ckv.reshape(4, 2, small, h2)
    keep = lax.dynamic_index_in_dim(cross, s, 1, False).reshape(4 * small, h2)
    come = swap(lax.dynamic_index_in_dim(cross, other, 1, False).reshape(4 * small, h2))
    pairs = lambda starts: [(side, 2 * i + side, at) for i, at in enumerate(starts) for side in range(2)]
    g_up, g_down = assemble(
        "assemble_mlp", ids, [m1, m2], m_got,
        [
            (each, [(side, side * units + i, i * each) for side in range(2) for i in range(units)]),
            (wide, pairs([units * each])),
        ],
    )
    g_qkv, g_out = assemble(
        "assemble_self", ids, [a1, a2], a_got,
        [(each, pairs([i * each for i in range(3)])), (each, pairs([3 * each]))],
    )
    g_cq, g_co, g_kv = assemble(
        "assemble_cross", ids, [keep], come,
        [(small, pairs([0])), (small, pairs([small])), (small, pairs([2 * small, 3 * small]))],
    )
    image_sums = packed[:, 7 * d : 9 * d]
    image_sums = image_sums + swap(image_sums)
    mine = lambda i: lax.dynamic_slice(packed, (0, i * d + me * each), (1, each))
    at = s * (d // 2) + me * small
    text_part = lambda i: lax.dynamic_slice(packed, (0, (5 + i) * d + at), (1, small))
    image_part = lambda i: lax.dynamic_slice(image_sums, (0, i * d + at), (1, small))
    g_bup = lax.dynamic_slice(packed, (0, 9 * d + me * wide), (1, wide))
    return (
        layer_out[None], input_grad[None], image_grad,
        mine(0), mine(1), g_qkv[None], g_out[None], mine(2), mine(3),
        g_up[None], g_bup, g_down[None], mine(4),
        jnp.concatenate([image_part(0), text_part(0)], 0), jnp.concatenate([image_part(1), text_part(1)], 0),
        g_cq, g_kv, g_co,
    )


def solution(mesh):
    placed = (
        P("dp", None), P("dp", "section", None), P("dp"), P("dp", None),
        P("section", None), P("section", None), P("section", None, None), P("section", None, None),
        P("section", None), P("section", None), P("section", None, None), P("section", None),
        P("section", None, None), P("section", None), P(), P(), P(), P(), P(),
    )
    two, three = P("section", "dp"), P("section", "dp", None)
    last = P(("section", "dp"), None)
    return jax.shard_map(
        on_device,
        mesh=mesh,
        in_specs=placed,
        out_specs=(
            three, three, P("dp", "section", None), two, two, three, three, two, two, three, two,
            three, two, P(None, ("section", "dp")), P(None, ("section", "dp")), last, last, last,
        ),
        check_vma=False,
    )
```
